128 devices in a mesh: narrow: 4 (over y_lo, core), wide: 32 (over y_hi, z, x).
Axes of the slice: x: 4, y: 4 (y_hi: 2, y_lo: 2; y = y_hi * 2 + y_lo), z: 4, core: 2. Of those that a mesh axis runs over, the one named last changes fastest.
Arguments:
- adjoint_hat: float32 [3, 2, 256, 256, 256], P(None, None, 'wide', 'narrow'), may hold values from -3 to 3
- velocity_hat: float32 [3, 2, 256, 256, 256], P(None, None, 'wide', 'narrow'), may hold values from -3 to 3
Outputs:
- adjoint_next: float32 [3, 2, 256, 256, 256], P(None, None, 'wide', 'narrow')
The draws below stay inside these ranges and needn't reach their ends.
All inputs are finite; a program needn't handle non-finite values.
Results may differ from the reference program's by a relative error of at most 0.00005.
Values sent between devices are 32-bit elements; how exact they have to be, the bound alone decides.
No kernel may reach another device: no remote copies, remote signals or barrier semaphores. Data moves between devices by JAX's collectives and lax.ppermute only.
A program may use at most 128 MiB of HBM per device.

```python
import math
import jax
import jax.numpy as jnp
from jax import lax

NX = 512
NY = 256
NZ = 256
KX = 256


def steps_of(stream_key, extent, pieces, smallest, largest):
    def one(axis_at, parts):
        steps = jax.random.uniform(jax.random.fold_in(jax.random.fold_in(stream_key, 6), axis_at), (parts,), jnp.float32, smallest / len(pieces), largest / len(pieces))
        return jnp.repeat(jnp.exp(steps), extent[axis_at] // parts).reshape((-1,) + (1,) * (len(extent) - axis_at - 1))

    level = one(*pieces[0])
    for cut in pieces[1:]:
        level = level * one(*cut)
    return level


def gaussian(rng, extent, deviation, bound, shards=(), kind=jnp.bfloat16):
    loudness = steps_of(rng, extent, shards, -0.22, 0.18) if shards else 1.0
    entries = jax.random.normal(rng, extent, jnp.float32) * deviation * loudness
    return jnp.minimum(jnp.maximum(entries, -bound), bound).astype(kind)


def setup_inputs(seed: int = 0) -> dict:
    keys = jax.random.split(jax.random.key(seed), 3)
    adjoint_hat = gaussian(keys[0], (3, 2, KX, NY, NZ), 0.5, 3.0, ((2, 32), (3, 4)), jnp.float32)
    velocity_hat = gaussian(keys[1], (3, 2, KX, NY, NZ), 0.5, 3.0, ((2, 32), (3, 4)), jnp.float32)
    return dict(adjoint_hat=adjoint_hat, velocity_hat=velocity_hat)


def signed_modes(length):
    number = jnp.arange(length, dtype=jnp.int32)
    return jnp.where(number < length // 2, number, number - length)


def synthesize(real_part, imag_part):
    spectra = lax.complex(real_part, imag_part)
    spectra = jnp.fft.ifft(spectra, axis=2, norm="ortho")
    spectra = jnp.fft.ifft(spectra, axis=1, norm="ortho")
    weights = jnp.where(jnp.arange(KX, dtype=jnp.int32) == 0, 1.0, 2.0).astype(real_part.dtype)[:, None, None]
    spectra = spectra * weights
    padded = jnp.concatenate([spectra, jnp.zeros((NX - KX, NY, NZ), spectra.dtype)], axis=0)
    return jnp.real(jnp.fft.ifft(padded, axis=0, norm="ortho"))


def analyze(field):
    spectra = jnp.fft.rfft(field, axis=0, norm="ortho")[:KX]
    spectra = jnp.fft.fft(spectra, axis=1, norm="ortho")
    spectra = jnp.fft.fft(spectra, axis=2, norm="ortho")
    return jnp.real(spectra), jnp.imag(spectra)


def cross_list(first, second):
    return [first[1] * second[2] - first[2] * second[1],
            first[2] * second[0] - first[0] * second[2],
            first[0] * second[1] - first[1] * second[0]]


def reference(adjoint_hat, velocity_hat):
    number_x = jnp.arange(KX, dtype=jnp.int32)[:, None, None]
    number_y = signed_modes(NY)[None, :, None]
    number_z = signed_modes(NZ)[None, None, :]
    waves = [(2.0 * math.pi / NX) * number_x.astype(jnp.float32),
             (2.0 * math.pi / NY) * number_y.astype(jnp.float32),
             (2.0 * math.pi / NZ) * number_z.astype(jnp.float32)]
    vel_real = [velocity_hat[c, 0] for c in range(3)]
    vel_imag = [velocity_hat[c, 1] for c in range(3)]
    vort_real = [-v for v in cross_list(waves, vel_imag)]
    vort_imag = cross_list(waves, vel_real)
    adjoint = [synthesize(adjoint_hat[c, 0], adjoint_hat[c, 1]) for c in range(3)]
    velocity = [synthesize(vel_real[c], vel_imag[c]) for c in range(3)]
    vorticity = [synthesize(vort_real[c], vort_imag[c]) for c in range(3)]
    rotation = [analyze(g) for g in cross_list(adjoint, vorticity)]
    transport = [analyze(g) for g in cross_list(velocity, adjoint)]
    curl_real = cross_list(waves, [t[1] for t in transport])
    curl_imag = cross_list(waves, [t[0] for t in transport])
    conv_real = [rotation[c][0] - curl_real[c] for c in range(3)]
    conv_imag = [rotation[c][1] + curl_imag[c] for c in range(3)]
    keep = ((3 * number_x < NX) & (3 * jnp.abs(number_y) < NY) & (3 * jnp.abs(number_z) < NZ)).astype(jnp.float32)
    ksq = waves[0] ** 2 + waves[1] ** 2 + waves[2] ** 2
    divisor = ksq + (ksq == 0).astype(jnp.float32)
    decay = jnp.exp(-0.05 * ksq)
    results = []
    for conv in (conv_real, conv_imag):
        along = (waves[0] * conv[0] + waves[1] * conv[1] + waves[2] * conv[2]) / divisor
        results.append([keep * (conv[c] - waves[c] * along) for c in range(3)])
    output = []
    for c in range(3):
        output.append(jnp.stack([decay * (adjoint_hat[c, 0] + 0.25 * results[0][c]),
                                 decay * (adjoint_hat[c, 1] + 0.25 * results[1][c])], 0))
    return jnp.stack(output, 0)
```

```python
import math

import jax
import jax.numpy as jnp
import ml_dtypes
import numpy as np
from jax import lax
from jax.experimental import pallas as pl
from jax.experimental.pallas import tpu as pltpu
from jax.sharding import PartitionSpec as P

NX = 512
NY = 256
NZ = 256
KX = 256
ROWS_X = 8
ROWS_Y = 64
WIDE = 32
NARROW = 4
DEVICES = WIDE * NARROW
SENT = 8
BACK = 5
KEPT_X = 176

section_step = 0.25
viscous_rate = 0.05
vmem_bytes = 60 * 1024 * 1024


def halves(table):
    upper = table.astype(ml_dtypes.bfloat16)
    lower = (table - upper.astype(np.float64)).astype(ml_dtypes.bfloat16)
    return np.stack([upper, lower])


def turn(modes, places, length):
    angle = 2.0 * np.pi / length * (np.outer(modes, places) % length)
    return np.cos(angle), np.sin(angle)


def tables_synth_z():
    quarter = np.arange(128)
    parts = []
    for plane in range(2):
        cosine, sine = turn(2 * np.arange(128) + plane, quarter, NZ)
        parts.append(halves(np.concatenate([cosine, sine], 1)))
    return np.stack(parts)


def tables_synth_y():
    mode = np.arange(128)
    parts = []
    for parity in range(2):
        cosine, sine = turn(mode, 2 * np.arange(128) + parity, NY)
        real_rows = np.concatenate([cosine, sine], 1)
        imag_rows = np.concatenate([-sine, cosine], 1)
        stacked = np.stack([real_rows.reshape(2, 64, 256), imag_rows.reshape(2, 64, 256)], 1)
        parts.append(halves(stacked.reshape(256, 256)))
    return np.stack(parts)


def norm_scale():
    return 1.0 / math.sqrt(NX * NY * NZ)


def tables_synth_x():
    weight = np.where(np.arange(KX) == 0, 1.0, 2.0) * norm_scale()
    cosine, sine = turn(np.arange(256), np.arange(KX), NX)
    return np.stack([halves(cosine * weight), halves(-sine * weight)])


def tables_anal_x():
    cosine, sine = turn(np.arange(KEPT_X), np.arange(256), NX)
    return np.stack([halves(cosine * norm_scale()), halves(-sine * norm_scale())])


def tables_anal_y():
    parts = []
    mode = np.arange(128)
    for parity in range(2):
        cosine, sine = turn(2 * np.arange(128) + parity, mode, NY)
        cosine = cosine.reshape(128, 2, 1, 64)
        sine = sine.reshape(128, 2, 1, 64)
        real_rows = np.concatenate([cosine, -sine], 2).reshape(128, 256)
        imag_rows = np.concatenate([sine, cosine], 2).reshape(128, 256)
        parts.append(halves(np.concatenate([real_rows, imag_rows], 0)))
    return np.stack(parts)


def tables_anal_z():
    place = np.concatenate([2 * np.arange(128), 2 * np.arange(128) + 1])
    cosine, sine = turn(place, np.arange(NZ), NZ)
    return halves(np.concatenate([cosine, sine], 1))


def split(value):
    upper = value.astype(jnp.bfloat16)
    lower = (value - upper.astype(jnp.float32)).astype(jnp.bfloat16)
    return upper, lower


def dot(left, right, dims):
    return lax.dot_general(left, right, (dims, ((), ())), preferred_element_type=jnp.float32)


def dot3(left, right, dims=((1,), (0,))):
    return (
        dot(left[0], right[0], dims)
        + dot(left[0], right[1], dims)
        + dot(left[1], right[0], dims)
    )


def signed(number, length):
    return jnp.where(number < length // 2, number, number - length)


def wave_y(start, shape, axis):
    number = lax.broadcasted_iota(jnp.int32, shape, axis) + start
    return 2.0 * math.pi / NY * signed(number, NY).astype(jnp.float32)


def wave_z(shape, axis):
    number = lax.broadcasted_iota(jnp.int32, shape, axis)
    return 2.0 * math.pi / NZ * signed(number, NZ).astype(jnp.float32)


def synth_z_kernel(place_ref, adjoint_ref, velocity_ref, table_ref, even_ref, odd_ref):
    outs = (even_ref, odd_ref)
    ky = wave_y(place_ref[1] * ROWS_Y, (ROWS_Y, 1), 0)
    kz = wave_z((1, NZ), 1)
    vel = [[velocity_ref[c, part, 0] for part in range(2)] for c in range(3)]
    fields = [(adjoint_ref[c, 0, 0], adjoint_ref[c, 1, 0]) for c in range(3)]
    fields += [(vel[c][0], vel[c][1]) for c in range(3)]
    fields.append((kz * vel[1][1] - ky * vel[2][1], ky * vel[2][0] - kz * vel[1][0]))
    fields.append((0.0, 0.0))
    number_x = place_ref[0] * ROWS_X + pl.program_id(0)
    kx = 2.0 * math.pi / NX * number_x.astype(jnp.float32)
    fields[7] = (kx * vel[2][1] - kz * vel[0][1], kz * vel[0][0] - kx * vel[2][0])
    for plane in range(2):
        table = (table_ref[plane, 0], table_ref[plane, 1])
        for pair in range(SENT // 2):
            blocks = []
            for real, imag in fields[2 * pair : 2 * pair + 2]:
                if plane == 0:
                    low_r = real[:, :128] + real[:, 128:]
                    low_i = imag[:, :128] + imag[:, 128:]
                else:
                    low_r = real[:, :128] - real[:, 128:]
                    low_i = imag[:, :128] - imag[:, 128:]
                blocks.append(jnp.concatenate([low_r, -low_i], 1))
                blocks.append(jnp.concatenate([low_i, low_r], 1))
            value = dot3(table, split(jnp.concatenate(blocks, 0)), ((1,), (1,)))
            outs[plane][:, 2 * pair, :] = value[:, :128]
            outs[plane][:, 2 * pair + 1, :] = value[:, 128:]


def synth_z(place, adjoint_hat, velocity_hat):
    whole = (3, 2, 1, ROWS_Y, NZ)
    table = tables_synth_z()
    shape = jax.ShapeDtypeStruct((DEVICES, ROWS_X * SENT, 128), jnp.float32)
    out_spec = pl.BlockSpec((DEVICES, SENT, 128), lambda k, s: (0, k, 0))
    return pl.pallas_call(
        synth_z_kernel,
        grid_spec=pltpu.PrefetchScalarGridSpec(
            num_scalar_prefetch=1,
            grid=(ROWS_X,),
            in_specs=[
                pl.BlockSpec(whole, lambda k, s: (0, 0, k, 0, 0)),
                pl.BlockSpec(whole, lambda k, s: (0, 0, k, 0, 0)),
                pl.BlockSpec(table.shape, lambda k, s: (0, 0, 0, 0)),
            ],
            out_specs=[out_spec, out_spec],
        ),
        out_shape=[shape, shape],
        compiler_params=pltpu.CompilerParams(vmem_limit_bytes=vmem_bytes),
        name="synth_z",
    )(place, adjoint_hat, velocity_hat, jnp.asarray(table))


def plane_kernel(got_ref, sy_ref, sx_ref, ax_ref, ay_ref, out_ref, spec_ref, cell_ref, anal_ref):
    chunk = ROWS_X * SENT
    half_sign = jnp.where(lax.broadcasted_iota(jnp.int32, (1, 128), 1) < 64, -1.0, 1.0)
    ky_lanes = []
    for n in range(NARROW):
        number = lax.broadcasted_iota(jnp.int32, (1, 128), 1) % 64 + n * ROWS_Y
        ky_lanes.append(2.0 * math.pi / NY * signed(number, NY).astype(jnp.float32))
    kx_rows = 2.0 * math.pi / NX * lax.broadcasted_iota(jnp.int32, (KX, 1), 0).astype(jnp.float32)
    alternate = jnp.where(lax.broadcasted_iota(jnp.int32, (KX, 1), 0) % 2 == 0, 1.0, -1.0)
    weight = (
        jnp.where(lax.broadcasted_iota(jnp.int32, (KX, 1), 0) == 0, 1.0, 2.0) * norm_scale()
    )
    first_row = lax.broadcasted_iota(jnp.int32, (256, 1), 0) == 0

    def rows_of(field, n):
        return jnp.concatenate(
            [
                got_ref[pl.ds((w * NARROW + n) * chunk + field, ROWS_X, stride=SENT), :]
                for w in range(WIDE)
            ],
            0,
        )

    def synth(parts, index):
        spans = []
        for parity in range(2):
            if parity == 0:
                merged = [parts[0] + parts[2], parts[1] + parts[3]]
            else:
                merged = [parts[0] - parts[2], parts[1] - parts[3]]
            spans.append(
                dot3(
                    split(jnp.concatenate(merged, 1)), (sy_ref[parity, 0], sy_ref[parity, 1])
                )
            )
        real = jnp.concatenate([spans[0][:, :128], spans[1][:, :128]], 1)
        imag = jnp.concatenate([spans[0][:, 128:], spans[1][:, 128:]], 1)
        cosine = dot3((sx_ref[0, 0], sx_ref[0, 1]), split(real))
        sine = dot3((sx_ref[1, 0], sx_ref[1, 1]), split(imag))
        middle = jnp.sum(real * (alternate * weight), 0, keepdims=True)
        cell_ref[index, 0] = cosine + sine
        cell_ref[index, 1] = jnp.where(first_row, middle, cosine - sine)

    def each_field(field, carry):
        synth([rows_of(field, n) for n in range(NARROW)], field)
        return carry

    lax.fori_loop(0, SENT, each_field, 0)
    swirl = []
    for n in range(NARROW):
        across = kx_rows * rows_of(4, n) - ky_lanes[n] * rows_of(3, n)
        swirl.append(pltpu.roll(across, 64, 1) * half_sign)
    synth(swirl, SENT)

    def product(kind, c, mirror):
        one, two = (c + 1) % 3, (c + 2) % 3
        if kind == 0:
            return (
                cell_ref[one, mirror] * cell_ref[6 + two, mirror]
                - cell_ref[two, mirror] * cell_ref[6 + one, mirror]
            )
        return (
            cell_ref[3 + one, mirror] * cell_ref[two, mirror]
            - cell_ref[3 + two, mirror] * cell_ref[one, mirror]
        )

    def analyse(index, kind, c):
        ahead = product(kind, c, 0)
        behind = product(kind, c, 1)
        middle = behind[0:1]
        both = ahead + jnp.where(first_row, 0.0, behind)
        apart = ahead - behind
        real = dot3((ax_ref[0, 0], ax_ref[0, 1]), split(both))
        real = real + alternate[:KEPT_X] * norm_scale() * middle
        imag = dot3((ax_ref[1, 0], ax_ref[1, 1]), split(apart))
        spans = []
        for parity in range(2):
            lanes = slice(128 * parity, 128 * parity + 128)
            spans.append(
                dot3(
                    split(jnp.concatenate([real[:, lanes], imag[:, lanes]], 1)),
                    (ay_ref[parity, 0], ay_ref[parity, 1]),
                )
            )
        spec_ref[index, 0] = spans[0] + spans[1]
        spec_ref[index, 1] = spans[0] - spans[1]

    for kind in range(2):
        for c in range(3):
            analyse(3 * kind + c, kind, c)

    kx_kept = kx_rows[:KEPT_X]

    def times_i(value):
        return pltpu.roll(value, 64, 1) * half_sign

    out_ref[KEPT_X // ROWS_X :] = jnp.zeros(
        (WIDE - KEPT_X // ROWS_X, NARROW, BACK * ROWS_X, 128), jnp.float32
    )
    for n in range(NARROW):
        at = (n // 2, slice(None), slice(128 * (n % 2), 128 * (n % 2) + 128))
        item = [spec_ref[(index,) + at] for index in range(6)]
        ky = ky_lanes[n]
        values = [
            item[0] + times_i(ky * item[5]),
            item[1] - times_i(kx_kept * item[5]),
            item[2] + times_i(kx_kept * item[4] - ky * item[3]),
            item[3],
            item[4],
        ]
        for f in range(BACK):
            out_ref[: KEPT_X // ROWS_X, n, f * ROWS_X : (f + 1) * ROWS_X, :] = values[f].reshape(
                KEPT_X // ROWS_X, ROWS_X, 128
            )


def plane(got):
    tables = [tables_synth_y(), tables_synth_x(), tables_anal_x(), tables_anal_y()]
    return pl.pallas_call(
        plane_kernel,
        out_shape=jax.ShapeDtypeStruct((WIDE, NARROW, BACK * ROWS_X, 128), jnp.float32),
        in_specs=[pl.BlockSpec(memory_space=pltpu.VMEM)] * 5,
        out_specs=pl.BlockSpec(memory_space=pltpu.VMEM),
        scratch_shapes=[
            pltpu.VMEM((6, 2, KEPT_X, 256), jnp.float32),
            pltpu.VMEM((9, 2, 256, 256), jnp.float32),
            pltpu.VMEM((8, 128), jnp.float32),
        ],
        compiler_params=pltpu.CompilerParams(vmem_limit_bytes=vmem_bytes),
        name="plane",
    )(got.reshape(DEVICES * ROWS_X * SENT, 128), *[jnp.asarray(t) for t in tables])


def finish_kernel(place_ref, even_ref, odd_ref, adjoint_ref, table_ref, out_ref):
    k = pl.program_id(0)
    number_x = place_ref[0] * ROWS_X + k
    kx = 2.0 * math.pi / NX * number_x.astype(jnp.float32)
    number_y = signed(
        lax.broadcasted_iota(jnp.int32, (ROWS_Y, 1), 0) + place_ref[1] * ROWS_Y, NY
    )
    number_z = signed(lax.broadcasted_iota(jnp.int32, (1, NZ), 1), NZ)
    ky = 2.0 * math.pi / NY * number_y.astype(jnp.float32)
    kz = 2.0 * math.pi / NZ * number_z.astype(jnp.float32)
    table = (table_ref[0], table_ref[1])
    got = []
    for f in range(BACK):
        stacked = jnp.concatenate(
            [
                ref[pl.ds(f * ROWS_X + k, DEVICES, stride=BACK * ROWS_X), :]
                for ref in (even_ref, odd_ref)
            ],
            0,
        )
        span = dot3(split(stacked.T), table)
        real = span[:64, :256] + span[64:, 256:]
        imag = span[64:, :256] - span[:64, 256:]
        got.append((real, imag))
    conv = [
        (got[0][0] + kz * got[4][1], got[0][1] - kz * got[4][0]),
        (got[1][0] - kz * got[3][1], got[1][1] + kz * got[3][0]),
        got[2],
    ]
    keep = (
        (3 * number_x < NX) & (3 * jnp.abs(number_y) < NY) & (3 * jnp.abs(number_z) < NZ)
    ).astype(jnp.float32)
    ksquare = kx * kx + ky * ky + kz * kz
    inverse = 1.0 / (ksquare + (ksquare == 0).astype(jnp.float32))
    decay = jnp.exp(-viscous_rate * ksquare)
    waves = (kx, ky, kz)
    for part in range(2):
        along = (kx * conv[0][part] + ky * conv[1][part] + kz * conv[2][part]) * inverse
        for c in range(3):
            projected = keep * (conv[c][part] - waves[c] * along)
            out_ref[c, part, 0] = decay * (adjoint_ref[c, part, 0] + section_step * projected)


def finish(place, even, odd, adjoint_hat):
    whole = (3, 2, 1, ROWS_Y, NZ)
    table = tables_anal_z()
    flat = (DEVICES * BACK * ROWS_X, 128)
    return pl.pallas_call(
        finish_kernel,
        grid_spec=pltpu.PrefetchScalarGridSpec(
            num_scalar_prefetch=1,
            grid=(ROWS_X,),
            in_specs=[
                pl.BlockSpec(flat, lambda k, s: (0, 0)),
                pl.BlockSpec(flat, lambda k, s: (0, 0)),
                pl.BlockSpec(whole, lambda k, s: (0, 0, k, 0, 0)),
                pl.BlockSpec(table.shape, lambda k, s: (0, 0, 0)),
            ],
            out_specs=pl.BlockSpec(whole, lambda k, s: (0, 0, k, 0, 0)),
        ),
        out_shape=jax.ShapeDtypeStruct((3, 2, ROWS_X, ROWS_Y, NZ), jnp.float32),
        compiler_params=pltpu.CompilerParams(vmem_limit_bytes=vmem_bytes),
        name="finish",
    )(place, even.reshape(flat), odd.reshape(flat), adjoint_hat, jnp.asarray(table))


def swap(chunks):
    return lax.all_to_all(chunks, ("wide", "narrow"), 0, 0, tiled=True)


def local(adjoint_hat, velocity_hat):
    place = jnp.stack([lax.axis_index("wide"), lax.axis_index("narrow")]).astype(jnp.int32)
    sent = synth_z(place, adjoint_hat, velocity_hat)
    got = [swap(part) for part in sent]
    back = [
        swap(plane(part).reshape(DEVICES, BACK * ROWS_X, 128)) for part in got
    ]
    return finish(place, back[0], back[1], adjoint_hat)


def solution(mesh):
    in_specs = (P(None, None, "wide", "narrow", None), P(None, None, "wide", "narrow", None))
    out_specs = P(None, None, "wide", "narrow", None)
    return jax.shard_map(local, mesh=mesh, in_specs=in_specs, out_specs=out_specs, check_vma=False)
```

```python
import functools
import math

import jax
import jax.numpy as jnp
import ml_dtypes
import numpy as np
from jax import lax
from jax.experimental import pallas as pl
from jax.experimental.pallas import tpu as pltpu
from jax.sharding import PartitionSpec as P

NX = 512
NY = 256
NZ = 256
KX = 256
ROWS_X = 8
ROWS_Y = 64
WIDE = 32
NARROW = 4
DEVICES = WIDE * NARROW
SENT = 8
BACK = 5
KEPT_X = 176
KEPT_W = KEPT_X // ROWS_X
HEAVY = (0, 3)
LIGHT = (1, 2)
LIGHT_ROW = (0, 40)
SLOT = 24

section_step = 0.25
viscous_rate = 0.05
vmem_bytes = 60 * 1024 * 1024


def halves(table):
    upper = table.astype(ml_dtypes.bfloat16)
    lower = (table - upper.astype(np.float64)).astype(ml_dtypes.bfloat16)
    return np.stack([upper, lower])


def turn(modes, places, length):
    angle = 2.0 * np.pi / length * (np.outer(modes, places) % length)
    return np.cos(angle), np.sin(angle)


def tables_synth_z():
    quarter = np.arange(128)
    parts = []
    for plane in range(2):
        cosine, sine = turn(2 * np.arange(128) + plane, quarter, NZ)
        parts.append(halves(np.concatenate([cosine, sine], 1)))
    return np.stack(parts)


def tables_synth_y():
    mode = np.arange(128)
    parts = []
    for parity in range(2):
        cosine, sine = turn(mode, 2 * np.arange(128) + parity, NY)
        real_rows = np.concatenate([cosine, sine], 1)
        imag_rows = np.concatenate([-sine, cosine], 1)
        stacked = np.stack([real_rows.reshape(2, 64, 256), imag_rows.reshape(2, 64, 256)], 1)
        parts.append(halves(stacked.reshape(256, 256)))
    return np.stack(parts)


def norm_scale():
    return 1.0 / math.sqrt(NX * NY * NZ)


def tables_synth_x():
    weight = np.where(np.arange(KX) == 0, 1.0, 2.0) * norm_scale()
    cosine, sine = turn(np.arange(256), np.arange(KX), NX)
    return np.stack([halves(cosine * weight), halves(-sine * weight)])


def tables_anal_x():
    cosine, sine = turn(np.arange(KEPT_X), np.arange(256), NX)
    return np.stack([halves(cosine * norm_scale()), halves(-sine * norm_scale())])


def tables_anal_y():
    parts = []
    mode = np.arange(128)
    for parity in range(2):
        cosine, sine = turn(2 * np.arange(128) + parity, mode, NY)
        cosine = cosine.reshape(128, 2, 1, 64)
        sine = sine.reshape(128, 2, 1, 64)
        real_rows = np.concatenate([cosine, -sine], 2).reshape(128, 256)
        imag_rows = np.concatenate([sine, cosine], 2).reshape(128, 256)
        parts.append(halves(np.concatenate([real_rows, imag_rows], 0)))
    return np.stack(parts)


def tables_anal_z():
    place = np.concatenate([2 * np.arange(128), 2 * np.arange(128) + 1])
    cosine, sine = turn(place, np.arange(NZ), NZ)
    return halves(np.concatenate([cosine, sine], 1))


def split(value):
    upper = value.astype(jnp.bfloat16)
    lower = (value - upper.astype(jnp.float32)).astype(jnp.bfloat16)
    return upper, lower


def dot(left, right, dims):
    return lax.dot_general(left, right, (dims, ((), ())), preferred_element_type=jnp.float32)


def dot3(left, right, dims=((1,), (0,))):
    return (
        dot(left[0], right[0], dims)
        + dot(left[0], right[1], dims)
        + dot(left[1], right[0], dims)
    )


def signed(number, length):
    return jnp.where(number < length // 2, number, number - length)


def wave_y(start, shape, axis):
    number = lax.broadcasted_iota(jnp.int32, shape, axis) + start
    return 2.0 * math.pi / NY * signed(number, NY).astype(jnp.float32)


def wave_z(shape, axis):
    number = lax.broadcasted_iota(jnp.int32, shape, axis)
    return 2.0 * math.pi / NZ * signed(number, NZ).astype(jnp.float32)


def synth_z_kernel(plane, place_ref, adjoint_ref, velocity_ref, table_ref, out_ref):
    ky = wave_y(place_ref[1] * ROWS_Y, (ROWS_Y, 1), 0)
    kz = wave_z((1, NZ), 1)
    vel = [[velocity_ref[c, part, 0] for part in range(2)] for c in range(3)]
    fields = [(adjoint_ref[c, 0, 0], adjoint_ref[c, 1, 0]) for c in range(3)]
    fields += [(vel[c][0], vel[c][1]) for c in range(3)]
    fields.append((kz * vel[1][1] - ky * vel[2][1], ky * vel[2][0] - kz * vel[1][0]))
    fields.append((0.0, 0.0))
    number_x = place_ref[0] * ROWS_X + pl.program_id(0)
    kx = 2.0 * math.pi / NX * number_x.astype(jnp.float32)
    fields[7] = (kx * vel[2][1] - kz * vel[0][1], kz * vel[0][0] - kx * vel[2][0])
    table = (table_ref[0], table_ref[1])
    for pair in range(SENT // 2):
        blocks = []
        for real, imag in fields[2 * pair : 2 * pair + 2]:
            if plane == 0:
                low_r = real[:, :128] + real[:, 128:]
                low_i = imag[:, :128] + imag[:, 128:]
            else:
                low_r = real[:, :128] - real[:, 128:]
                low_i = imag[:, :128] - imag[:, 128:]
            blocks.append(jnp.concatenate([low_r, -low_i], 1))
            blocks.append(jnp.concatenate([low_i, low_r], 1))
        value = dot3(table, split(jnp.concatenate(blocks, 0)), ((1,), (1,)))
        out_ref[:, 2 * pair, :] = value[:, :128]
        out_ref[:, 2 * pair + 1, :] = value[:, 128:]


def synth_z(place, adjoint_hat, velocity_hat, plane):
    whole = (3, 2, 1, ROWS_Y, NZ)
    table = tables_synth_z()[plane]
    return pl.pallas_call(
        functools.partial(synth_z_kernel, plane),
        grid_spec=pltpu.PrefetchScalarGridSpec(
            num_scalar_prefetch=1,
            grid=(ROWS_X,),
            in_specs=[
                pl.BlockSpec(whole, lambda k, s: (0, 0, k, 0, 0)),
                pl.BlockSpec(whole, lambda k, s: (0, 0, k, 0, 0)),
                pl.BlockSpec(table.shape, lambda k, s: (0, 0, 0)),
            ],
            out_specs=pl.BlockSpec((DEVICES, SENT, 128), lambda k, s: (0, k, 0)),
        ),
        out_shape=jax.ShapeDtypeStruct((DEVICES, ROWS_X * SENT, 128), jnp.float32),
        compiler_params=pltpu.CompilerParams(vmem_limit_bytes=vmem_bytes),
        name="synth_z",
    )(place, adjoint_hat, velocity_hat, jnp.asarray(table))


def plane_kernel(plane, got_ref, sy_ref, sx_ref, ax_ref, ay_ref, *refs):
    if plane == 0:
        out_ref, rest_ref, spec_ref, cell_ref = refs
    else:
        rest_ref, out_ref, spec_ref, cell_ref = refs
    chunk = ROWS_X * SENT
    half_sign = jnp.where(lax.broadcasted_iota(jnp.int32, (1, 128), 1) < 64, -1.0, 1.0)
    ky_lanes = []
    for n in range(NARROW):
        number = lax.broadcasted_iota(jnp.int32, (1, 128), 1) % 64 + n * ROWS_Y
        ky_lanes.append(2.0 * math.pi / NY * signed(number, NY).astype(jnp.float32))
    kx_rows = 2.0 * math.pi / NX * lax.broadcasted_iota(jnp.int32, (KX, 1), 0).astype(jnp.float32)
    alternate = jnp.where(lax.broadcasted_iota(jnp.int32, (KX, 1), 0) % 2 == 0, 1.0, -1.0)
    weight = (
        jnp.where(lax.broadcasted_iota(jnp.int32, (KX, 1), 0) == 0, 1.0, 2.0) * norm_scale()
    )
    first_row = lax.broadcasted_iota(jnp.int32, (256, 1), 0) == 0

    def rows_of(field, n):
        return jnp.concatenate(
            [
                got_ref[pl.ds((w * NARROW + n) * chunk + field, ROWS_X, stride=SENT), :]
                for w in range(WIDE)
            ],
            0,
        )

    def synth(parts, index):
        spans = []
        for parity in range(2):
            if parity == 0:
                merged = [parts[0] + parts[2], parts[1] + parts[3]]
            else:
                merged = [parts[0] - parts[2], parts[1] - parts[3]]
            spans.append(
                dot3(
                    split(jnp.concatenate(merged, 1)), (sy_ref[parity, 0], sy_ref[parity, 1])
                )
            )
        real = jnp.concatenate([spans[0][:, :128], spans[1][:, :128]], 1)
        imag = jnp.concatenate([spans[0][:, 128:], spans[1][:, 128:]], 1)
        cosine = dot3((sx_ref[0, 0], sx_ref[0, 1]), split(real))
        sine = dot3((sx_ref[1, 0], sx_ref[1, 1]), split(imag))
        middle = jnp.sum(real * (alternate * weight), 0, keepdims=True)
        cell_ref[index, 0] = cosine + sine
        cell_ref[index, 1] = jnp.where(first_row, middle, cosine - sine)

    def each_field(field, carry):
        synth([rows_of(field, n) for n in range(NARROW)], field)
        return carry

    lax.fori_loop(0, SENT, each_field, 0)
    swirl = []
    for n in range(NARROW):
        across = kx_rows * rows_of(4, n) - ky_lanes[n] * rows_of(3, n)
        swirl.append(pltpu.roll(across, 64, 1) * half_sign)
    synth(swirl, SENT)

    def product(kind, c, mirror):
        one, two = (c + 1) % 3, (c + 2) % 3
        if kind == 0:
            return (
                cell_ref[one, mirror] * cell_ref[6 + two, mirror]
                - cell_ref[two, mirror] * cell_ref[6 + one, mirror]
            )
        return (
            cell_ref[3 + one, mirror] * cell_ref[two, mirror]
            - cell_ref[3 + two, mirror] * cell_ref[one, mirror]
        )

    def analyse(index, kind, c):
        ahead = product(kind, c, 0)
        behind = product(kind, c, 1)
        middle = behind[0:1]
        both = ahead + jnp.where(first_row, 0.0, behind)
        apart = ahead - behind
        real = dot3((ax_ref[0, 0], ax_ref[0, 1]), split(both))
        real = real + alternate[:KEPT_X] * norm_scale() * middle
        imag = dot3((ax_ref[1, 0], ax_ref[1, 1]), split(apart))
        spans = []
        for parity in range(2):
            lanes = slice(128 * parity, 128 * parity + 128)
            spans.append(
                dot3(
                    split(jnp.concatenate([real[:, lanes], imag[:, lanes]], 1)),
                    (ay_ref[parity, 0], ay_ref[parity, 1]),
                )
            )
        spec_ref[index, 0] = spans[0] + spans[1]
        spec_ref[index, 1] = spans[0] - spans[1]

    for kind in range(2):
        for c in range(3):
            analyse(3 * kind + c, kind, c)

    kx_kept = kx_rows[:KEPT_X]

    def times_i(value):
        return pltpu.roll(value, 64, 1) * half_sign

    out_ref[KEPT_W:] = jnp.zeros((WIDE - KEPT_W,) + out_ref.shape[1:], jnp.float32)
    if plane == 0:
        rest_ref[KEPT_W:] = jnp.zeros((WIDE - KEPT_W,) + rest_ref.shape[1:], jnp.float32)

    def put(n, tile, value):
        rows = slice(tile * ROWS_X, tile * ROWS_X + ROWS_X)
        out_ref[:KEPT_W, n, rows, :] = value.reshape(KEPT_W, ROWS_X, 128)

    def values_of(n):
        at = (n // 2, slice(None), slice(128 * (n % 2), 128 * (n % 2) + 128))
        item = [spec_ref[(index,) + at] for index in range(6)]
        ky = ky_lanes[n]
        return [
            item[0] + times_i(ky * item[5]),
            item[1] - times_i(kx_kept * item[5]),
            item[2] + times_i(kx_kept * item[4] - ky * item[3]),
            item[3],
            item[4],
        ]

    lane = lax.broadcasted_iota(jnp.int32, (1, 128), 1)
    for half in range(2):
        heavy, light = HEAVY[half], LIGHT[half]
        values = values_of(heavy)
        direct = 3 if plane == 0 else 4
        for f in range(BACK):
            if f < direct:
                put(heavy, f, values[f])
            else:
                put(light, f - direct if plane == 0 else 3, values[f])
        values = values_of(light)
        packed = []
        for tile in range(2):
            value = jnp.zeros((KEPT_X, 128), jnp.float32)
            for slot in range(5):
                f, part = divmod(5 * tile + slot, 2)
                moved = pltpu.roll(
                    values[f], (SLOT * slot - 64 * part - LIGHT_ROW[half]) % 128, 1
                )
                value = jnp.where((lane >= SLOT * slot) & (lane < SLOT * slot + SLOT), moved, value)
            packed.append(value)
        if plane == 0:
            put(light, 2, packed[0])
            rest_ref[:KEPT_W, half] = packed[1].reshape(KEPT_W, ROWS_X, 128)
        else:
            out_ref[:, light, 0:ROWS_X, :] = rest_ref[:, half]
            put(light, 1, packed[0])
            put(light, 2, packed[1])


def run_plane(plane, got, rest=None):
    tables = [tables_synth_y(), tables_synth_x(), tables_anal_x(), tables_anal_y()]
    tiles = 3 + plane
    out_shape = [jax.ShapeDtypeStruct((WIDE, NARROW, tiles * ROWS_X, 128), jnp.float32)]
    operands = [got.reshape(DEVICES * ROWS_X * SENT, 128)] + [jnp.asarray(t) for t in tables]
    if plane == 0:
        out_shape.append(jax.ShapeDtypeStruct((WIDE, 2, ROWS_X, 128), jnp.float32))
    else:
        operands.append(rest)
    outs = pl.pallas_call(
        functools.partial(plane_kernel, plane),
        out_shape=out_shape,
        in_specs=[pl.BlockSpec(memory_space=pltpu.VMEM)] * len(operands),
        out_specs=[pl.BlockSpec(memory_space=pltpu.VMEM)] * len(out_shape),
        scratch_shapes=[
            pltpu.VMEM((6, 2, KEPT_X, 256), jnp.float32),
            pltpu.VMEM((9, 2, 256, 256), jnp.float32),
        ],
        compiler_params=pltpu.CompilerParams(vmem_limit_bytes=vmem_bytes),
        name="plane",
    )(*operands)
    return [outs[0].reshape(DEVICES, tiles * ROWS_X, 128)] + list(outs[1:])


def finish_kernel(
    place_ref, got0_ref, got1_ref, more0_ref, more1_ref, adjoint_ref, table_ref, out_ref
):
    k = pl.program_id(0)
    narrow = place_ref[1]
    number_x = place_ref[0] * ROWS_X + k
    kx = 2.0 * math.pi / NX * number_x.astype(jnp.float32)
    number_z = signed(lax.broadcasted_iota(jnp.int32, (1, NZ), 1), NZ)
    kz = 2.0 * math.pi / NZ * number_z.astype(jnp.float32)
    table = (table_ref[0], table_ref[1])

    def span_of(first, second):
        rows = [
            ref[pl.ds(tile * ROWS_X + k, DEVICES, stride=tiles * ROWS_X), :]
            for ref, tile, tiles in (first, second)
        ]
        return dot3(split(jnp.concatenate(rows, 0).T), table)

    def unite(real_rows, imag_rows):
        return (
            real_rows[:, :NZ] + imag_rows[:, NZ:],
            imag_rows[:, :NZ] - real_rows[:, NZ:],
        )

    def emit(got, start, rows):
        number_y = lax.broadcasted_iota(jnp.int32, (rows, 1), 0) + start + narrow * ROWS_Y
        number_y = signed(number_y, NY)
        ky = 2.0 * math.pi / NY * number_y.astype(jnp.float32)
        conv = [
            (got[0][0] + kz * got[4][1], got[0][1] - kz * got[4][0]),
            (got[1][0] - kz * got[3][1], got[1][1] + kz * got[3][0]),
            got[2],
        ]
        keep = (
            (3 * number_x < NX) & (3 * jnp.abs(number_y) < NY) & (3 * jnp.abs(number_z) < NZ)
        ).astype(jnp.float32)
        ksquare = kx * kx + ky * ky + kz * kz
        inverse = 1.0 / (ksquare + (ksquare == 0).astype(jnp.float32))
        decay = jnp.exp(-viscous_rate * ksquare)
        waves = (kx, ky, kz)
        for part in range(2):
            along = (kx * conv[0][part] + ky * conv[1][part] + kz * conv[2][part]) * inverse
            for c in range(3):
                projected = keep * (conv[c][part] - waves[c] * along)
                old = adjoint_ref[c, part, 0, pl.ds(start, rows), :]
                out_ref[c, part, 0, pl.ds(start, rows), :] = decay * (
                    old + section_step * projected
                )

    is_light = (narrow == LIGHT[0]) | (narrow == LIGHT[1])

    @pl.when(jnp.logical_not(is_light))
    def _():
        got = []
        for f in range(BACK):
            first = (got0_ref, f, 3) if f < 3 else (more0_ref, f - 3, 2)
            second = (got1_ref, f, 4) if f < 4 else (more1_ref, 0, 1)
            span = span_of(first, second)
            got.append(unite(span[:64], span[64:]))
        emit(got, 0, ROWS_Y)

    @pl.when(is_light)
    def _():
        spans = [
            span_of((got0_ref, 2, 3), (got1_ref, 1, 4)),
            span_of((got1_ref, 0, 4), (got1_ref, 2, 4)),
        ]

        def item(index):
            tile, slot = divmod(index, 5)
            return spans[tile][SLOT * slot : SLOT * slot + SLOT]

        number_y = lax.broadcasted_iota(jnp.int32, (ROWS_Y, 1), 0) + narrow * ROWS_Y
        ky = 2.0 * math.pi / NY * signed(number_y, NY).astype(jnp.float32)
        decay = jnp.exp(-viscous_rate * (kx * kx + ky * ky + kz * kz))
        for c in range(3):
            for part in range(2):
                out_ref[c, part, 0] = decay * adjoint_ref[c, part, 0]
        got = [unite(item(2 * f), item(2 * f + 1)) for f in range(BACK)]
        start = jnp.where(narrow == LIGHT[0], 0, LIGHT_ROW[1])
        emit(got, pl.multiple_of(start, 8), SLOT)


def finish(place, arrays, adjoint_hat):
    whole = (3, 2, 1, ROWS_Y, NZ)
    table = tables_anal_z()
    flats = [array.reshape(-1, 128) for array in arrays]
    return pl.pallas_call(
        finish_kernel,
        grid_spec=pltpu.PrefetchScalarGridSpec(
            num_scalar_prefetch=1,
            grid=(ROWS_X,),
            in_specs=[pl.BlockSpec(flat.shape, lambda k, s: (0, 0)) for flat in flats]
            + [
                pl.BlockSpec(whole, lambda k, s: (0, 0, k, 0, 0)),
                pl.BlockSpec(table.shape, lambda k, s: (0, 0, 0)),
            ],
            out_specs=pl.BlockSpec(whole, lambda k, s: (0, 0, k, 0, 0)),
        ),
        out_shape=jax.ShapeDtypeStruct((3, 2, ROWS_X, ROWS_Y, NZ), jnp.float32),
        compiler_params=pltpu.CompilerParams(vmem_limit_bytes=vmem_bytes),
        name="finish",
    )(place, *flats, adjoint_hat, jnp.asarray(table))


def swap(chunks):
    return lax.all_to_all(chunks, ("wide", "narrow"), 0, 0, tiled=True)


def forward(tiles):
    return lax.ppermute(tiles, "narrow", [(LIGHT[0], HEAVY[0]), (LIGHT[1], HEAVY[1])])


def local(adjoint_hat, velocity_hat):
    place = jnp.stack([lax.axis_index("wide"), lax.axis_index("narrow")]).astype(jnp.int32)
    got = [swap(synth_z(place, adjoint_hat, velocity_hat, plane)) for plane in range(2)]
    out0, rest = run_plane(0, got[0])
    back0 = swap(out0)
    (out1,) = run_plane(1, got[1], rest)
    back1 = swap(out1)
    more0 = forward(back0[:, : 2 * ROWS_X])
    more1 = forward(back1[:, 3 * ROWS_X :])
    return finish(place, [back0, back1, more0, more1], adjoint_hat)


def solution(mesh):
    in_specs = (P(None, None, "wide", "narrow", None), P(None, None, "wide", "narrow", None))
    out_specs = P(None, None, "wide", "narrow", None)
    return jax.shard_map(local, mesh=mesh, in_specs=in_specs, out_specs=out_specs, check_vma=False)
```

```python
import functools
import math

import jax
import jax.numpy as jnp
import ml_dtypes
import numpy as np
from jax import lax
from jax.experimental import pallas as pl
from jax.experimental.pallas import tpu as pltpu
from jax.sharding import PartitionSpec as P

NX = 512
NY = 256
NZ = 256
KX = 256
ROWS_X = 8
ROWS_Y = 64
WIDE = 32
NARROW = 4
DEVICES = WIDE * NARROW
SENT = 8
BACK = 5
KEPT_X = 176
KEPT_W = KEPT_X // ROWS_X
HEAVY = (0, 3)
LIGHT = (1, 2)
LIGHT_ROW = (0, 40)
SLOT = 24
TILES = 7

section_step = 0.25
viscous_rate = 0.05
vmem_bytes = 60 * 1024 * 1024


def halves(table):
    upper = table.astype(ml_dtypes.bfloat16)
    lower = (table - upper.astype(np.float64)).astype(ml_dtypes.bfloat16)
    return np.stack([upper, lower])


def turn(modes, places, length):
    angle = 2.0 * np.pi / length * (np.outer(modes, places) % length)
    return np.cos(angle), np.sin(angle)


def tables_synth_z():
    quarter = np.arange(128)
    parts = []
    for plane in range(2):
        cosine, sine = turn(2 * np.arange(128) + plane, quarter, NZ)
        upper, lower = halves(np.concatenate([cosine, sine], 0))
        parts.append(np.concatenate([upper, upper, lower], 1))
    return np.stack(parts)


def tables_synth_y():
    mode = np.arange(128)
    parts = []
    for parity in range(2):
        cosine, sine = turn(mode, 2 * np.arange(128) + parity, NY)
        real_rows = np.concatenate([cosine, sine], 1)
        imag_rows = np.concatenate([-sine, cosine], 1)
        stacked = np.stack([real_rows.reshape(2, 64, 256), imag_rows.reshape(2, 64, 256)], 1)
        parts.append(halves(stacked.reshape(256, 256)))
    return np.stack(parts)


def norm_scale():
    return 1.0 / math.sqrt(NX * NY * NZ)


def tables_synth_x():
    weight = np.where(np.arange(KX) == 0, 1.0, 2.0) * norm_scale()
    cosine, sine = turn(np.arange(256), np.arange(KX), NX)
    return np.stack([halves(cosine * weight), halves(-sine * weight)])


def tables_anal_x():
    cosine, sine = turn(np.arange(KEPT_X), np.arange(256), NX)
    return np.stack([halves(cosine * norm_scale()), halves(-sine * norm_scale())])


def tables_anal_y():
    parts = []
    mode = np.arange(128)
    for parity in range(2):
        cosine, sine = turn(2 * np.arange(128) + parity, mode, NY)
        cosine = cosine.reshape(128, 2, 1, 64)
        sine = sine.reshape(128, 2, 1, 64)
        real_rows = np.concatenate([cosine, -sine], 2).reshape(128, 256)
        imag_rows = np.concatenate([sine, cosine], 2).reshape(128, 256)
        parts.append(halves(np.concatenate([real_rows, imag_rows], 0)))
    return np.stack(parts)


def tables_anal_z():
    parts = []
    for plane in range(2):
        cosine, sine = turn(2 * np.arange(128) + plane, np.arange(128), NZ)
        upper, lower = halves(np.concatenate([cosine, sine], 1))
        parts.append(np.concatenate([upper, upper, lower], 0))
    return np.stack(parts)


def split(value):
    upper = value.astype(jnp.bfloat16)
    lower = (value - upper.astype(jnp.float32)).astype(jnp.bfloat16)
    return upper, lower


def dot(left, right, dims):
    return lax.dot_general(left, right, (dims, ((), ())), preferred_element_type=jnp.float32)


def dot3(left, right, dims=((1,), (0,))):
    return (
        dot(left[0], right[0], dims)
        + dot(left[0], right[1], dims)
        + dot(left[1], right[0], dims)
    )


def signed(number, length):
    return jnp.where(number < length // 2, number, number - length)


def wave_y(start, shape, axis):
    number = lax.broadcasted_iota(jnp.int32, shape, axis) + start
    return 2.0 * math.pi / NY * signed(number, NY).astype(jnp.float32)


def wave_z(shape, axis):
    number = lax.broadcasted_iota(jnp.int32, shape, axis)
    return 2.0 * math.pi / NZ * signed(number, NZ).astype(jnp.float32)


def synth_z_kernel(
    place_ref, adjoint_ref, velocity_ref, table_ref, out_ref, adj_ref, vel_ref, sent_ref, sems
):
    def load(k, which):
        source, target = ((adjoint_ref, adj_ref), (velocity_ref, vel_ref))[which]
        return pltpu.make_async_copy(source.at[:, :, k], target.at[:, :, k], sems.at[which, k])

    def store(k):
        rows = pl.ds(k * SENT, SENT)
        return pltpu.make_async_copy(
            sent_ref.at[:, :, rows], out_ref.at[:, :, rows], sems.at[2, k]
        )

    for k in range(ROWS_X):
        for which in range(2):
            load(k, which).start()
    ky = wave_y(place_ref[1] * ROWS_Y, (ROWS_Y, 1), 0)
    kz = wave_z((1, NZ), 1)
    half_sign = jnp.where(lax.broadcasted_iota(jnp.int32, (1, 128), 1) < 64, -1.0, 1.0)

    for k in range(ROWS_X):
        number_x = place_ref[0] * ROWS_X + k
        kx = 2.0 * math.pi / NX * number_x.astype(jnp.float32)
        for which in range(2):
            load(k, which).wait()
        vel = [[vel_ref[c, part, k] for part in range(2)] for c in range(3)]
        fields = [(adj_ref[c, 0, k], adj_ref[c, 1, k]) for c in range(3)]
        fields += [(vel[c][0], vel[c][1]) for c in range(3)]
        fields.append((kz * vel[1][1] - ky * vel[2][1], ky * vel[2][0] - kz * vel[1][0]))
        fields.append((kx * vel[2][1] - kz * vel[0][1], kz * vel[0][0] - kx * vel[2][0]))
        for pair in range(SENT // 2):
            rows = [part for field in fields[2 * pair : 2 * pair + 2] for part in field]
            value = jnp.concatenate(rows, 0)
            for plane in range(2):
                if plane == 0:
                    merged = value[:, :128] + value[:, 128:]
                else:
                    merged = value[:, :128] - value[:, 128:]
                upper, lower = split(merged)
                both = dot(
                    table_ref[plane],
                    jnp.concatenate([upper, lower, upper], 1),
                    ((1,), (1,)),
                )
                for f in range(2):
                    lanes = slice(128 * f, 128 * f + 128)
                    sent_ref[:, plane, k * SENT + 2 * pair + f, :] = both[
                        :128, lanes
                    ] + half_sign * pltpu.roll(both[128:, lanes], 64, 1)
        store(k).start()
    for k in range(ROWS_X):
        store(k).wait()


def synth_z(place, adjoint_hat, velocity_hat):
    table = tables_synth_z()
    shape = (DEVICES, 2, ROWS_X * SENT, 128)
    block = (3, 2, ROWS_X, ROWS_Y, NZ)
    return pl.pallas_call(
        synth_z_kernel,
        in_specs=[
            pl.BlockSpec(memory_space=pltpu.SMEM),
            pl.BlockSpec(memory_space=pl.ANY),
            pl.BlockSpec(memory_space=pl.ANY),
            pl.BlockSpec(memory_space=pltpu.VMEM),
        ],
        out_specs=pl.BlockSpec(memory_space=pl.ANY),
        out_shape=jax.ShapeDtypeStruct(shape, jnp.float32),
        scratch_shapes=[
            pltpu.VMEM(block, jnp.float32),
            pltpu.VMEM(block, jnp.float32),
            pltpu.VMEM(shape, jnp.float32),
            pltpu.SemaphoreType.DMA((3, ROWS_X)),
        ],
        compiler_params=pltpu.CompilerParams(vmem_limit_bytes=vmem_bytes),
        name="synth_z",
    )(place, adjoint_hat, velocity_hat, jnp.asarray(table))


def plane_kernel(got_ref, sy_ref, sx_ref, ax_ref, ay_ref, out_ref, spec_ref, cell_ref):
    plane = pl.program_id(0)
    half_sign = jnp.where(lax.broadcasted_iota(jnp.int32, (1, 128), 1) < 64, -1.0, 1.0)
    ky_lanes = []
    for n in range(NARROW):
        number = lax.broadcasted_iota(jnp.int32, (1, 128), 1) % 64 + n * ROWS_Y
        ky_lanes.append(2.0 * math.pi / NY * signed(number, NY).astype(jnp.float32))
    kx_rows = 2.0 * math.pi / NX * lax.broadcasted_iota(jnp.int32, (KX, 1), 0).astype(jnp.float32)
    alternate = jnp.where(lax.broadcasted_iota(jnp.int32, (KX, 1), 0) % 2 == 0, 1.0, -1.0)
    weight = (
        jnp.where(lax.broadcasted_iota(jnp.int32, (KX, 1), 0) == 0, 1.0, 2.0) * norm_scale()
    )
    first_row = lax.broadcasted_iota(jnp.int32, (256, 1), 0) == 0

    def rows_of(field, n):
        return jnp.concatenate(
            [
                got_ref[w * NARROW + n, 0, pl.ds(field, ROWS_X, stride=SENT), :]
                for w in range(WIDE)
            ],
            0,
        )

    def synth(parts, index):
        spans = []
        for parity in range(2):
            if parity == 0:
                merged = [parts[0] + parts[2], parts[1] + parts[3]]
            else:
                merged = [parts[0] - parts[2], parts[1] - parts[3]]
            spans.append(
                dot3(
                    split(jnp.concatenate(merged, 1)), (sy_ref[parity, 0], sy_ref[parity, 1])
                )
            )
        real = jnp.concatenate([spans[0][:, :128], spans[1][:, :128]], 1)
        imag = jnp.concatenate([spans[0][:, 128:], spans[1][:, 128:]], 1)
        cosine = dot3((sx_ref[0, 0], sx_ref[0, 1]), split(real))
        sine = dot3((sx_ref[1, 0], sx_ref[1, 1]), split(imag))
        middle = jnp.sum(real * (alternate * weight), 0, keepdims=True)
        cell_ref[index, 0] = cosine + sine
        cell_ref[index, 1] = jnp.where(first_row, middle, cosine - sine)

    def each_field(field, carry):
        synth([rows_of(field, n) for n in range(NARROW)], field)
        return carry

    lax.fori_loop(0, SENT, each_field, 0, unroll=True)
    swirl = []
    for n in range(NARROW):
        across = kx_rows * rows_of(4, n) - ky_lanes[n] * rows_of(3, n)
        swirl.append(pltpu.roll(across, 64, 1) * half_sign)
    synth(swirl, SENT)

    def product(kind, c, mirror):
        one, two = (c + 1) % 3, (c + 2) % 3
        if kind == 0:
            return (
                cell_ref[one, mirror] * cell_ref[6 + two, mirror]
                - cell_ref[two, mirror] * cell_ref[6 + one, mirror]
            )
        return (
            cell_ref[3 + one, mirror] * cell_ref[two, mirror]
            - cell_ref[3 + two, mirror] * cell_ref[one, mirror]
        )

    def analyse(index, kind, c):
        ahead = product(kind, c, 0)
        behind = product(kind, c, 1)
        middle = behind[0:1]
        both = ahead + jnp.where(first_row, 0.0, behind)
        apart = ahead - behind
        real = dot3((ax_ref[0, 0], ax_ref[0, 1]), split(both))
        real = real + alternate[:KEPT_X] * norm_scale() * middle
        imag = dot3((ax_ref[1, 0], ax_ref[1, 1]), split(apart))
        spans = []
        for parity in range(2):
            lanes = slice(128 * parity, 128 * parity + 128)
            spans.append(
                dot3(
                    split(jnp.concatenate([real[:, lanes], imag[:, lanes]], 1)),
                    (ay_ref[parity, 0], ay_ref[parity, 1]),
                )
            )
        spec_ref[index, 0] = spans[0] + spans[1]
        spec_ref[index, 1] = spans[0] - spans[1]

    for kind in range(2):
        for c in range(3):
            analyse(3 * kind + c, kind, c)

    kx_kept = kx_rows[:KEPT_X]

    def times_i(value):
        return pltpu.roll(value, 64, 1) * half_sign

    @pl.when(plane == 0)
    def _():
        out_ref[KEPT_W:] = jnp.zeros((WIDE - KEPT_W,) + out_ref.shape[1:], jnp.float32)

    def put(n, tile, value):
        rows = pl.ds(pl.multiple_of(tile * ROWS_X, ROWS_X), ROWS_X)
        out_ref[:KEPT_W, n, rows, :] = value.reshape(KEPT_W, ROWS_X, 128)

    def values_of(n):
        at = (n // 2, slice(None), slice(128 * (n % 2), 128 * (n % 2) + 128))
        item = [spec_ref[(index,) + at] for index in range(6)]
        ky = ky_lanes[n]
        return [
            item[0] + times_i(ky * item[5]),
            item[1] - times_i(kx_kept * item[5]),
            item[2] + times_i(kx_kept * item[4] - ky * item[3]),
            item[3],
            item[4],
        ]

    lane = lax.broadcasted_iota(jnp.int32, (1, 128), 1)
    for half in range(2):
        heavy, light = HEAVY[half], LIGHT[half]
        values = values_of(heavy)
        for f in range(3):
            put(heavy, 3 * plane + f, values[f])

        @pl.when(plane == 0)
        def _(heavy=heavy, value=values[3]):
            put(heavy, 6, value)

        @pl.when(plane == 1)
        def _(light=light, value=values[3]):
            put(light, 1, value)

        put(light, 2 * plane, values[4])
        values = values_of(light)
        packed = []
        for tile in range(2):
            value = jnp.zeros((KEPT_X, 128), jnp.float32)
            for slot in range(5):
                f, part = divmod(5 * tile + slot, 2)
                moved = pltpu.roll(
                    values[f], (SLOT * slot - 64 * part - LIGHT_ROW[half]) % 128, 1
                )
                value = jnp.where((lane >= SLOT * slot) & (lane < SLOT * slot + SLOT), moved, value)
            packed.append(value)
        for tile in range(2):
            put(light, 3 + 2 * plane + tile, packed[tile])


def run_planes(got):
    tables = [tables_synth_y(), tables_synth_x(), tables_anal_x(), tables_anal_y()]
    shape = (WIDE, NARROW, TILES * ROWS_X, 128)
    return pl.pallas_call(
        plane_kernel,
        grid=(2,),
        out_shape=jax.ShapeDtypeStruct(shape, jnp.float32),
        in_specs=[pl.BlockSpec((DEVICES, 1, ROWS_X * SENT, 128), lambda i: (0, i, 0, 0))]
        + [pl.BlockSpec(table.shape, lambda i: (0, 0, 0, 0)) for table in tables],
        out_specs=pl.BlockSpec(shape, lambda i: (0, 0, 0, 0)),
        scratch_shapes=[
            pltpu.VMEM((6, 2, KEPT_X, 256), jnp.float32),
            pltpu.VMEM((9, 2, 256, 256), jnp.float32),
        ],
        compiler_params=pltpu.CompilerParams(vmem_limit_bytes=vmem_bytes),
        name="plane",
    )(got, *[jnp.asarray(table) for table in tables])


def finish_kernel(
    place_ref,
    back_ref,
    more_ref,
    adjoint_ref,
    table_ref,
    out_ref,
    got_ref,
    fwd_ref,
    old_ref,
    new_ref,
    sems,
    whole_sems,
):
    narrow = place_ref[1]
    is_light = (narrow == LIGHT[0]) | (narrow == LIGHT[1])

    def load(k):
        return pltpu.make_async_copy(
            adjoint_ref.at[:, :, k], old_ref.at[:, :, k], sems.at[0, k]
        )

    def store(k):
        return pltpu.make_async_copy(new_ref.at[:, :, k], out_ref.at[:, :, k], sems.at[1, k])

    wholes = [
        pltpu.make_async_copy(back_ref, got_ref, whole_sems.at[0]),
        pltpu.make_async_copy(more_ref, fwd_ref, whole_sems.at[1]),
    ]
    for copy in wholes:
        copy.start()
    for k in range(ROWS_X):
        load(k).start()
    for copy in wholes:
        copy.wait()
    number_z = signed(lax.broadcasted_iota(jnp.int32, (1, NZ), 1), NZ)
    kz = 2.0 * math.pi / NZ * number_z.astype(jnp.float32)

    def span_of(k, first, second):
        spans = []
        for plane, (ref, tile) in enumerate((first, second)):
            rows = ref[:, tile * ROWS_X + k, :]
            upper, lower = split(rows.T)
            spans.append(dot(jnp.concatenate([upper, lower, upper], 1), table_ref[plane], ((1,), (0,))))
        return spans

    def unite(spans, real_rows, imag_rows):
        parts = []
        for span in spans:
            real, imag = span[real_rows], span[imag_rows]
            parts.append((real[:, :128] + imag[:, 128:], imag[:, :128] - real[:, 128:]))
        (real_0, imag_0), (real_1, imag_1) = parts
        return (
            jnp.concatenate([real_0 + real_1, real_0 - real_1], 1),
            jnp.concatenate([imag_0 + imag_1, imag_0 - imag_1], 1),
        )

    def emit(k, got, start, rows):
        number_x = place_ref[0] * ROWS_X + k
        kx = 2.0 * math.pi / NX * number_x.astype(jnp.float32)
        number_y = lax.broadcasted_iota(jnp.int32, (rows, 1), 0) + start + narrow * ROWS_Y
        number_y = signed(number_y, NY)
        ky = 2.0 * math.pi / NY * number_y.astype(jnp.float32)
        conv = [
            (got[0][0] + kz * got[4][1], got[0][1] - kz * got[4][0]),
            (got[1][0] - kz * got[3][1], got[1][1] + kz * got[3][0]),
            got[2],
        ]
        keep = (
            (3 * number_x < NX) & (3 * jnp.abs(number_y) < NY) & (3 * jnp.abs(number_z) < NZ)
        ).astype(jnp.float32)
        ksquare = kx * kx + ky * ky + kz * kz
        inverse = 1.0 / (ksquare + (ksquare == 0).astype(jnp.float32))
        decay = jnp.exp(-viscous_rate * ksquare)
        waves = (kx, ky, kz)
        for part in range(2):
            along = (kx * conv[0][part] + ky * conv[1][part] + kz * conv[2][part]) * inverse
            for c in range(3):
                projected = keep * (conv[c][part] - waves[c] * along)
                old = old_ref[c, part, k, pl.ds(start, rows), :]
                new_ref[c, part, k, pl.ds(start, rows), :] = decay * (
                    old + section_step * projected
                )

    @pl.when(jnp.logical_not(is_light))
    def _():
        for k in range(ROWS_X):
            got = []
            for f in range(BACK):
                first = (got_ref, (0, 1, 2, 6)[f]) if f < 4 else (fwd_ref, 0)
                second = (got_ref, 3 + f) if f < 3 else (fwd_ref, f - 2)
                spans = span_of(k, first, second)
                got.append(unite(spans, slice(0, 64), slice(64, 128)))
            load(k).wait()
            emit(k, got, 0, ROWS_Y)
            store(k).start()

    @pl.when(is_light)
    def _():
        for k in range(ROWS_X):
            tiles = [
                span_of(k, (got_ref, 3), (got_ref, 5)),
                span_of(k, (got_ref, 4), (got_ref, 6)),
            ]
            number_x = place_ref[0] * ROWS_X + k
            kx = 2.0 * math.pi / NX * number_x.astype(jnp.float32)
            number_y = lax.broadcasted_iota(jnp.int32, (ROWS_Y, 1), 0) + narrow * ROWS_Y
            ky = 2.0 * math.pi / NY * signed(number_y, NY).astype(jnp.float32)
            decay = jnp.exp(-viscous_rate * (kx * kx + ky * ky + kz * kz))
            load(k).wait()
            for c in range(3):
                for part in range(2):
                    new_ref[c, part, k] = decay * old_ref[c, part, k]
            got = []
            for f in range(BACK):
                (tile, slot), (tile_i, slot_i) = divmod(2 * f, 5), divmod(2 * f + 1, 5)
                real = [span[SLOT * slot : SLOT * slot + SLOT] for span in tiles[tile]]
                imag = [span[SLOT * slot_i : SLOT * slot_i + SLOT] for span in tiles[tile_i]]
                pairs = [jnp.concatenate([r, i], 0) for r, i in zip(real, imag)]
                got.append(unite(pairs, slice(0, SLOT), slice(SLOT, 2 * SLOT)))
            start = pl.multiple_of(jnp.where(narrow == LIGHT[0], 0, LIGHT_ROW[1]), 8)
            emit(k, got, start, SLOT)
            store(k).start()

    for k in range(ROWS_X):
        store(k).wait()


def finish(place, back, more, adjoint_hat):
    table = tables_anal_z()
    block = (3, 2, ROWS_X, ROWS_Y, NZ)
    return pl.pallas_call(
        finish_kernel,
        in_specs=[
            pl.BlockSpec(memory_space=pltpu.SMEM),
            pl.BlockSpec(memory_space=pl.ANY),
            pl.BlockSpec(memory_space=pl.ANY),
            pl.BlockSpec(memory_space=pl.ANY),
            pl.BlockSpec(memory_space=pltpu.VMEM),
        ],
        out_specs=pl.BlockSpec(memory_space=pl.ANY),
        out_shape=jax.ShapeDtypeStruct(block, jnp.float32),
        scratch_shapes=[
            pltpu.VMEM(back.shape, jnp.float32),
            pltpu.VMEM(more.shape, jnp.float32),
            pltpu.VMEM(block, jnp.float32),
            pltpu.VMEM(block, jnp.float32),
            pltpu.SemaphoreType.DMA((2, ROWS_X)),
            pltpu.SemaphoreType.DMA((2,)),
        ],
        compiler_params=pltpu.CompilerParams(vmem_limit_bytes=vmem_bytes),
        name="finish",
    )(place, back, more, adjoint_hat, jnp.asarray(table))


def swap(chunks):
    return lax.all_to_all(chunks, ("wide", "narrow"), 0, 0, tiled=True)


def forward(tiles):
    return lax.ppermute(tiles, "narrow", [(LIGHT[0], HEAVY[0]), (LIGHT[1], HEAVY[1])])


def local(adjoint_hat, velocity_hat):
    place = jnp.stack([lax.axis_index("wide"), lax.axis_index("narrow")]).astype(jnp.int32)
    got = swap(synth_z(place, adjoint_hat, velocity_hat))
    back = swap(run_planes(got).reshape(DEVICES, TILES * ROWS_X, 128))
    more = forward(back[:, : 3 * ROWS_X])
    return finish(place, back, more, adjoint_hat)


def solution(mesh):
    in_specs = (P(None, None, "wide", "narrow", None), P(None, None, "wide", "narrow", None))
    out_specs = P(None, None, "wide", "narrow", None)
    return jax.shard_map(local, mesh=mesh, in_specs=in_specs, out_specs=out_specs, check_vma=False)
```

```python
import functools
import math

import jax
import jax.numpy as jnp
import ml_dtypes
import numpy as np
from jax import lax
from jax.experimental import pallas as pl
from jax.experimental.pallas import tpu as pltpu
from jax.sharding import PartitionSpec as P

NX = 512
NY = 256
NZ = 256
KX = 256
ROWS_X = 8
ROWS_Y = 64
WIDE = 32
NARROW = 4
DEVICES = WIDE * NARROW
SENT = 8
BACK = 5
KEPT_X = 176
KEPT_W = KEPT_X // ROWS_X
HEAVY = (0, 3)
LIGHT = (1, 2)
LIGHT_ROW = (0, 40)
SLOT = 24
TILES = 7

section_step = 0.25
viscous_rate = 0.05
vmem_bytes = 60 * 1024 * 1024


def halves(table):
    upper = table.astype(ml_dtypes.bfloat16)
    lower = (table - upper.astype(np.float64)).astype(ml_dtypes.bfloat16)
    return np.stack([upper, lower])


def turn(modes, places, length):
    angle = 2.0 * np.pi / length * (np.outer(modes, places) % length)
    return np.cos(angle), np.sin(angle)


def tables_synth_z():
    quarter = np.arange(128)
    parts = []
    for plane in range(2):
        cosine, sine = turn(2 * np.arange(128) + plane, quarter, NZ)
        upper, lower = halves(np.concatenate([cosine, sine], 0))
        parts.append(np.concatenate([upper, upper, lower], 1))
    return np.stack(parts)


def tables_synth_y():
    mode = np.arange(128)
    parts = []
    for parity in range(2):
        cosine, sine = turn(mode, 2 * np.arange(128) + parity, NY)
        real_rows = np.concatenate([cosine, sine], 1)
        imag_rows = np.concatenate([-sine, cosine], 1)
        stacked = np.stack([real_rows.reshape(2, 64, 256), imag_rows.reshape(2, 64, 256)], 1)
        parts.append(halves(stacked.reshape(256, 256)))
    return np.stack(parts)


def norm_scale():
    return 1.0 / math.sqrt(NX * NY * NZ)


def tables_synth_x():
    weight = np.where(np.arange(KX) == 0, 1.0, 2.0) * norm_scale()
    cosine, sine = turn(np.arange(256), np.arange(KX), NX)
    return np.stack([halves(cosine * weight), halves(-sine * weight)])


def tables_anal_x():
    cosine, sine = turn(np.arange(KEPT_X), np.arange(256), NX)
    return np.stack([halves(cosine * norm_scale()), halves(-sine * norm_scale())])


def tables_anal_y():
    parts = []
    mode = np.arange(128)
    for parity in range(2):
        cosine, sine = turn(2 * np.arange(128) + parity, mode, NY)
        cosine = cosine.reshape(128, 2, 1, 64)
        sine = sine.reshape(128, 2, 1, 64)
        real_rows = np.concatenate([cosine, -sine], 2).reshape(128, 256)
        imag_rows = np.concatenate([sine, cosine], 2).reshape(128, 256)
        parts.append(halves(np.concatenate([real_rows, imag_rows], 0)))
    return np.stack(parts)


def tables_anal_z():
    parts = []
    for plane in range(2):
        cosine, sine = turn(2 * np.arange(128) + plane, np.arange(128), NZ)
        upper, lower = halves(np.concatenate([cosine, sine], 1))
        parts.append(np.concatenate([upper, upper, lower], 0))
    return np.stack(parts)


def split(value):
    upper = value.astype(jnp.bfloat16)
    lower = (value - upper.astype(jnp.float32)).astype(jnp.bfloat16)
    return upper, lower


def dot(left, right, dims):
    return lax.dot_general(left, right, (dims, ((), ())), preferred_element_type=jnp.float32)


def dot3(left, right, dims=((1,), (0,))):
    return (
        dot(left[0], right[0], dims)
        + dot(left[0], right[1], dims)
        + dot(left[1], right[0], dims)
    )


def signed(number, length):
    return jnp.where(number < length // 2, number, number - length)


def wave_y(start, shape, axis):
    number = lax.broadcasted_iota(jnp.int32, shape, axis) + start
    return 2.0 * math.pi / NY * signed(number, NY).astype(jnp.float32)


def wave_z(shape, axis):
    number = lax.broadcasted_iota(jnp.int32, shape, axis)
    return 2.0 * math.pi / NZ * signed(number, NZ).astype(jnp.float32)


def synth_z_kernel(
    place_ref, adjoint_ref, velocity_ref, table_ref, out_ref, adj_ref, vel_ref, sent_ref, sems
):
    def load(k, which):
        source, target = ((adjoint_ref, adj_ref), (velocity_ref, vel_ref))[which]
        return pltpu.make_async_copy(source.at[:, :, k], target.at[:, :, k], sems.at[which, k])

    def store(k, plane):
        return pltpu.make_async_copy(
            sent_ref.at[k, plane],
            out_ref.at[:, plane, pl.ds(k * SENT, SENT)],
            sems.at[2 + plane, k],
        )

    for k in range(ROWS_X):
        for which in range(2):
            load(k, which).start()
    ky = wave_y(place_ref[1] * ROWS_Y, (ROWS_Y, 1), 0)
    kz = wave_z((1, NZ), 1)
    half_sign = jnp.where(lax.broadcasted_iota(jnp.int32, (1, 128), 1) < 64, -1.0, 1.0)

    for k in range(ROWS_X):
        number_x = place_ref[0] * ROWS_X + k
        kx = 2.0 * math.pi / NX * number_x.astype(jnp.float32)
        for which in range(2):
            load(k, which).wait()
        vel = [[vel_ref[c, part, k] for part in range(2)] for c in range(3)]
        fields = [(adj_ref[c, 0, k], adj_ref[c, 1, k]) for c in range(3)]
        fields += [(vel[c][0], vel[c][1]) for c in range(3)]
        fields.append((kz * vel[1][1] - ky * vel[2][1], ky * vel[2][0] - kz * vel[1][0]))
        fields.append((kx * vel[2][1] - kz * vel[0][1], kz * vel[0][0] - kx * vel[2][0]))
        for pair in range(SENT // 2):
            rows = [part for field in fields[2 * pair : 2 * pair + 2] for part in field]
            value = jnp.concatenate(rows, 0)
            for plane in range(2):
                if plane == 0:
                    merged = value[:, :128] + value[:, 128:]
                else:
                    merged = value[:, :128] - value[:, 128:]
                upper, lower = split(merged)
                both = dot(
                    table_ref[plane],
                    jnp.concatenate([upper, lower, upper], 1),
                    ((1,), (1,)),
                )
                for f in range(2):
                    lanes = slice(128 * f, 128 * f + 128)
                    sent_ref[k, plane, :, 2 * pair + f, :] = both[
                        :128, lanes
                    ] + half_sign * pltpu.roll(both[128:, lanes], 64, 1)
        for plane in range(2):
            store(k, plane).start()
    for k in range(ROWS_X):
        for plane in range(2):
            store(k, plane).wait()


def synth_z(place, adjoint_hat, velocity_hat):
    table = tables_synth_z()
    shape = (DEVICES, 2, ROWS_X * SENT, 128)
    block = (3, 2, ROWS_X, ROWS_Y, NZ)
    return pl.pallas_call(
        synth_z_kernel,
        in_specs=[
            pl.BlockSpec(memory_space=pltpu.SMEM),
            pl.BlockSpec(memory_space=pl.ANY),
            pl.BlockSpec(memory_space=pl.ANY),
            pl.BlockSpec(memory_space=pltpu.VMEM),
        ],
        out_specs=pl.BlockSpec(memory_space=pl.ANY),
        out_shape=jax.ShapeDtypeStruct(shape, jnp.float32),
        scratch_shapes=[
            pltpu.VMEM(block, jnp.float32),
            pltpu.VMEM(block, jnp.float32),
            pltpu.VMEM((ROWS_X, 2, DEVICES, SENT, 128), jnp.float32),
            pltpu.SemaphoreType.DMA((4, ROWS_X)),
        ],
        compiler_params=pltpu.CompilerParams(vmem_limit_bytes=vmem_bytes),
        name="synth_z",
    )(place, adjoint_hat, velocity_hat, jnp.asarray(table))


def plane_kernel(got_ref, sy_ref, sx_ref, ax_ref, ay_ref, out_ref, spec_ref, cell_ref):
    plane = pl.program_id(0)
    half_sign = jnp.where(lax.broadcasted_iota(jnp.int32, (1, 128), 1) < 64, -1.0, 1.0)
    ky_lanes = []
    for n in range(NARROW):
        number = lax.broadcasted_iota(jnp.int32, (1, 128), 1) % 64 + n * ROWS_Y
        ky_lanes.append(2.0 * math.pi / NY * signed(number, NY).astype(jnp.float32))
    kx_rows = 2.0 * math.pi / NX * lax.broadcasted_iota(jnp.int32, (KX, 1), 0).astype(jnp.float32)
    alternate = jnp.where(lax.broadcasted_iota(jnp.int32, (KX, 1), 0) % 2 == 0, 1.0, -1.0)
    weight = (
        jnp.where(lax.broadcasted_iota(jnp.int32, (KX, 1), 0) == 0, 1.0, 2.0) * norm_scale()
    )
    first_row = lax.broadcasted_iota(jnp.int32, (256, 1), 0) == 0

    def rows_of(field, n):
        return jnp.concatenate(
            [
                got_ref[w * NARROW + n, 0, pl.ds(field, ROWS_X, stride=SENT), :]
                for w in range(WIDE)
            ],
            0,
        )

    def synth(parts, index):
        spans = []
        for parity in range(2):
            if parity == 0:
                merged = [parts[0] + parts[2], parts[1] + parts[3]]
            else:
                merged = [parts[0] - parts[2], parts[1] - parts[3]]
            spans.append(
                dot3(
                    split(jnp.concatenate(merged, 1)), (sy_ref[parity, 0], sy_ref[parity, 1])
                )
            )
        real = jnp.concatenate([spans[0][:, :128], spans[1][:, :128]], 1)
        imag = jnp.concatenate([spans[0][:, 128:], spans[1][:, 128:]], 1)
        cosine = dot3((sx_ref[0, 0], sx_ref[0, 1]), split(real))
        sine = dot3((sx_ref[1, 0], sx_ref[1, 1]), split(imag))
        middle = jnp.sum(real * (alternate * weight), 0, keepdims=True)
        cell_ref[index, 0] = cosine + sine
        cell_ref[index, 1] = jnp.where(first_row, middle, cosine - sine)

    def each_field(field, carry):
        synth([rows_of(field, n) for n in range(NARROW)], field)
        return carry

    lax.fori_loop(0, SENT, each_field, 0, unroll=True)
    swirl = []
    for n in range(NARROW):
        across = kx_rows * rows_of(4, n) - ky_lanes[n] * rows_of(3, n)
        swirl.append(pltpu.roll(across, 64, 1) * half_sign)
    synth(swirl, SENT)

    def product(kind, c, mirror):
        one, two = (c + 1) % 3, (c + 2) % 3
        if kind == 0:
            return (
                cell_ref[one, mirror] * cell_ref[6 + two, mirror]
                - cell_ref[two, mirror] * cell_ref[6 + one, mirror]
            )
        return (
            cell_ref[3 + one, mirror] * cell_ref[two, mirror]
            - cell_ref[3 + two, mirror] * cell_ref[one, mirror]
        )

    def analyse(index, kind, c):
        ahead = product(kind, c, 0)
        behind = product(kind, c, 1)
        middle = behind[0:1]
        both = ahead + jnp.where(first_row, 0.0, behind)
        apart = ahead - behind
        real = dot3((ax_ref[0, 0], ax_ref[0, 1]), split(both))
        real = real + alternate[:KEPT_X] * norm_scale() * middle
        imag = dot3((ax_ref[1, 0], ax_ref[1, 1]), split(apart))
        spans = []
        for parity in range(2):
            lanes = slice(128 * parity, 128 * parity + 128)
            spans.append(
                dot3(
                    split(jnp.concatenate([real[:, lanes], imag[:, lanes]], 1)),
                    (ay_ref[parity, 0], ay_ref[parity, 1]),
                )
            )
        spec_ref[index, 0] = spans[0] + spans[1]
        spec_ref[index, 1] = spans[0] - spans[1]

    for kind in range(2):
        for c in range(3):
            analyse(3 * kind + c, kind, c)

    kx_kept = kx_rows[:KEPT_X]

    def times_i(value):
        return pltpu.roll(value, 64, 1) * half_sign

    @pl.when(plane == 0)
    def _():
        out_ref[KEPT_W:] = jnp.zeros((WIDE - KEPT_W,) + out_ref.shape[1:], jnp.float32)

    def put(n, tile, value):
        rows = pl.ds(pl.multiple_of(tile * ROWS_X, ROWS_X), ROWS_X)
        out_ref[:KEPT_W, n, rows, :] = value.reshape(KEPT_W, ROWS_X, 128)

    def values_of(n):
        at = (n // 2, slice(None), slice(128 * (n % 2), 128 * (n % 2) + 128))
        item = [spec_ref[(index,) + at] for index in range(6)]
        ky = ky_lanes[n]
        return [
            item[0] + times_i(ky * item[5]),
            item[1] - times_i(kx_kept * item[5]),
            item[2] + times_i(kx_kept * item[4] - ky * item[3]),
            item[3],
            item[4],
        ]

    lane = lax.broadcasted_iota(jnp.int32, (1, 128), 1)
    for half in range(2):
        heavy, light = HEAVY[half], LIGHT[half]
        values = values_of(heavy)
        for f in range(3):
            put(heavy, 3 * plane + f, values[f])

        @pl.when(plane == 0)
        def _(heavy=heavy, value=values[3]):
            put(heavy, 6, value)

        @pl.when(plane == 1)
        def _(light=light, value=values[3]):
            put(light, 1, value)

        put(light, 2 * plane, values[4])
        values = values_of(light)
        packed = []
        for tile in range(2):
            value = jnp.zeros((KEPT_X, 128), jnp.float32)
            for slot in range(5):
                f, part = divmod(5 * tile + slot, 2)
                moved = pltpu.roll(
                    values[f], (SLOT * slot - 64 * part - LIGHT_ROW[half]) % 128, 1
                )
                value = jnp.where((lane >= SLOT * slot) & (lane < SLOT * slot + SLOT), moved, value)
            packed.append(value)
        for tile in range(2):
            put(light, 3 + 2 * plane + tile, packed[tile])


def run_planes(got):
    tables = [tables_synth_y(), tables_synth_x(), tables_anal_x(), tables_anal_y()]
    shape = (WIDE, NARROW, TILES * ROWS_X, 128)
    return pl.pallas_call(
        plane_kernel,
        grid=(2,),
        out_shape=jax.ShapeDtypeStruct(shape, jnp.float32),
        in_specs=[pl.BlockSpec((DEVICES, 1, ROWS_X * SENT, 128), lambda i: (0, i, 0, 0))]
        + [pl.BlockSpec(table.shape, lambda i: (0, 0, 0, 0)) for table in tables],
        out_specs=pl.BlockSpec(shape, lambda i: (0, 0, 0, 0)),
        scratch_shapes=[
            pltpu.VMEM((6, 2, KEPT_X, 256), jnp.float32),
            pltpu.VMEM((9, 2, 256, 256), jnp.float32),
        ],
        compiler_params=pltpu.CompilerParams(vmem_limit_bytes=vmem_bytes),
        name="plane",
    )(got, *[jnp.asarray(table) for table in tables])


def take_kernel(back_ref, out_ref, sem):
    copy = pltpu.make_async_copy(back_ref.at[:, pl.ds(0, 3 * ROWS_X)], out_ref, sem)
    copy.start()
    copy.wait()


def take(back):
    return pl.pallas_call(
        take_kernel,
        in_specs=[pl.BlockSpec(memory_space=pltpu.HBM)],
        out_specs=pl.BlockSpec(memory_space=pltpu.HBM),
        out_shape=jax.ShapeDtypeStruct((DEVICES, 3 * ROWS_X, 128), jnp.float32),
        scratch_shapes=[pltpu.SemaphoreType.DMA],
        name="take",
    )(back)


def span_of(got_ref, table_ref, k, *tiles):
    spans = []
    for plane, tile in enumerate(tiles):
        upper, lower = split(got_ref[tile, :, k, :].T)
        stacked = jnp.concatenate([upper, lower, upper], 1)
        spans.append(dot(stacked, table_ref[plane], ((1,), (0,))))
    return spans


def unite(spans, real_rows, imag_rows):
    parts = []
    for span in spans:
        real, imag = span[real_rows], span[imag_rows]
        parts.append((real[:, :128] + imag[:, 128:], imag[:, :128] - real[:, 128:]))
    (real_0, imag_0), (real_1, imag_1) = parts
    return (
        jnp.concatenate([real_0 + real_1, real_0 - real_1], 1),
        jnp.concatenate([imag_0 + imag_1, imag_0 - imag_1], 1),
    )


def light_narrow(narrow):
    return (narrow == LIGHT[0]) | (narrow == LIGHT[1])


def begin_kernel(place_ref, back_ref, table_ref, part_ref, got_ref, new_ref, sems, whole_sems):
    is_light = light_narrow(place_ref[1])

    def store(k):
        return pltpu.make_async_copy(new_ref.at[:, :, k], part_ref.at[:, :, k], sems.at[k])

    pieces = [
        pltpu.make_async_copy(
            back_ref.at[:, pl.ds(tile * ROWS_X, ROWS_X)], got_ref.at[tile], whole_sems.at[tile]
        )
        for tile in range(TILES)
    ]
    for copy in pieces:
        copy.start()
    for copy in pieces:
        copy.wait()

    @pl.when(jnp.logical_not(is_light))
    def _():
        for k in range(ROWS_X):
            for f in range(3):
                spans = span_of(got_ref, table_ref, k, f, 3 + f)
                real, imag = unite(spans, slice(0, 64), slice(64, 128))
                new_ref[f, 0, k] = real
                new_ref[f, 1, k] = imag
            store(k).start()

    @pl.when(is_light)
    def _():
        for k in range(ROWS_X):
            tiles = [
                span_of(got_ref, table_ref, k, 3, 5),
                span_of(got_ref, table_ref, k, 4, 6),
            ]
            for f in range(BACK):
                (tile, slot), (tile_i, slot_i) = divmod(2 * f, 5), divmod(2 * f + 1, 5)
                real = [span[SLOT * slot : SLOT * slot + SLOT] for span in tiles[tile]]
                imag = [span[SLOT * slot_i : SLOT * slot_i + SLOT] for span in tiles[tile_i]]
                pairs = [jnp.concatenate([r, i], 0) for r, i in zip(real, imag)]
                real, imag = unite(pairs, slice(0, SLOT), slice(SLOT, 2 * SLOT))
                at = slice(SLOT * (f // 3), SLOT * (f // 3) + SLOT)
                new_ref[f % 3, 0, k, at] = real
                new_ref[f % 3, 1, k, at] = imag
            store(k).start()

    for k in range(ROWS_X):
        store(k).wait()


def begin(place, back):
    table = tables_anal_z()
    block = (3, 2, ROWS_X, ROWS_Y, NZ)
    return pl.pallas_call(
        begin_kernel,
        in_specs=[
            pl.BlockSpec(memory_space=pltpu.SMEM),
            pl.BlockSpec(memory_space=pltpu.HBM),
            pl.BlockSpec(memory_space=pltpu.VMEM),
        ],
        out_specs=pl.BlockSpec(memory_space=pltpu.HBM),
        out_shape=jax.ShapeDtypeStruct(block, jnp.float32),
        scratch_shapes=[
            pltpu.VMEM((TILES, DEVICES, ROWS_X, 128), jnp.float32),
            pltpu.VMEM(block, jnp.float32),
            pltpu.SemaphoreType.DMA((ROWS_X,)),
            pltpu.SemaphoreType.DMA((TILES,)),
        ],
        compiler_params=pltpu.CompilerParams(vmem_limit_bytes=vmem_bytes),
        name="begin",
    )(place, back, jnp.asarray(table))


def finish_kernel(
    place_ref,
    back_ref,
    more_ref,
    part_ref,
    adjoint_ref,
    table_ref,
    out_ref,
    got_ref,
    mid_ref,
    old_ref,
    new_ref,
    sems,
    whole_sems,
):
    narrow = place_ref[1]
    is_light = light_narrow(narrow)

    def load(k, which):
        source, target = ((adjoint_ref, old_ref), (part_ref, mid_ref))[which]
        return pltpu.make_async_copy(source.at[:, :, k], target.at[:, :, k], sems.at[which, k])

    def store(k):
        return pltpu.make_async_copy(new_ref.at[:, :, k], out_ref.at[:, :, k], sems.at[2, k])

    pieces = [
        pltpu.make_async_copy(
            more_ref.at[:, pl.ds(tile * ROWS_X, ROWS_X)], got_ref.at[tile], whole_sems.at[tile]
        )
        for tile in range(3)
    ]
    pieces.append(
        pltpu.make_async_copy(
            back_ref.at[:, pl.ds(6 * ROWS_X, ROWS_X)], got_ref.at[3], whole_sems.at[3]
        )
    )
    for copy in pieces:
        copy.start()
    for k in range(ROWS_X):
        load(k, 0).start()
        load(k, 1).start()
    for copy in pieces:
        copy.wait()
    number_z = signed(lax.broadcasted_iota(jnp.int32, (1, NZ), 1), NZ)
    kz = 2.0 * math.pi / NZ * number_z.astype(jnp.float32)

    def emit(k, got, start, rows):
        number_x = place_ref[0] * ROWS_X + k
        kx = 2.0 * math.pi / NX * number_x.astype(jnp.float32)
        number_y = lax.broadcasted_iota(jnp.int32, (rows, 1), 0) + start + narrow * ROWS_Y
        number_y = signed(number_y, NY)
        ky = 2.0 * math.pi / NY * number_y.astype(jnp.float32)
        conv = [
            (got[0][0] + kz * got[4][1], got[0][1] - kz * got[4][0]),
            (got[1][0] - kz * got[3][1], got[1][1] + kz * got[3][0]),
            got[2],
        ]
        keep = (
            (3 * number_x < NX) & (3 * jnp.abs(number_y) < NY) & (3 * jnp.abs(number_z) < NZ)
        ).astype(jnp.float32)
        ksquare = kx * kx + ky * ky + kz * kz
        inverse = 1.0 / (ksquare + (ksquare == 0).astype(jnp.float32))
        decay = jnp.exp(-viscous_rate * ksquare)
        waves = (kx, ky, kz)
        for part in range(2):
            along = (kx * conv[0][part] + ky * conv[1][part] + kz * conv[2][part]) * inverse
            for c in range(3):
                projected = keep * (conv[c][part] - waves[c] * along)
                old = old_ref[c, part, k, pl.ds(start, rows), :]
                new_ref[c, part, k, pl.ds(start, rows), :] = decay * (
                    old + section_step * projected
                )

    @pl.when(jnp.logical_not(is_light))
    def _():
        for k in range(ROWS_X):
            across = [
                unite(span_of(got_ref, table_ref, k, first, second), slice(0, 64), slice(64, 128))
                for first, second in ((3, 1), (0, 2))
            ]
            load(k, 0).wait()
            load(k, 1).wait()
            got = [(mid_ref[f, 0, k], mid_ref[f, 1, k]) for f in range(3)] + across
            emit(k, got, 0, ROWS_Y)
            store(k).start()

    @pl.when(is_light)
    def _():
        number_y = lax.broadcasted_iota(jnp.int32, (ROWS_Y, 1), 0) + narrow * ROWS_Y
        ky = 2.0 * math.pi / NY * signed(number_y, NY).astype(jnp.float32)
        for k in range(ROWS_X):
            number_x = place_ref[0] * ROWS_X + k
            kx = 2.0 * math.pi / NX * number_x.astype(jnp.float32)
            decay = jnp.exp(-viscous_rate * (kx * kx + ky * ky + kz * kz))
            load(k, 0).wait()
            load(k, 1).wait()
            for c in range(3):
                for part in range(2):
                    new_ref[c, part, k] = decay * old_ref[c, part, k]
            got = []
            for f in range(BACK):
                at = slice(SLOT * (f // 3), SLOT * (f // 3) + SLOT)
                got.append((mid_ref[f % 3, 0, k, at], mid_ref[f % 3, 1, k, at]))
            start = pl.multiple_of(jnp.where(narrow == LIGHT[0], 0, LIGHT_ROW[1]), 8)
            emit(k, got, start, SLOT)
            store(k).start()

    for k in range(ROWS_X):
        store(k).wait()


def finish(place, back, more, part, adjoint_hat):
    table = tables_anal_z()
    block = (3, 2, ROWS_X, ROWS_Y, NZ)
    return pl.pallas_call(
        finish_kernel,
        in_specs=[
            pl.BlockSpec(memory_space=pltpu.SMEM),
            pl.BlockSpec(memory_space=pltpu.HBM),
            pl.BlockSpec(memory_space=pltpu.HBM),
            pl.BlockSpec(memory_space=pltpu.HBM),
            pl.BlockSpec(memory_space=pltpu.HBM),
            pl.BlockSpec(memory_space=pltpu.VMEM),
        ],
        out_specs=pl.BlockSpec(memory_space=pltpu.HBM),
        out_shape=jax.ShapeDtypeStruct(block, jnp.float32),
        scratch_shapes=[
            pltpu.VMEM((4, DEVICES, ROWS_X, 128), jnp.float32),
            pltpu.VMEM(block, jnp.float32),
            pltpu.VMEM(block, jnp.float32),
            pltpu.VMEM(block, jnp.float32),
            pltpu.SemaphoreType.DMA((3, ROWS_X)),
            pltpu.SemaphoreType.DMA((4,)),
        ],
        compiler_params=pltpu.CompilerParams(vmem_limit_bytes=vmem_bytes),
        name="finish",
    )(place, back, more, part, adjoint_hat, jnp.asarray(table))


def swap(chunks):
    return lax.all_to_all(chunks, ("wide", "narrow"), 0, 0, tiled=True)


def forward(tiles):
    return lax.ppermute(tiles, "narrow", [(LIGHT[0], HEAVY[0]), (LIGHT[1], HEAVY[1])])


def local(adjoint_hat, velocity_hat):
    place = jnp.stack([lax.axis_index("wide"), lax.axis_index("narrow")]).astype(jnp.int32)
    got = swap(synth_z(place, adjoint_hat, velocity_hat))
    back = swap(run_planes(got).reshape(DEVICES, TILES * ROWS_X, 128))
    more = pltpu.with_memory_space_constraint(forward(take(back)), pltpu.HBM)
    part = begin(place, back)
    return finish(place, back, more, part, adjoint_hat)


def solution(mesh):
    in_specs = (P(None, None, "wide", "narrow", None), P(None, None, "wide", "narrow", None))
    out_specs = P(None, None, "wide", "narrow", None)
    return jax.shard_map(local, mesh=mesh, in_specs=in_specs, out_specs=out_specs, check_vma=False)
```

```python
import functools
import math

import jax
import jax.numpy as jnp
import ml_dtypes
import numpy as np
from jax import lax
from jax.experimental import pallas as pl
from jax.experimental.pallas import tpu as pltpu
from jax.sharding import PartitionSpec as P

NX = 512
NY = 256
NZ = 256
KX = 256
ROWS_X = 8
ROWS_Y = 64
WIDE = 32
NARROW = 4
DEVICES = WIDE * NARROW
SENT = 8
BACK = 5
KEPT_X = 176
KEPT_W = KEPT_X // ROWS_X
HEAVY = (0, 3)
LIGHT = (1, 2)
LIGHT_ROW = (0, 40)
SLOT = 24

section_step = 0.25
viscous_rate = 0.05
vmem_bytes = 60 * 1024 * 1024


def halves(table):
    upper = table.astype(ml_dtypes.bfloat16)
    lower = (table - upper.astype(np.float64)).astype(ml_dtypes.bfloat16)
    return np.stack([upper, lower])


def turn(modes, places, length):
    angle = 2.0 * np.pi / length * (np.outer(modes, places) % length)
    return np.cos(angle), np.sin(angle)


def tables_synth_z():
    quarter = np.arange(128)
    parts = []
    for plane in range(2):
        cosine, sine = turn(2 * np.arange(128) + plane, quarter, NZ)
        upper, lower = halves(np.concatenate([cosine, sine], 0))
        parts.append(np.concatenate([upper, upper, lower], 1))
    return np.stack(parts)


def tables_synth_y():
    mode = np.arange(128)
    parts = []
    for parity in range(2):
        cosine, sine = turn(mode, 2 * np.arange(128) + parity, NY)
        real_rows = np.concatenate([cosine, sine], 1)
        imag_rows = np.concatenate([-sine, cosine], 1)
        stacked = np.stack([real_rows.reshape(2, 64, 256), imag_rows.reshape(2, 64, 256)], 1)
        parts.append(halves(stacked.reshape(256, 256)))
    return np.stack(parts)


def norm_scale():
    return 1.0 / math.sqrt(NX * NY * NZ)


def tables_synth_x():
    weight = np.where(np.arange(KX) == 0, 1.0, 2.0) * norm_scale()
    cosine, sine = turn(np.arange(256), np.arange(KX), NX)
    return np.stack([halves(cosine * weight), halves(-sine * weight)])


def tables_anal_x():
    cosine, sine = turn(np.arange(KEPT_X), np.arange(256), NX)
    return np.stack([halves(cosine * norm_scale()), halves(-sine * norm_scale())])


def tables_anal_y():
    parts = []
    mode = np.arange(128)
    for parity in range(2):
        cosine, sine = turn(2 * np.arange(128) + parity, mode, NY)
        cosine = cosine.reshape(128, 2, 1, 64)
        sine = sine.reshape(128, 2, 1, 64)
        real_rows = np.concatenate([cosine, -sine], 2).reshape(128, 256)
        imag_rows = np.concatenate([sine, cosine], 2).reshape(128, 256)
        parts.append(halves(np.concatenate([real_rows, imag_rows], 0)))
    return np.stack(parts)


def tables_anal_z():
    parts = []
    for plane in range(2):
        cosine, sine = turn(2 * np.arange(128) + plane, np.arange(128), NZ)
        upper, lower = halves(np.concatenate([cosine, sine], 1))
        parts.append(np.concatenate([upper, upper, lower], 0))
    return np.stack(parts)


def split(value):
    upper = value.astype(jnp.bfloat16)
    lower = (value - upper.astype(jnp.float32)).astype(jnp.bfloat16)
    return upper, lower


def dot(left, right, dims):
    return lax.dot_general(left, right, (dims, ((), ())), preferred_element_type=jnp.float32)


def dot3(left, right, dims=((1,), (0,))):
    return (
        dot(left[0], right[0], dims)
        + dot(left[0], right[1], dims)
        + dot(left[1], right[0], dims)
    )


def signed(number, length):
    return jnp.where(number < length // 2, number, number - length)


def wave_y(start, shape, axis):
    number = lax.broadcasted_iota(jnp.int32, shape, axis) + start
    return 2.0 * math.pi / NY * signed(number, NY).astype(jnp.float32)


def wave_z(shape, axis):
    number = lax.broadcasted_iota(jnp.int32, shape, axis)
    return 2.0 * math.pi / NZ * signed(number, NZ).astype(jnp.float32)


def synth_z_kernel(
    plane, place_ref, adjoint_ref, velocity_ref, table_ref, out_ref, adj_ref, vel_ref, sent_ref, sems
):
    def load(k, which):
        source, target = ((adjoint_ref, adj_ref), (velocity_ref, vel_ref))[which]
        return pltpu.make_async_copy(source.at[:, :, k], target.at[:, :, k], sems.at[which, k])

    def store(k):
        return pltpu.make_async_copy(
            sent_ref.at[k], out_ref.at[:, pl.ds(k * SENT, SENT)], sems.at[2, k]
        )

    for k in range(ROWS_X):
        for which in range(2):
            load(k, which).start()
    ky = wave_y(place_ref[1] * ROWS_Y, (ROWS_Y, 1), 0)
    kz = wave_z((1, NZ), 1)
    half_sign = jnp.where(lax.broadcasted_iota(jnp.int32, (1, 128), 1) < 64, -1.0, 1.0)

    for k in range(ROWS_X):
        number_x = place_ref[0] * ROWS_X + k
        kx = 2.0 * math.pi / NX * number_x.astype(jnp.float32)
        for which in range(2):
            load(k, which).wait()
        vel = [[vel_ref[c, part, k] for part in range(2)] for c in range(3)]
        fields = [(adj_ref[c, 0, k], adj_ref[c, 1, k]) for c in range(3)]
        fields += [(vel[c][0], vel[c][1]) for c in range(3)]
        fields.append((kz * vel[1][1] - ky * vel[2][1], ky * vel[2][0] - kz * vel[1][0]))
        fields.append((kx * vel[2][1] - kz * vel[0][1], kz * vel[0][0] - kx * vel[2][0]))
        for pair in range(SENT // 2):
            rows = [part for field in fields[2 * pair : 2 * pair + 2] for part in field]
            value = jnp.concatenate(rows, 0)
            if plane == 0:
                merged = value[:, :128] + value[:, 128:]
            else:
                merged = value[:, :128] - value[:, 128:]
            upper, lower = split(merged)
            stacked = jnp.concatenate([upper, lower, upper], 1)
            both = dot(table_ref[...], stacked, ((1,), (1,)))
            for f in range(2):
                lanes = slice(128 * f, 128 * f + 128)
                turned = pltpu.roll(both[128:, lanes], 64, 1)
                sent_ref[k, :, 2 * pair + f, :] = both[:128, lanes] + half_sign * turned
        store(k).start()
    for k in range(ROWS_X):
        store(k).wait()


def synth_z(place, adjoint_hat, velocity_hat, plane):
    table = tables_synth_z()[plane]
    shape = (DEVICES, ROWS_X * SENT, 128)
    block = (3, 2, ROWS_X, ROWS_Y, NZ)
    return pl.pallas_call(
        functools.partial(synth_z_kernel, plane),
        in_specs=[
            pl.BlockSpec(memory_space=pltpu.SMEM),
            pl.BlockSpec(memory_space=pl.ANY),
            pl.BlockSpec(memory_space=pl.ANY),
            pl.BlockSpec(memory_space=pltpu.VMEM),
        ],
        out_specs=pl.BlockSpec(memory_space=pl.ANY),
        out_shape=jax.ShapeDtypeStruct(shape, jnp.float32),
        scratch_shapes=[
            pltpu.VMEM(block, jnp.float32),
            pltpu.VMEM(block, jnp.float32),
            pltpu.VMEM((ROWS_X, DEVICES, SENT, 128), jnp.float32),
            pltpu.SemaphoreType.DMA((3, ROWS_X)),
        ],
        compiler_params=pltpu.CompilerParams(vmem_limit_bytes=vmem_bytes),
        name="synth_z",
    )(place, adjoint_hat, velocity_hat, jnp.asarray(table))


def plane_kernel(plane, got_ref, sy_ref, sx_ref, ax_ref, ay_ref, *refs):
    if plane == 0:
        out_ref, rest_ref, spec_ref, cell_ref = refs
    else:
        rest_ref, out_ref, spec_ref, cell_ref = refs
    chunk = ROWS_X * SENT
    half_sign = jnp.where(lax.broadcasted_iota(jnp.int32, (1, 128), 1) < 64, -1.0, 1.0)
    ky_lanes = []
    for n in range(NARROW):
        number = lax.broadcasted_iota(jnp.int32, (1, 128), 1) % 64 + n * ROWS_Y
        ky_lanes.append(2.0 * math.pi / NY * signed(number, NY).astype(jnp.float32))
    kx_rows = 2.0 * math.pi / NX * lax.broadcasted_iota(jnp.int32, (KX, 1), 0).astype(jnp.float32)
    alternate = jnp.where(lax.broadcasted_iota(jnp.int32, (KX, 1), 0) % 2 == 0, 1.0, -1.0)
    weight = (
        jnp.where(lax.broadcasted_iota(jnp.int32, (KX, 1), 0) == 0, 1.0, 2.0) * norm_scale()
    )
    first_row = lax.broadcasted_iota(jnp.int32, (256, 1), 0) == 0

    def rows_of(field, n):
        return jnp.concatenate(
            [
                got_ref[pl.ds((w * NARROW + n) * chunk + field, ROWS_X, stride=SENT), :]
                for w in range(WIDE)
            ],
            0,
        )

    def synth(parts, index):
        spans = []
        for parity in range(2):
            if parity == 0:
                merged = [parts[0] + parts[2], parts[1] + parts[3]]
            else:
                merged = [parts[0] - parts[2], parts[1] - parts[3]]
            spans.append(
                dot3(
                    split(jnp.concatenate(merged, 1)), (sy_ref[parity, 0], sy_ref[parity, 1])
                )
            )
        real = jnp.concatenate([spans[0][:, :128], spans[1][:, :128]], 1)
        imag = jnp.concatenate([spans[0][:, 128:], spans[1][:, 128:]], 1)
        cosine = dot3((sx_ref[0, 0], sx_ref[0, 1]), split(real))
        sine = dot3((sx_ref[1, 0], sx_ref[1, 1]), split(imag))
        middle = jnp.sum(real * (alternate * weight), 0, keepdims=True)
        cell_ref[index, 0] = cosine + sine
        cell_ref[index, 1] = jnp.where(first_row, middle, cosine - sine)

    def each_field(field, carry):
        synth([rows_of(field, n) for n in range(NARROW)], field)
        return carry

    lax.fori_loop(0, SENT, each_field, 0)
    swirl = []
    for n in range(NARROW):
        across = kx_rows * rows_of(4, n) - ky_lanes[n] * rows_of(3, n)
        swirl.append(pltpu.roll(across, 64, 1) * half_sign)
    synth(swirl, SENT)

    def product(kind, c, mirror):
        one, two = (c + 1) % 3, (c + 2) % 3
        if kind == 0:
            return (
                cell_ref[one, mirror] * cell_ref[6 + two, mirror]
                - cell_ref[two, mirror] * cell_ref[6 + one, mirror]
            )
        return (
            cell_ref[3 + one, mirror] * cell_ref[two, mirror]
            - cell_ref[3 + two, mirror] * cell_ref[one, mirror]
        )

    def analyse(index, kind, c):
        ahead = product(kind, c, 0)
        behind = product(kind, c, 1)
        middle = behind[0:1]
        both = ahead + jnp.where(first_row, 0.0, behind)
        apart = ahead - behind
        real = dot3((ax_ref[0, 0], ax_ref[0, 1]), split(both))
        real = real + alternate[:KEPT_X] * norm_scale() * middle
        imag = dot3((ax_ref[1, 0], ax_ref[1, 1]), split(apart))
        spans = []
        for parity in range(2):
            lanes = slice(128 * parity, 128 * parity + 128)
            spans.append(
                dot3(
                    split(jnp.concatenate([real[:, lanes], imag[:, lanes]], 1)),
                    (ay_ref[parity, 0], ay_ref[parity, 1]),
                )
            )
        spec_ref[index, 0] = spans[0] + spans[1]
        spec_ref[index, 1] = spans[0] - spans[1]

    for kind in range(2):
        for c in range(3):
            analyse(3 * kind + c, kind, c)

    kx_kept = kx_rows[:KEPT_X]

    def times_i(value):
        return pltpu.roll(value, 64, 1) * half_sign

    out_ref[KEPT_W:] = jnp.zeros((WIDE - KEPT_W,) + out_ref.shape[1:], jnp.float32)
    if plane == 0:
        rest_ref[KEPT_W:] = jnp.zeros((WIDE - KEPT_W,) + rest_ref.shape[1:], jnp.float32)

    def put(n, tile, value):
        rows = slice(tile * ROWS_X, tile * ROWS_X + ROWS_X)
        out_ref[:KEPT_W, n, rows, :] = value.reshape(KEPT_W, ROWS_X, 128)

    def values_of(n):
        at = (n // 2, slice(None), slice(128 * (n % 2), 128 * (n % 2) + 128))
        item = [spec_ref[(index,) + at] for index in range(6)]
        ky = ky_lanes[n]
        return [
            item[0] + times_i(ky * item[5]),
            item[1] - times_i(kx_kept * item[5]),
            item[2] + times_i(kx_kept * item[4] - ky * item[3]),
            item[3],
            item[4],
        ]

    lane = lax.broadcasted_iota(jnp.int32, (1, 128), 1)
    for half in range(2):
        heavy, light = HEAVY[half], LIGHT[half]
        values = values_of(heavy)
        direct = 3 if plane == 0 else 4
        for f in range(BACK):
            if f < direct:
                put(heavy, f, values[f])
            else:
                put(light, f - direct if plane == 0 else 3, values[f])
        values = values_of(light)
        packed = []
        for tile in range(2):
            value = jnp.zeros((KEPT_X, 128), jnp.float32)
            for slot in range(5):
                f, part = divmod(5 * tile + slot, 2)
                moved = pltpu.roll(
                    values[f], (SLOT * slot - 64 * part - LIGHT_ROW[half]) % 128, 1
                )
                value = jnp.where((lane >= SLOT * slot) & (lane < SLOT * slot + SLOT), moved, value)
            packed.append(value)
        if plane == 0:
            put(light, 2, packed[0])
            rest_ref[:KEPT_W, half] = packed[1].reshape(KEPT_W, ROWS_X, 128)
        else:
            out_ref[:, light, 0:ROWS_X, :] = rest_ref[:, half]
            put(light, 1, packed[0])
            put(light, 2, packed[1])


def run_plane(plane, got, rest=None):
    tables = [tables_synth_y(), tables_synth_x(), tables_anal_x(), tables_anal_y()]
    tiles = 3 + plane
    out_shape = [jax.ShapeDtypeStruct((WIDE, NARROW, tiles * ROWS_X, 128), jnp.float32)]
    operands = [got.reshape(DEVICES * ROWS_X * SENT, 128)] + [jnp.asarray(t) for t in tables]
    if plane == 0:
        out_shape.append(jax.ShapeDtypeStruct((WIDE, 2, ROWS_X, 128), jnp.float32))
    else:
        operands.append(rest)
    outs = pl.pallas_call(
        functools.partial(plane_kernel, plane),
        out_shape=out_shape,
        in_specs=[pl.BlockSpec(memory_space=pltpu.VMEM)] * len(operands),
        out_specs=[pl.BlockSpec(memory_space=pltpu.VMEM)] * len(out_shape),
        scratch_shapes=[
            pltpu.VMEM((6, 2, KEPT_X, 256), jnp.float32),
            pltpu.VMEM((9, 2, 256, 256), jnp.float32),
        ],
        compiler_params=pltpu.CompilerParams(vmem_limit_bytes=vmem_bytes),
        name="plane",
    )(*operands)
    return [outs[0].reshape(DEVICES, tiles * ROWS_X, 128)] + list(outs[1:])


def span_of(rows, table):
    upper, lower = split(rows.T)
    return dot(jnp.concatenate([upper, lower, upper], 1), table, ((1,), (0,)))


def unite(span, real_rows, imag_rows):
    real, imag = span[real_rows], span[imag_rows]
    return real[:, :128] + imag[:, 128:], imag[:, :128] - real[:, 128:]


def mirror(first, second):
    return tuple(
        jnp.concatenate([one + two, one - two], 1) for one, two in zip(first, second)
    )


def light_narrow(narrow):
    return (narrow == LIGHT[0]) | (narrow == LIGHT[1])


def tile_copies(source_ref, first, count, target_ref, at, sems):
    return [
        pltpu.make_async_copy(
            source_ref.at[:, pl.ds((first + tile) * ROWS_X, ROWS_X)],
            target_ref.at[at + tile],
            sems.at[at + tile],
        )
        for tile in range(count)
    ]


def begin_kernel(
    place_ref, back_ref, more_ref, table_ref, part_ref, got_ref, new_ref, sems, whole_sems
):
    def store(k):
        return pltpu.make_async_copy(new_ref.at[:, :, k], part_ref.at[:, :, k], sems.at[k])

    @pl.when(jnp.logical_not(light_narrow(place_ref[1])))
    def _():
        pieces = tile_copies(back_ref, 0, 3, got_ref, 0, whole_sems)
        pieces += tile_copies(more_ref, 0, 2, got_ref, 3, whole_sems)
        for copy in pieces:
            copy.start()
        for copy in pieces:
            copy.wait()
        for k in range(ROWS_X):
            for f in range(BACK):
                span = span_of(got_ref[f, :, k, :], table_ref[0])
                real, imag = unite(span, slice(0, 64), slice(64, 128))
                new_ref[f, 0, k] = real
                new_ref[f, 1, k] = imag
            store(k).start()
        for k in range(ROWS_X):
            store(k).wait()


def begin(place, back, more):
    table = tables_anal_z()
    block = (BACK, 2, ROWS_X, ROWS_Y, 128)
    return pl.pallas_call(
        begin_kernel,
        in_specs=[
            pl.BlockSpec(memory_space=pltpu.SMEM),
            pl.BlockSpec(memory_space=pltpu.HBM),
            pl.BlockSpec(memory_space=pltpu.HBM),
            pl.BlockSpec(memory_space=pltpu.VMEM),
        ],
        out_specs=pl.BlockSpec(memory_space=pltpu.HBM),
        out_shape=jax.ShapeDtypeStruct(block, jnp.float32),
        scratch_shapes=[
            pltpu.VMEM((BACK, DEVICES, ROWS_X, 128), jnp.float32),
            pltpu.VMEM(block, jnp.float32),
            pltpu.SemaphoreType.DMA((ROWS_X,)),
            pltpu.SemaphoreType.DMA((BACK,)),
        ],
        compiler_params=pltpu.CompilerParams(vmem_limit_bytes=vmem_bytes),
        name="begin",
    )(place, back, more, jnp.asarray(table))


def finish_kernel(
    place_ref,
    back0_ref,
    back1_ref,
    more_ref,
    part_ref,
    adjoint_ref,
    table_ref,
    out_ref,
    got_ref,
    mid_ref,
    old_ref,
    new_ref,
    sems,
    whole_sems,
):
    narrow = place_ref[1]
    is_light = light_narrow(narrow)

    def load(k):
        return pltpu.make_async_copy(adjoint_ref.at[:, :, k], old_ref.at[:, :, k], sems.at[0, k])

    def fetch(k):
        return pltpu.make_async_copy(part_ref.at[:, :, k], mid_ref.at[:, :, k], sems.at[2, k])

    def store(k):
        return pltpu.make_async_copy(new_ref.at[:, :, k], out_ref.at[:, :, k], sems.at[1, k])

    number_z = signed(lax.broadcasted_iota(jnp.int32, (1, NZ), 1), NZ)
    kz = 2.0 * math.pi / NZ * number_z.astype(jnp.float32)

    def emit(k, got, start, rows):
        number_x = place_ref[0] * ROWS_X + k
        kx = 2.0 * math.pi / NX * number_x.astype(jnp.float32)
        number_y = lax.broadcasted_iota(jnp.int32, (rows, 1), 0) + start + narrow * ROWS_Y
        number_y = signed(number_y, NY)
        ky = 2.0 * math.pi / NY * number_y.astype(jnp.float32)
        conv = [
            (got[0][0] + kz * got[4][1], got[0][1] - kz * got[4][0]),
            (got[1][0] - kz * got[3][1], got[1][1] + kz * got[3][0]),
            got[2],
        ]
        keep = (
            (3 * number_x < NX) & (3 * jnp.abs(number_y) < NY) & (3 * jnp.abs(number_z) < NZ)
        ).astype(jnp.float32)
        ksquare = kx * kx + ky * ky + kz * kz
        inverse = 1.0 / (ksquare + (ksquare == 0).astype(jnp.float32))
        decay = jnp.exp(-viscous_rate * ksquare)
        waves = (kx, ky, kz)
        for part in range(2):
            along = (kx * conv[0][part] + ky * conv[1][part] + kz * conv[2][part]) * inverse
            for c in range(3):
                projected = keep * (conv[c][part] - waves[c] * along)
                old = old_ref[c, part, k, pl.ds(start, rows), :]
                new_ref[c, part, k, pl.ds(start, rows), :] = decay * (
                    old + section_step * projected
                )

    @pl.when(jnp.logical_not(is_light))
    def _():
        pieces = tile_copies(back1_ref, 0, 4, got_ref, 0, whole_sems)
        pieces += tile_copies(more_ref, 0, 1, got_ref, 4, whole_sems)
        for copy in pieces:
            copy.start()
        for k in range(ROWS_X):
            fetch(k).start()
            load(k).start()
        for copy in pieces:
            copy.wait()
        for k in range(ROWS_X):
            fetch(k).wait()
            got = []
            for f in range(BACK):
                span = span_of(got_ref[f, :, k, :], table_ref[1])
                second = unite(span, slice(0, 64), slice(64, 128))
                got.append(mirror((mid_ref[f, 0, k], mid_ref[f, 1, k]), second))
            load(k).wait()
            emit(k, got, 0, ROWS_Y)
            store(k).start()

    @pl.when(is_light)
    def _():
        pieces = tile_copies(back1_ref, 0, 3, got_ref, 0, whole_sems)
        pieces += tile_copies(back0_ref, 2, 1, got_ref, 3, whole_sems)
        for copy in pieces:
            copy.start()
        for k in range(ROWS_X):
            load(k).start()
        for copy in pieces:
            copy.wait()
        number_y = lax.broadcasted_iota(jnp.int32, (ROWS_Y, 1), 0) + narrow * ROWS_Y
        ky = 2.0 * math.pi / NY * signed(number_y, NY).astype(jnp.float32)
        for k in range(ROWS_X):
            spans = [
                [
                    span_of(got_ref[tile, :, k, :], table_ref[plane])
                    for plane, tile in enumerate(tiles)
                ]
                for tiles in ((3, 1), (0, 2))
            ]

            def item(index, plane):
                tile, slot = divmod(index, 5)
                return spans[tile][plane][SLOT * slot : SLOT * slot + SLOT]

            got = []
            for f in range(BACK):
                halves_of = [
                    unite(
                        jnp.concatenate([item(2 * f, plane), item(2 * f + 1, plane)], 0),
                        slice(0, SLOT),
                        slice(SLOT, 2 * SLOT),
                    )
                    for plane in range(2)
                ]
                got.append(mirror(*halves_of))
            number_x = place_ref[0] * ROWS_X + k
            kx = 2.0 * math.pi / NX * number_x.astype(jnp.float32)
            decay = jnp.exp(-viscous_rate * (kx * kx + ky * ky + kz * kz))
            load(k).wait()
            for c in range(3):
                for part in range(2):
                    new_ref[c, part, k] = decay * old_ref[c, part, k]
            start = pl.multiple_of(jnp.where(narrow == LIGHT[0], 0, LIGHT_ROW[1]), 8)
            emit(k, got, start, SLOT)
            store(k).start()

    for k in range(ROWS_X):
        store(k).wait()


def finish(place, arrays, adjoint_hat):
    table = tables_anal_z()
    block = (3, 2, ROWS_X, ROWS_Y, NZ)
    return pl.pallas_call(
        finish_kernel,
        in_specs=[pl.BlockSpec(memory_space=pltpu.SMEM)]
        + [pl.BlockSpec(memory_space=pltpu.HBM)] * 5
        + [pl.BlockSpec(memory_space=pltpu.VMEM)],
        out_specs=pl.BlockSpec(memory_space=pltpu.HBM),
        out_shape=jax.ShapeDtypeStruct(block, jnp.float32),
        scratch_shapes=[
            pltpu.VMEM((BACK, DEVICES, ROWS_X, 128), jnp.float32),
            pltpu.VMEM((BACK, 2, ROWS_X, ROWS_Y, 128), jnp.float32),
            pltpu.VMEM(block, jnp.float32),
            pltpu.VMEM(block, jnp.float32),
            pltpu.SemaphoreType.DMA((3, ROWS_X)),
            pltpu.SemaphoreType.DMA((BACK,)),
        ],
        compiler_params=pltpu.CompilerParams(vmem_limit_bytes=vmem_bytes),
        name="finish",
    )(place, *arrays, adjoint_hat, jnp.asarray(table))


def swap(chunks):
    return lax.all_to_all(chunks, ("wide", "narrow"), 0, 0, tiled=True)


def forward(tiles):
    return lax.ppermute(tiles, "narrow", [(LIGHT[0], HEAVY[0]), (LIGHT[1], HEAVY[1])])


def local(adjoint_hat, velocity_hat):
    place = jnp.stack([lax.axis_index("wide"), lax.axis_index("narrow")]).astype(jnp.int32)
    got = [swap(synth_z(place, adjoint_hat, velocity_hat, plane)) for plane in range(2)]
    out0, rest = run_plane(0, got[0])
    back0 = swap(out0)
    (out1,) = run_plane(1, got[1], rest)
    back1 = swap(out1)
    more0 = forward(back0[:, : 2 * ROWS_X])
    part = begin(place, back0, more0)
    back1, part = lax.optimization_barrier((back1, part))
    more1 = forward(back1[:, 3 * ROWS_X :])
    return finish(place, [back0, back1, more1, part], adjoint_hat)


def solution(mesh):
    in_specs = (P(None, None, "wide", "narrow", None), P(None, None, "wide", "narrow", None))
    out_specs = P(None, None, "wide", "narrow", None)
    return jax.shard_map(local, mesh=mesh, in_specs=in_specs, out_specs=out_specs, check_vma=False)
```

```python
import functools
import math

import jax
import jax.numpy as jnp
import ml_dtypes
import numpy as np
from jax import lax
from jax.experimental import pallas as pl
from jax.experimental.pallas import tpu as pltpu
from jax.sharding import PartitionSpec as P

NX = 512
NY = 256
NZ = 256
KX = 256
ROWS_X = 8
ROWS_Y = 64
WIDE = 32
NARROW = 4
DEVICES = WIDE * NARROW
SENT = 8
BACK = 5
KEPT_X = 176
KEPT_W = KEPT_X // ROWS_X
HEAVY = (0, 3)
LIGHT = (1, 2)
LIGHT_ROW = (0, 40)
SLOT = 24

section_step = 0.25
viscous_rate = 0.05
vmem_bytes = 60 * 1024 * 1024


def halves(table):
    upper = table.astype(ml_dtypes.bfloat16)
    lower = (table - upper.astype(np.float64)).astype(ml_dtypes.bfloat16)
    return np.stack([upper, lower])


def turn(modes, places, length):
    angle = 2.0 * np.pi / length * (np.outer(modes, places) % length)
    return np.cos(angle), np.sin(angle)


def tables_synth_z():
    quarter = np.arange(128)
    parts = []
    for plane in range(2):
        cosine, sine = turn(2 * np.arange(128) + plane, quarter, NZ)
        upper, lower = halves(np.concatenate([cosine, sine], 0))
        parts.append(np.concatenate([upper, upper, lower], 1))
    return np.stack(parts)


def tables_synth_y():
    mode = np.arange(128)
    parts = []
    for parity in range(2):
        cosine, sine = turn(mode, 2 * np.arange(128) + parity, NY)
        real_rows = np.concatenate([cosine, sine], 1)
        imag_rows = np.concatenate([-sine, cosine], 1)
        stacked = np.stack([real_rows.reshape(2, 64, 256), imag_rows.reshape(2, 64, 256)], 1)
        parts.append(halves(stacked.reshape(256, 256)))
    return np.stack(parts)


def norm_scale():
    return 1.0 / math.sqrt(NX * NY * NZ)


def tables_synth_x():
    weight = np.where(np.arange(KX) == 0, 1.0, 2.0) * norm_scale()
    cosine, sine = turn(np.arange(256), np.arange(KX), NX)
    return np.stack([halves(cosine * weight), halves(-sine * weight)])


def tables_anal_x():
    cosine, sine = turn(np.arange(KEPT_X), np.arange(256), NX)
    return np.stack([halves(cosine * norm_scale()), halves(-sine * norm_scale())])


def tables_anal_y():
    parts = []
    mode = np.arange(128)
    for parity in range(2):
        cosine, sine = turn(2 * np.arange(128) + parity, mode, NY)
        cosine = cosine.reshape(128, 2, 1, 64)
        sine = sine.reshape(128, 2, 1, 64)
        real_rows = np.concatenate([cosine, -sine], 2).reshape(128, 256)
        imag_rows = np.concatenate([sine, cosine], 2).reshape(128, 256)
        parts.append(halves(np.concatenate([real_rows, imag_rows], 0)))
    return np.stack(parts)


def tables_anal_z():
    parts = []
    for plane in range(2):
        cosine, sine = turn(2 * np.arange(128) + plane, np.arange(128), NZ)
        upper, lower = halves(np.concatenate([cosine, sine], 1))
        parts.append(np.concatenate([upper, upper, lower], 0))
    return np.stack(parts)


def split(value):
    upper = value.astype(jnp.bfloat16)
    lower = (value - upper.astype(jnp.float32)).astype(jnp.bfloat16)
    return upper, lower


def dot(left, right, dims):
    return lax.dot_general(left, right, (dims, ((), ())), preferred_element_type=jnp.float32)


def dot3(left, right, dims=((1,), (0,))):
    return (
        dot(left[0], right[0], dims)
        + dot(left[0], right[1], dims)
        + dot(left[1], right[0], dims)
    )


def signed(number, length):
    return jnp.where(number < length // 2, number, number - length)


def wave_y(start, shape, axis):
    number = lax.broadcasted_iota(jnp.int32, shape, axis) + start
    return 2.0 * math.pi / NY * signed(number, NY).astype(jnp.float32)


def wave_z(shape, axis):
    number = lax.broadcasted_iota(jnp.int32, shape, axis)
    return 2.0 * math.pi / NZ * signed(number, NZ).astype(jnp.float32)


def synth_z_kernel(
    plane, adjoint_ref, velocity_ref, table_ref, out_ref, adj_ref, vel_ref, sent_ref, sems
):
    def load(k, which):
        source, target = ((adjoint_ref, adj_ref), (velocity_ref, vel_ref))[which]
        return pltpu.make_async_copy(source.at[:, :, k], target.at[:, :, k], sems.at[which, k])

    def store(k):
        return pltpu.make_async_copy(
            sent_ref.at[k], out_ref.at[:, pl.ds(k * SENT, SENT)], sems.at[2, k]
        )

    for k in range(ROWS_X):
        for which in range(2):
            load(k, which).start()
    ky = wave_y(lax.axis_index("narrow") * ROWS_Y, (ROWS_Y, 1), 0)
    kz = wave_z((1, NZ), 1)
    half_sign = jnp.where(lax.broadcasted_iota(jnp.int32, (1, 128), 1) < 64, -1.0, 1.0)

    for k in range(ROWS_X):
        number_x = lax.axis_index("wide") * ROWS_X + k
        kx = 2.0 * math.pi / NX * number_x.astype(jnp.float32)
        for which in range(2):
            load(k, which).wait()
        vel = [[vel_ref[c, part, k] for part in range(2)] for c in range(3)]
        fields = [(adj_ref[c, 0, k], adj_ref[c, 1, k]) for c in range(3)]
        fields += [(vel[c][0], vel[c][1]) for c in range(3)]
        fields.append((kz * vel[1][1] - ky * vel[2][1], ky * vel[2][0] - kz * vel[1][0]))
        fields.append((kx * vel[2][1] - kz * vel[0][1], kz * vel[0][0] - kx * vel[2][0]))
        for pair in range(SENT // 2):
            rows = [part for field in fields[2 * pair : 2 * pair + 2] for part in field]
            value = jnp.concatenate(rows, 0)
            if plane == 0:
                merged = value[:, :128] + value[:, 128:]
            else:
                merged = value[:, :128] - value[:, 128:]
            upper, lower = split(merged)
            stacked = jnp.concatenate([upper, lower, upper], 1)
            both = dot(table_ref[...], stacked, ((1,), (1,)))
            for f in range(2):
                lanes = slice(128 * f, 128 * f + 128)
                turned = pltpu.roll(both[128:, lanes], 64, 1)
                sent_ref[k, :, 2 * pair + f, :] = both[:128, lanes] + half_sign * turned
        store(k).start()
    for k in range(ROWS_X):
        store(k).wait()


def synth_z(adjoint_hat, velocity_hat, plane):
    table = tables_synth_z()[plane]
    shape = (DEVICES, ROWS_X * SENT, 128)
    block = (3, 2, ROWS_X, ROWS_Y, NZ)
    return pl.pallas_call(
        functools.partial(synth_z_kernel, plane),
        in_specs=[
            pl.BlockSpec(memory_space=pl.ANY),
            pl.BlockSpec(memory_space=pl.ANY),
            pl.BlockSpec(memory_space=pltpu.VMEM),
        ],
        out_specs=pl.BlockSpec(memory_space=pl.ANY),
        out_shape=jax.ShapeDtypeStruct(shape, jnp.float32),
        scratch_shapes=[
            pltpu.VMEM(block, jnp.float32),
            pltpu.VMEM(block, jnp.float32),
            pltpu.VMEM((ROWS_X, DEVICES, SENT, 128), jnp.float32),
            pltpu.SemaphoreType.DMA((3, ROWS_X)),
        ],
        compiler_params=pltpu.CompilerParams(vmem_limit_bytes=vmem_bytes),
        name="synth_z",
    )(adjoint_hat, velocity_hat, jnp.asarray(table))


def plane_kernel(plane, got_ref, sy_ref, sx_ref, ax_ref, ay_ref, *refs):
    if plane == 0:
        out_ref, rest_ref, spec_ref, cell_ref = refs
    else:
        rest_ref, out_ref, spec_ref, cell_ref = refs
    chunk = ROWS_X * SENT
    half_sign = jnp.where(lax.broadcasted_iota(jnp.int32, (1, 128), 1) < 64, -1.0, 1.0)
    ky_lanes = []
    for n in range(NARROW):
        number = lax.broadcasted_iota(jnp.int32, (1, 128), 1) % 64 + n * ROWS_Y
        ky_lanes.append(2.0 * math.pi / NY * signed(number, NY).astype(jnp.float32))
    kx_rows = 2.0 * math.pi / NX * lax.broadcasted_iota(jnp.int32, (KX, 1), 0).astype(jnp.float32)
    alternate = jnp.where(lax.broadcasted_iota(jnp.int32, (KX, 1), 0) % 2 == 0, 1.0, -1.0)
    weight = (
        jnp.where(lax.broadcasted_iota(jnp.int32, (KX, 1), 0) == 0, 1.0, 2.0) * norm_scale()
    )
    first_row = lax.broadcasted_iota(jnp.int32, (256, 1), 0) == 0

    def rows_of(field, n):
        return jnp.concatenate(
            [
                got_ref[pl.ds((w * NARROW + n) * chunk + field, ROWS_X, stride=SENT), :]
                for w in range(WIDE)
            ],
            0,
        )

    def synth(parts, index):
        spans = []
        for parity in range(2):
            if parity == 0:
                merged = [parts[0] + parts[2], parts[1] + parts[3]]
            else:
                merged = [parts[0] - parts[2], parts[1] - parts[3]]
            spans.append(
                dot3(
                    split(jnp.concatenate(merged, 1)), (sy_ref[parity, 0], sy_ref[parity, 1])
                )
            )
        real = jnp.concatenate([spans[0][:, :128], spans[1][:, :128]], 1)
        imag = jnp.concatenate([spans[0][:, 128:], spans[1][:, 128:]], 1)
        cosine = dot3((sx_ref[0, 0], sx_ref[0, 1]), split(real))
        sine = dot3((sx_ref[1, 0], sx_ref[1, 1]), split(imag))
        middle = jnp.sum(real * (alternate * weight), 0, keepdims=True)
        cell_ref[index, 0] = cosine + sine
        cell_ref[index, 1] = jnp.where(first_row, middle, cosine - sine)

    def each_field(field, carry):
        synth([rows_of(field, n) for n in range(NARROW)], field)
        return carry

    lax.fori_loop(0, SENT, each_field, 0)
    swirl = []
    for n in range(NARROW):
        across = kx_rows * rows_of(4, n) - ky_lanes[n] * rows_of(3, n)
        swirl.append(pltpu.roll(across, 64, 1) * half_sign)
    synth(swirl, SENT)

    def product(kind, c, mirror):
        one, two = (c + 1) % 3, (c + 2) % 3
        if kind == 0:
            return (
                cell_ref[one, mirror] * cell_ref[6 + two, mirror]
                - cell_ref[two, mirror] * cell_ref[6 + one, mirror]
            )
        return (
            cell_ref[3 + one, mirror] * cell_ref[two, mirror]
            - cell_ref[3 + two, mirror] * cell_ref[one, mirror]
        )

    def analyse(index, kind, c):
        ahead = product(kind, c, 0)
        behind = product(kind, c, 1)
        middle = behind[0:1]
        both = ahead + jnp.where(first_row, 0.0, behind)
        apart = ahead - behind
        real = dot3((ax_ref[0, 0], ax_ref[0, 1]), split(both))
        real = real + alternate[:KEPT_X] * norm_scale() * middle
        imag = dot3((ax_ref[1, 0], ax_ref[1, 1]), split(apart))
        spans = []
        for parity in range(2):
            lanes = slice(128 * parity, 128 * parity + 128)
            spans.append(
                dot3(
                    split(jnp.concatenate([real[:, lanes], imag[:, lanes]], 1)),
                    (ay_ref[parity, 0], ay_ref[parity, 1]),
                )
            )
        spec_ref[index, 0] = spans[0] + spans[1]
        spec_ref[index, 1] = spans[0] - spans[1]

    for kind in range(2):
        for c in range(3):
            analyse(3 * kind + c, kind, c)

    kx_kept = kx_rows[:KEPT_X]

    def times_i(value):
        return pltpu.roll(value, 64, 1) * half_sign

    out_ref[KEPT_W:] = jnp.zeros((WIDE - KEPT_W,) + out_ref.shape[1:], jnp.float32)
    if plane == 0:
        rest_ref[KEPT_W:] = jnp.zeros((WIDE - KEPT_W,) + rest_ref.shape[1:], jnp.float32)

    def put(n, tile, value):
        rows = slice(tile * ROWS_X, tile * ROWS_X + ROWS_X)
        out_ref[:KEPT_W, n, rows, :] = value.reshape(KEPT_W, ROWS_X, 128)

    def values_of(n):
        at = (n // 2, slice(None), slice(128 * (n % 2), 128 * (n % 2) + 128))
        item = [spec_ref[(index,) + at] for index in range(6)]
        ky = ky_lanes[n]
        return [
            item[0] + times_i(ky * item[5]),
            item[1] - times_i(kx_kept * item[5]),
            item[2] + times_i(kx_kept * item[4] - ky * item[3]),
            item[3],
            item[4],
        ]

    lane = lax.broadcasted_iota(jnp.int32, (1, 128), 1)
    for half in range(2):
        heavy, light = HEAVY[half], LIGHT[half]
        values = values_of(heavy)
        direct = 3 if plane == 0 else 4
        for f in range(BACK):
            if f < direct:
                put(heavy, f, values[f])
            else:
                put(light, f - direct if plane == 0 else 3, values[f])
        values = values_of(light)
        packed = []
        for tile in range(2):
            value = jnp.zeros((KEPT_X, 128), jnp.float32)
            for slot in range(5):
                f, part = divmod(5 * tile + slot, 2)
                moved = pltpu.roll(
                    values[f], (SLOT * slot - 64 * part - LIGHT_ROW[half]) % 128, 1
                )
                value = jnp.where((lane >= SLOT * slot) & (lane < SLOT * slot + SLOT), moved, value)
            packed.append(value)
        if plane == 0:
            put(light, 2, packed[0])
            rest_ref[:KEPT_W, half] = packed[1].reshape(KEPT_W, ROWS_X, 128)
        else:
            out_ref[:, light, 0:ROWS_X, :] = rest_ref[:, half]
            put(light, 1, packed[0])
            put(light, 2, packed[1])


def run_plane(plane, got, rest=None):
    tables = [tables_synth_y(), tables_synth_x(), tables_anal_x(), tables_anal_y()]
    tiles = 3 + plane
    out_shape = [jax.ShapeDtypeStruct((WIDE, NARROW, tiles * ROWS_X, 128), jnp.float32)]
    operands = [got.reshape(DEVICES * ROWS_X * SENT, 128)] + [jnp.asarray(t) for t in tables]
    if plane == 0:
        out_shape.append(jax.ShapeDtypeStruct((WIDE, 2, ROWS_X, 128), jnp.float32))
    else:
        operands.append(rest)
    outs = pl.pallas_call(
        functools.partial(plane_kernel, plane),
        out_shape=out_shape,
        in_specs=[pl.BlockSpec(memory_space=pltpu.VMEM)] * len(operands),
        out_specs=[pl.BlockSpec(memory_space=pltpu.VMEM)] * len(out_shape),
        scratch_shapes=[
            pltpu.VMEM((6, 2, KEPT_X, 256), jnp.float32),
            pltpu.VMEM((9, 2, 256, 256), jnp.float32),
        ],
        compiler_params=pltpu.CompilerParams(vmem_limit_bytes=vmem_bytes),
        name="plane",
    )(*operands)
    return [outs[0].reshape(DEVICES, tiles * ROWS_X, 128)] + list(outs[1:])


def spans_of(tiles, table):
    upper, lower = split(jnp.concatenate([rows.T for rows in tiles], 0))
    span = dot(jnp.concatenate([upper, lower, upper], 1), table, ((1,), (0,)))
    return [span[128 * at : 128 * at + 128] for at in range(len(tiles))]


def unite(span, real_rows, imag_rows):
    real, imag = span[real_rows], span[imag_rows]
    return real[:, :128] + imag[:, 128:], imag[:, :128] - real[:, 128:]


def mirror(first, second):
    return tuple(
        jnp.concatenate([one + two, one - two], 1) for one, two in zip(first, second)
    )


def light_narrow(narrow):
    return (narrow == LIGHT[0]) | (narrow == LIGHT[1])


def tile_copies(source_ref, first, count, target_ref, at, sems):
    return [
        pltpu.make_async_copy(
            source_ref.at[:, pl.ds((first + tile) * ROWS_X, ROWS_X)],
            target_ref.at[at + tile],
            sems.at[at + tile],
        )
        for tile in range(count)
    ]


def begin_kernel(
    back_ref, more_ref, table_ref, part_ref, got_ref, new_ref, sems, whole_sems
):
    def store(k):
        return pltpu.make_async_copy(new_ref.at[:, :, k], part_ref.at[:, :, k], sems.at[k])

    @pl.when(jnp.logical_not(light_narrow(lax.axis_index("narrow"))))
    def _():
        pieces = tile_copies(back_ref, 0, 3, got_ref, 0, whole_sems)
        pieces += tile_copies(more_ref, 0, 2, got_ref, 3, whole_sems)
        for copy in pieces:
            copy.start()
        for copy in pieces:
            copy.wait()
        for k in range(ROWS_X):
            spans = spans_of([got_ref[f, :, k, :] for f in range(BACK)], table_ref[0])
            for f, span in enumerate(spans):
                real, imag = unite(span, slice(0, 64), slice(64, 128))
                new_ref[f, 0, k] = real
                new_ref[f, 1, k] = imag
            store(k).start()
        for k in range(ROWS_X):
            store(k).wait()


def begin(back, more):
    table = tables_anal_z()
    block = (BACK, 2, ROWS_X, ROWS_Y, 128)
    return pl.pallas_call(
        begin_kernel,
        in_specs=[
            pl.BlockSpec(memory_space=pltpu.HBM),
            pl.BlockSpec(memory_space=pltpu.HBM),
            pl.BlockSpec(memory_space=pltpu.VMEM),
        ],
        out_specs=pl.BlockSpec(memory_space=pltpu.HBM),
        out_shape=jax.ShapeDtypeStruct(block, jnp.float32),
        scratch_shapes=[
            pltpu.VMEM((BACK, DEVICES, ROWS_X, 128), jnp.float32),
            pltpu.VMEM(block, jnp.float32),
            pltpu.SemaphoreType.DMA((ROWS_X,)),
            pltpu.SemaphoreType.DMA((BACK,)),
        ],
        compiler_params=pltpu.CompilerParams(vmem_limit_bytes=vmem_bytes),
        name="begin",
    )(back, more, jnp.asarray(table))


def finish_kernel(
    back0_ref,
    back1_ref,
    more_ref,
    part_ref,
    adjoint_ref,
    table_ref,
    out_ref,
    got_ref,
    mid_ref,
    old_ref,
    new_ref,
    factor_ref,
    sems,
    whole_sems,
):
    wide, narrow = lax.axis_index("wide"), lax.axis_index("narrow")
    is_light = light_narrow(narrow)

    def load(k):
        return pltpu.make_async_copy(adjoint_ref.at[:, :, k], old_ref.at[:, :, k], sems.at[0, k])

    def fetch(k):
        return pltpu.make_async_copy(part_ref.at[:, :, k], mid_ref.at[:, :, k], sems.at[2, k])

    def store(k):
        return pltpu.make_async_copy(new_ref.at[:, :, k], out_ref.at[:, :, k], sems.at[1, k])

    number_z = signed(lax.broadcasted_iota(jnp.int32, (1, NZ), 1), NZ)
    kz = 2.0 * math.pi / NZ * number_z.astype(jnp.float32)

    number_y = signed(
        lax.broadcasted_iota(jnp.int32, (ROWS_Y, 1), 0) + narrow * ROWS_Y, NY
    )
    all_ky = 2.0 * math.pi / NY * number_y.astype(jnp.float32)

    def wave_x(k):
        number_x = wide * ROWS_X + k
        return number_x, 2.0 * math.pi / NX * number_x.astype(jnp.float32)

    def prepare():
        keep_yz = (3 * jnp.abs(number_y) < NY) & (3 * jnp.abs(number_z) < NZ)
        scale_yz = keep_yz.astype(jnp.float32) * section_step
        square_yz = all_ky * all_ky + kz * kz
        for k in range(ROWS_X):
            number_x, kx = wave_x(k)
            ksquare = kx * kx + square_yz
            decay = jnp.exp(-viscous_rate * ksquare)
            factor_ref[0, k] = 1.0 / (ksquare + (ksquare == 0).astype(jnp.float32))
            factor_ref[1, k] = decay
            factor_ref[2, k] = scale_yz * (3 * number_x < NX).astype(jnp.float32) * decay

    def emit(k, got, start, rows):
        at = pl.ds(start, rows)
        kx = wave_x(k)[1]
        row = lax.broadcasted_iota(jnp.int32, (rows, 1), 0) + start + narrow * ROWS_Y
        ky = 2.0 * math.pi / NY * signed(row, NY).astype(jnp.float32)
        conv = [
            (got[0][0] + kz * got[4][1], got[0][1] - kz * got[4][0]),
            (got[1][0] - kz * got[3][1], got[1][1] + kz * got[3][0]),
            got[2],
        ]
        inverse, decay, gain = [factor_ref[which, k, at, :] for which in range(3)]
        waves = (kx, ky, kz)
        for part in range(2):
            along = (kx * conv[0][part] + ky * conv[1][part] + kz * conv[2][part]) * inverse
            for c in range(3):
                new_ref[c, part, k, at, :] = decay * old_ref[c, part, k, at, :] + gain * (
                    conv[c][part] - waves[c] * along
                )

    @pl.when(jnp.logical_not(is_light))
    def _():
        pieces = tile_copies(back1_ref, 0, 4, got_ref, 0, whole_sems)
        pieces += tile_copies(more_ref, 0, 1, got_ref, 4, whole_sems)
        for copy in pieces:
            copy.start()
        for k in range(ROWS_X):
            fetch(k).start()
            load(k).start()
        prepare()
        for copy in pieces:
            copy.wait()
        for k in range(ROWS_X):
            fetch(k).wait()
            got = []
            spans = spans_of([got_ref[f, :, k, :] for f in range(BACK)], table_ref[1])
            for f, span in enumerate(spans):
                second = unite(span, slice(0, 64), slice(64, 128))
                got.append(mirror((mid_ref[f, 0, k], mid_ref[f, 1, k]), second))
            load(k).wait()
            emit(k, got, 0, ROWS_Y)
            store(k).start()

    @pl.when(is_light)
    def _():
        pieces = tile_copies(back1_ref, 0, 3, got_ref, 0, whole_sems)
        pieces += tile_copies(back0_ref, 2, 1, got_ref, 3, whole_sems)
        for copy in pieces:
            copy.start()
        for k in range(ROWS_X):
            load(k).start()
        prepare()
        for copy in pieces:
            copy.wait()
        for k in range(ROWS_X):
            by_plane = [
                spans_of([got_ref[tile, :, k, :] for tile in tiles], table_ref[plane])
                for plane, tiles in enumerate(((3, 0), (1, 2)))
            ]

            def item(index, plane):
                tile, slot = divmod(index, 5)
                return by_plane[plane][tile][SLOT * slot : SLOT * slot + SLOT]

            got = []
            for f in range(BACK):
                halves_of = [
                    unite(
                        jnp.concatenate([item(2 * f, plane), item(2 * f + 1, plane)], 0),
                        slice(0, SLOT),
                        slice(SLOT, 2 * SLOT),
                    )
                    for plane in range(2)
                ]
                got.append(mirror(*halves_of))
            load(k).wait()
            for c in range(3):
                for part in range(2):
                    new_ref[c, part, k] = factor_ref[1, k] * old_ref[c, part, k]
            start = pl.multiple_of(jnp.where(narrow == LIGHT[0], 0, LIGHT_ROW[1]), 8)
            emit(k, got, start, SLOT)
            store(k).start()

    for k in range(ROWS_X):
        store(k).wait()


def finish(arrays, adjoint_hat):
    table = tables_anal_z()
    block = (3, 2, ROWS_X, ROWS_Y, NZ)
    return pl.pallas_call(
        finish_kernel,
        in_specs=[pl.BlockSpec(memory_space=pltpu.HBM)] * 5
        + [pl.BlockSpec(memory_space=pltpu.VMEM)],
        out_specs=pl.BlockSpec(memory_space=pltpu.HBM),
        out_shape=jax.ShapeDtypeStruct(block, jnp.float32),
        scratch_shapes=[
            pltpu.VMEM((BACK, DEVICES, ROWS_X, 128), jnp.float32),
            pltpu.VMEM((BACK, 2, ROWS_X, ROWS_Y, 128), jnp.float32),
            pltpu.VMEM(block, jnp.float32),
            pltpu.VMEM(block, jnp.float32),
            pltpu.VMEM((3, ROWS_X, ROWS_Y, NZ), jnp.float32),
            pltpu.SemaphoreType.DMA((3, ROWS_X)),
            pltpu.SemaphoreType.DMA((BACK,)),
        ],
        compiler_params=pltpu.CompilerParams(vmem_limit_bytes=vmem_bytes),
        name="finish",
    )(*arrays, adjoint_hat, jnp.asarray(table))


def swap(chunks):
    return lax.all_to_all(chunks, ("wide", "narrow"), 0, 0, tiled=True)


def forward(tiles):
    return lax.ppermute(tiles, "narrow", [(LIGHT[0], HEAVY[0]), (LIGHT[1], HEAVY[1])])


def local(adjoint_hat, velocity_hat):
    got = [swap(synth_z(adjoint_hat, velocity_hat, plane)) for plane in range(2)]
    out0, rest = run_plane(0, got[0])
    back0 = swap(out0)
    (out1,) = run_plane(1, got[1], rest)
    back1 = swap(out1)
    more0 = forward(back0[:, : 2 * ROWS_X])
    part = begin(back0, more0)
    back1, part = lax.optimization_barrier((back1, part))
    more1 = forward(back1[:, 3 * ROWS_X :])
    return finish([back0, back1, more1, part], adjoint_hat)


def solution(mesh):
    in_specs = (P(None, None, "wide", "narrow", None), P(None, None, "wide", "narrow", None))
    out_specs = P(None, None, "wide", "narrow", None)
    return jax.shard_map(local, mesh=mesh, in_specs=in_specs, out_specs=out_specs, check_vma=False)
```

```python
import functools
import math

import jax
import jax.numpy as jnp
import ml_dtypes
import numpy as np
from jax import lax
from jax.experimental import pallas as pl
from jax.experimental.pallas import tpu as pltpu
from jax.sharding import PartitionSpec as P

NX = 512
NY = 256
NZ = 256
KX = 256
ROWS_X = 8
ROWS_Y = 64
WIDE = 32
NARROW = 4
DEVICES = WIDE * NARROW
SENT = 8
BACK = 5
KEPT_X = 176
KEPT_W = KEPT_X // ROWS_X
HEAVY = (0, 3)
LIGHT = (1, 2)
LIGHT_ROW = (0, 40)
SLOT = 24

section_step = 0.25
viscous_rate = 0.05
vmem_bytes = 60 * 1024 * 1024
finish_bytes = 24 * 1024 * 1024


def halves(table):
    upper = table.astype(ml_dtypes.bfloat16)
    lower = (table - upper.astype(np.float64)).astype(ml_dtypes.bfloat16)
    return np.stack([upper, lower])


def turn(modes, places, length):
    angle = 2.0 * np.pi / length * (np.outer(modes, places) % length)
    return np.cos(angle), np.sin(angle)


def tables_synth_z():
    quarter = np.arange(128)
    parts = []
    for plane in range(2):
        cosine, sine = turn(2 * np.arange(128) + plane, quarter, NZ)
        upper, lower = halves(np.concatenate([cosine, sine], 0))
        parts.append(np.concatenate([upper, upper, lower], 1))
    return np.stack(parts)


def tables_synth_y():
    mode = np.arange(128)
    parts = []
    for parity in range(2):
        cosine, sine = turn(mode, 2 * np.arange(128) + parity, NY)
        real_rows = np.concatenate([cosine, sine], 1)
        imag_rows = np.concatenate([-sine, cosine], 1)
        stacked = np.stack([real_rows.reshape(2, 64, 256), imag_rows.reshape(2, 64, 256)], 1)
        parts.append(halves(stacked.reshape(256, 256)))
    return np.stack(parts)


def norm_scale():
    return 1.0 / math.sqrt(NX * NY * NZ)


def tables_synth_x():
    weight = np.where(np.arange(KX) == 0, 1.0, 2.0) * norm_scale()
    cosine, sine = turn(np.arange(256), np.arange(KX), NX)
    return np.stack([halves(cosine * weight), halves(-sine * weight)])


def tables_anal_x():
    cosine, sine = turn(np.arange(KEPT_X), np.arange(256), NX)
    return np.stack([halves(cosine * norm_scale()), halves(-sine * norm_scale())])


def tables_anal_y():
    parts = []
    mode = np.arange(128)
    for parity in range(2):
        cosine, sine = turn(2 * np.arange(128) + parity, mode, NY)
        cosine = cosine.reshape(128, 2, 1, 64)
        sine = sine.reshape(128, 2, 1, 64)
        real_rows = np.concatenate([cosine, -sine], 2).reshape(128, 256)
        imag_rows = np.concatenate([sine, cosine], 2).reshape(128, 256)
        parts.append(halves(np.concatenate([real_rows, imag_rows], 0)))
    return np.stack(parts)


def tables_anal_z():
    parts = []
    for plane in range(2):
        cosine, sine = turn(2 * np.arange(128) + plane, np.arange(128), NZ)
        upper, lower = halves(np.concatenate([cosine, sine], 1))
        parts.append(np.concatenate([upper, upper, lower], 0))
    return np.stack(parts)


def split(value):
    upper = value.astype(jnp.bfloat16)
    lower = (value - upper.astype(jnp.float32)).astype(jnp.bfloat16)
    return upper, lower


def dot(left, right, dims):
    return lax.dot_general(left, right, (dims, ((), ())), preferred_element_type=jnp.float32)


def dot3(left, right, dims=((1,), (0,))):
    return (
        dot(left[0], right[0], dims)
        + dot(left[0], right[1], dims)
        + dot(left[1], right[0], dims)
    )


def signed(number, length):
    return jnp.where(number < length // 2, number, number - length)


def wave_y(start, shape, axis):
    number = lax.broadcasted_iota(jnp.int32, shape, axis) + start
    return 2.0 * math.pi / NY * signed(number, NY).astype(jnp.float32)


def wave_z(shape, axis):
    number = lax.broadcasted_iota(jnp.int32, shape, axis)
    return 2.0 * math.pi / NZ * signed(number, NZ).astype(jnp.float32)


def synth_z_kernel(
    plane, adjoint_ref, velocity_ref, table_ref, out_ref, adj_ref, vel_ref, sent_ref, sems
):
    def load(k, which):
        source, target = ((adjoint_ref, adj_ref), (velocity_ref, vel_ref))[which]
        return pltpu.make_async_copy(source.at[:, :, k], target.at[:, :, k], sems.at[which, k])

    def store(k):
        return pltpu.make_async_copy(
            sent_ref.at[k], out_ref.at[:, pl.ds(k * SENT, SENT)], sems.at[2, k]
        )

    for k in range(ROWS_X):
        for which in range(2):
            load(k, which).start()
    ky = wave_y(lax.axis_index("narrow") * ROWS_Y, (ROWS_Y, 1), 0)
    kz = wave_z((1, NZ), 1)
    half_sign = jnp.where(lax.broadcasted_iota(jnp.int32, (1, 128), 1) < 64, -1.0, 1.0)

    for k in range(ROWS_X):
        number_x = lax.axis_index("wide") * ROWS_X + k
        kx = 2.0 * math.pi / NX * number_x.astype(jnp.float32)
        for which in range(2):
            load(k, which).wait()
        vel = [[vel_ref[c, part, k] for part in range(2)] for c in range(3)]
        fields = [(adj_ref[c, 0, k], adj_ref[c, 1, k]) for c in range(3)]
        fields += [(vel[c][0], vel[c][1]) for c in range(3)]
        fields.append((kz * vel[1][1] - ky * vel[2][1], ky * vel[2][0] - kz * vel[1][0]))
        fields.append((kx * vel[2][1] - kz * vel[0][1], kz * vel[0][0] - kx * vel[2][0]))
        for pair in range(SENT // 2):
            rows = [part for field in fields[2 * pair : 2 * pair + 2] for part in field]
            value = jnp.concatenate(rows, 0)
            if plane == 0:
                merged = value[:, :128] + value[:, 128:]
            else:
                merged = value[:, :128] - value[:, 128:]
            upper, lower = split(merged)
            stacked = jnp.concatenate([upper, lower, upper], 1)
            both = dot(table_ref[...], stacked, ((1,), (1,)))
            for f in range(2):
                lanes = slice(128 * f, 128 * f + 128)
                turned = pltpu.roll(both[128:, lanes], 64, 1)
                sent_ref[k, :, 2 * pair + f, :] = both[:128, lanes] + half_sign * turned
        store(k).start()
    for k in range(ROWS_X):
        store(k).wait()


def synth_z(adjoint_hat, velocity_hat, plane):
    table = tables_synth_z()[plane]
    shape = (DEVICES, ROWS_X * SENT, 128)
    block = (3, 2, ROWS_X, ROWS_Y, NZ)
    return pl.pallas_call(
        functools.partial(synth_z_kernel, plane),
        in_specs=[
            pl.BlockSpec(memory_space=pl.ANY),
            pl.BlockSpec(memory_space=pl.ANY),
            pl.BlockSpec(memory_space=pltpu.VMEM),
        ],
        out_specs=pl.BlockSpec(memory_space=pl.ANY),
        out_shape=jax.ShapeDtypeStruct(shape, jnp.float32),
        scratch_shapes=[
            pltpu.VMEM(block, jnp.float32),
            pltpu.VMEM(block, jnp.float32),
            pltpu.VMEM((ROWS_X, DEVICES, SENT, 128), jnp.float32),
            pltpu.SemaphoreType.DMA((3, ROWS_X)),
        ],
        compiler_params=pltpu.CompilerParams(vmem_limit_bytes=vmem_bytes),
        name="synth_z",
    )(adjoint_hat, velocity_hat, jnp.asarray(table))


def plane_kernel(plane, got_ref, sy_ref, sx_ref, ax_ref, ay_ref, *refs):
    if plane == 0:
        out_ref, rest_ref, spec_ref, cell_ref = refs
    else:
        rest_ref, out_ref, spec_ref, cell_ref = refs
    chunk = ROWS_X * SENT
    half_sign = jnp.where(lax.broadcasted_iota(jnp.int32, (1, 128), 1) < 64, -1.0, 1.0)
    ky_lanes = []
    for n in range(NARROW):
        number = lax.broadcasted_iota(jnp.int32, (1, 128), 1) % 64 + n * ROWS_Y
        ky_lanes.append(2.0 * math.pi / NY * signed(number, NY).astype(jnp.float32))
    kx_rows = 2.0 * math.pi / NX * lax.broadcasted_iota(jnp.int32, (KX, 1), 0).astype(jnp.float32)
    alternate = jnp.where(lax.broadcasted_iota(jnp.int32, (KX, 1), 0) % 2 == 0, 1.0, -1.0)
    weight = (
        jnp.where(lax.broadcasted_iota(jnp.int32, (KX, 1), 0) == 0, 1.0, 2.0) * norm_scale()
    )
    first_row = lax.broadcasted_iota(jnp.int32, (256, 1), 0) == 0

    def rows_of(field, n):
        return jnp.concatenate(
            [
                got_ref[pl.ds((w * NARROW + n) * chunk + field, ROWS_X, stride=SENT), :]
                for w in range(WIDE)
            ],
            0,
        )

    def synth(parts, index):
        spans = []
        for parity in range(2):
            if parity == 0:
                merged = [parts[0] + parts[2], parts[1] + parts[3]]
            else:
                merged = [parts[0] - parts[2], parts[1] - parts[3]]
            spans.append(
                dot3(
                    split(jnp.concatenate(merged, 1)), (sy_ref[parity, 0], sy_ref[parity, 1])
                )
            )
        real = jnp.concatenate([spans[0][:, :128], spans[1][:, :128]], 1)
        imag = jnp.concatenate([spans[0][:, 128:], spans[1][:, 128:]], 1)
        cosine = dot3((sx_ref[0, 0], sx_ref[0, 1]), split(real))
        sine = dot3((sx_ref[1, 0], sx_ref[1, 1]), split(imag))
        middle = jnp.sum(real * (alternate * weight), 0, keepdims=True)
        cell_ref[index, 0] = cosine + sine
        cell_ref[index, 1] = jnp.where(first_row, middle, cosine - sine)

    def each_field(field, carry):
        synth([rows_of(field, n) for n in range(NARROW)], field)
        return carry

    lax.fori_loop(0, SENT, each_field, 0)
    swirl = []
    for n in range(NARROW):
        across = kx_rows * rows_of(4, n) - ky_lanes[n] * rows_of(3, n)
        swirl.append(pltpu.roll(across, 64, 1) * half_sign)
    synth(swirl, SENT)

    def product(kind, c, mirror):
        one, two = (c + 1) % 3, (c + 2) % 3
        if kind == 0:
            return (
                cell_ref[one, mirror] * cell_ref[6 + two, mirror]
                - cell_ref[two, mirror] * cell_ref[6 + one, mirror]
            )
        return (
            cell_ref[3 + one, mirror] * cell_ref[two, mirror]
            - cell_ref[3 + two, mirror] * cell_ref[one, mirror]
        )

    def analyse(index, kind, c):
        ahead = product(kind, c, 0)
        behind = product(kind, c, 1)
        middle = behind[0:1]
        both = ahead + jnp.where(first_row, 0.0, behind)
        apart = ahead - behind
        real = dot3((ax_ref[0, 0], ax_ref[0, 1]), split(both))
        real = real + alternate[:KEPT_X] * norm_scale() * middle
        imag = dot3((ax_ref[1, 0], ax_ref[1, 1]), split(apart))
        spans = []
        for parity in range(2):
            lanes = slice(128 * parity, 128 * parity + 128)
            spans.append(
                dot3(
                    split(jnp.concatenate([real[:, lanes], imag[:, lanes]], 1)),
                    (ay_ref[parity, 0], ay_ref[parity, 1]),
                )
            )
        spec_ref[index, 0] = spans[0] + spans[1]
        spec_ref[index, 1] = spans[0] - spans[1]

    for kind in range(2):
        for c in range(3):
            analyse(3 * kind + c, kind, c)

    kx_kept = kx_rows[:KEPT_X]

    def times_i(value):
        return pltpu.roll(value, 64, 1) * half_sign

    out_ref[KEPT_W:] = jnp.zeros((WIDE - KEPT_W,) + out_ref.shape[1:], jnp.float32)
    if plane == 0:
        rest_ref[KEPT_W:] = jnp.zeros((WIDE - KEPT_W,) + rest_ref.shape[1:], jnp.float32)

    def put(n, tile, value):
        rows = slice(tile * ROWS_X, tile * ROWS_X + ROWS_X)
        out_ref[:KEPT_W, n, rows, :] = value.reshape(KEPT_W, ROWS_X, 128)

    def values_of(n):
        at = (n // 2, slice(None), slice(128 * (n % 2), 128 * (n % 2) + 128))
        item = [spec_ref[(index,) + at] for index in range(6)]
        ky = ky_lanes[n]
        return [
            item[0] + times_i(ky * item[5]),
            item[1] - times_i(kx_kept * item[5]),
            item[2] + times_i(kx_kept * item[4] - ky * item[3]),
            item[3],
            item[4],
        ]

    lane = lax.broadcasted_iota(jnp.int32, (1, 128), 1)
    for half in range(2):
        heavy, light = HEAVY[half], LIGHT[half]
        values = values_of(heavy)
        direct = 3 if plane == 0 else 4
        for f in range(BACK):
            if f < direct:
                put(heavy, f, values[f])
            else:
                put(light, f - direct if plane == 0 else 3, values[f])
        values = values_of(light)
        packed = []
        for tile in range(2):
            value = jnp.zeros((KEPT_X, 128), jnp.float32)
            for slot in range(5):
                f, part = divmod(5 * tile + slot, 2)
                moved = pltpu.roll(
                    values[f], (SLOT * slot - 64 * part - LIGHT_ROW[half]) % 128, 1
                )
                value = jnp.where((lane >= SLOT * slot) & (lane < SLOT * slot + SLOT), moved, value)
            packed.append(value)
        if plane == 0:
            put(light, 2, packed[0])
            rest_ref[:KEPT_W, half] = packed[1].reshape(KEPT_W, ROWS_X, 128)
        else:
            out_ref[:, light, 0:ROWS_X, :] = rest_ref[:, half]
            put(light, 1, packed[0])
            put(light, 2, packed[1])


def run_plane(plane, got, rest=None):
    tables = [tables_synth_y(), tables_synth_x(), tables_anal_x(), tables_anal_y()]
    tiles = 3 + plane
    out_shape = [jax.ShapeDtypeStruct((WIDE, NARROW, tiles * ROWS_X, 128), jnp.float32)]
    operands = [got.reshape(DEVICES * ROWS_X * SENT, 128)] + [jnp.asarray(t) for t in tables]
    if plane == 0:
        out_shape.append(jax.ShapeDtypeStruct((WIDE, 2, ROWS_X, 128), jnp.float32))
    else:
        operands.append(rest)
    outs = pl.pallas_call(
        functools.partial(plane_kernel, plane),
        out_shape=out_shape,
        in_specs=[pl.BlockSpec(memory_space=pltpu.VMEM)] * len(operands),
        out_specs=[pl.BlockSpec(memory_space=pltpu.VMEM)] * len(out_shape),
        scratch_shapes=[
            pltpu.VMEM((6, 2, KEPT_X, 256), jnp.float32),
            pltpu.VMEM((9, 2, 256, 256), jnp.float32),
        ],
        compiler_params=pltpu.CompilerParams(vmem_limit_bytes=vmem_bytes),
        name="plane",
    )(*operands)
    return [outs[0].reshape(DEVICES, tiles * ROWS_X, 128)] + list(outs[1:])


def spans_of(tiles, table):
    upper, lower = split(jnp.concatenate([rows.T for rows in tiles], 0))
    span = dot(jnp.concatenate([upper, lower, upper], 1), table, ((1,), (0,)))
    return [span[128 * at : 128 * at + 128] for at in range(len(tiles))]


def unite(span, real_rows, imag_rows):
    real, imag = span[real_rows], span[imag_rows]
    return real[:, :128] + imag[:, 128:], imag[:, :128] - real[:, 128:]


def mirror(first, second):
    return tuple(
        jnp.concatenate([one + two, one - two], 1) for one, two in zip(first, second)
    )


def light_narrow(narrow):
    return (narrow == LIGHT[0]) | (narrow == LIGHT[1])


def tile_copies(source_ref, first, count, target_ref, at, sems):
    return [
        pltpu.make_async_copy(
            source_ref.at[:, pl.ds((first + tile) * ROWS_X, ROWS_X)],
            target_ref.at[at + tile],
            sems.at[at + tile],
        )
        for tile in range(count)
    ]


def begin_kernel(
    back_ref, more_ref, table_ref, part_ref, got_ref, new_ref, sems, whole_sems
):
    def store(k):
        return pltpu.make_async_copy(new_ref.at[:, :, k], part_ref.at[:, :, k], sems.at[k])

    @pl.when(jnp.logical_not(light_narrow(lax.axis_index("narrow"))))
    def _():
        pieces = tile_copies(back_ref, 0, 3, got_ref, 0, whole_sems)
        pieces += tile_copies(more_ref, 0, 2, got_ref, 3, whole_sems)
        for copy in pieces:
            copy.start()
        for copy in pieces:
            copy.wait()
        for k in range(ROWS_X):
            spans = spans_of([got_ref[f, :, k, :] for f in range(BACK)], table_ref[0])
            for f, span in enumerate(spans):
                real, imag = unite(span, slice(0, 64), slice(64, 128))
                new_ref[f, 0, k] = real
                new_ref[f, 1, k] = imag
            store(k).start()
        for k in range(ROWS_X):
            store(k).wait()


def begin(back, more):
    table = tables_anal_z()
    block = (BACK, 2, ROWS_X, ROWS_Y, 128)
    return pl.pallas_call(
        begin_kernel,
        in_specs=[
            pl.BlockSpec(memory_space=pltpu.HBM),
            pl.BlockSpec(memory_space=pltpu.HBM),
            pl.BlockSpec(memory_space=pltpu.VMEM),
        ],
        out_specs=pl.BlockSpec(memory_space=pltpu.HBM),
        out_shape=jax.ShapeDtypeStruct(block, jnp.float32),
        scratch_shapes=[
            pltpu.VMEM((BACK, DEVICES, ROWS_X, 128), jnp.float32),
            pltpu.VMEM(block, jnp.float32),
            pltpu.SemaphoreType.DMA((ROWS_X,)),
            pltpu.SemaphoreType.DMA((BACK,)),
        ],
        compiler_params=pltpu.CompilerParams(vmem_limit_bytes=finish_bytes),
        name="begin",
    )(back, more, jnp.asarray(table))


def in_vmem(array):
    return pltpu.with_memory_space_constraint(array, pltpu.VMEM)


def finish_kernel(
    back0_ref,
    back1_ref,
    more_ref,
    part_ref,
    adjoint_ref,
    table_ref,
    out_ref,
    new_ref,
    factor_ref,
    sems,
):
    wide, narrow = lax.axis_index("wide"), lax.axis_index("narrow")
    is_light = light_narrow(narrow)

    def store(k):
        return pltpu.make_async_copy(new_ref.at[:, :, k], out_ref.at[:, :, k], sems.at[k])

    number_z = signed(lax.broadcasted_iota(jnp.int32, (1, NZ), 1), NZ)
    kz = 2.0 * math.pi / NZ * number_z.astype(jnp.float32)

    number_y = signed(
        lax.broadcasted_iota(jnp.int32, (ROWS_Y, 1), 0) + narrow * ROWS_Y, NY
    )
    all_ky = 2.0 * math.pi / NY * number_y.astype(jnp.float32)

    def wave_x(k):
        number_x = wide * ROWS_X + k
        return number_x, 2.0 * math.pi / NX * number_x.astype(jnp.float32)

    def prepare():
        keep_yz = (3 * jnp.abs(number_y) < NY) & (3 * jnp.abs(number_z) < NZ)
        scale_yz = keep_yz.astype(jnp.float32) * section_step
        square_yz = all_ky * all_ky + kz * kz
        for k in range(ROWS_X):
            number_x, kx = wave_x(k)
            ksquare = kx * kx + square_yz
            decay = jnp.exp(-viscous_rate * ksquare)
            factor_ref[0, k] = 1.0 / (ksquare + (ksquare == 0).astype(jnp.float32))
            factor_ref[1, k] = decay
            factor_ref[2, k] = scale_yz * (3 * number_x < NX).astype(jnp.float32) * decay

    def emit(k, got, start, rows):
        at = pl.ds(start, rows)
        kx = wave_x(k)[1]
        row = lax.broadcasted_iota(jnp.int32, (rows, 1), 0) + start + narrow * ROWS_Y
        ky = 2.0 * math.pi / NY * signed(row, NY).astype(jnp.float32)
        conv = [
            (got[0][0] + kz * got[4][1], got[0][1] - kz * got[4][0]),
            (got[1][0] - kz * got[3][1], got[1][1] + kz * got[3][0]),
            got[2],
        ]
        inverse, decay, gain = [factor_ref[which, k, at, :] for which in range(3)]
        waves = (kx, ky, kz)
        for part in range(2):
            along = (kx * conv[0][part] + ky * conv[1][part] + kz * conv[2][part]) * inverse
            for c in range(3):
                new_ref[c, part, k, at, :] = decay * adjoint_ref[c, part, k, at, :] + gain * (
                    conv[c][part] - waves[c] * along
                )

    @pl.when(jnp.logical_not(is_light))
    def _():
        prepare()
        for k in range(ROWS_X):
            got = []
            spans = spans_of(
                [back1_ref[:, f * ROWS_X + k, :] for f in range(4)] + [more_ref[:, k, :]],
                table_ref[1],
            )
            for f, span in enumerate(spans):
                second = unite(span, slice(0, 64), slice(64, 128))
                got.append(mirror((part_ref[f, 0, k], part_ref[f, 1, k]), second))
            emit(k, got, 0, ROWS_Y)
            store(k).start()

    @pl.when(is_light)
    def _():
        prepare()
        for k in range(ROWS_X):
            by_plane = [
                spans_of([ref[:, tile * ROWS_X + k, :] for ref, tile in tiles], table_ref[plane])
                for plane, tiles in enumerate(
                    (((back0_ref, 2), (back1_ref, 0)), ((back1_ref, 1), (back1_ref, 2)))
                )
            ]

            def item(index, plane):
                tile, slot = divmod(index, 5)
                return by_plane[plane][tile][SLOT * slot : SLOT * slot + SLOT]

            got = []
            for f in range(BACK):
                halves_of = [
                    unite(
                        jnp.concatenate([item(2 * f, plane), item(2 * f + 1, plane)], 0),
                        slice(0, SLOT),
                        slice(SLOT, 2 * SLOT),
                    )
                    for plane in range(2)
                ]
                got.append(mirror(*halves_of))
            for c in range(3):
                for part in range(2):
                    new_ref[c, part, k] = factor_ref[1, k] * adjoint_ref[c, part, k]
            start = pl.multiple_of(jnp.where(narrow == LIGHT[0], 0, LIGHT_ROW[1]), 8)
            emit(k, got, start, SLOT)
            store(k).start()

    for k in range(ROWS_X):
        store(k).wait()


def finish(arrays, adjoint_hat):
    table = tables_anal_z()
    block = (3, 2, ROWS_X, ROWS_Y, NZ)
    return pl.pallas_call(
        finish_kernel,
        in_specs=[pl.BlockSpec(memory_space=pltpu.VMEM)] * 6,
        out_specs=pl.BlockSpec(memory_space=pltpu.HBM),
        out_shape=jax.ShapeDtypeStruct(block, jnp.float32),
        scratch_shapes=[
            pltpu.VMEM(block, jnp.float32),
            pltpu.VMEM((3, ROWS_X, ROWS_Y, NZ), jnp.float32),
            pltpu.SemaphoreType.DMA((ROWS_X,)),
        ],
        compiler_params=pltpu.CompilerParams(vmem_limit_bytes=finish_bytes),
        name="finish",
    )(*[in_vmem(array) for array in (*arrays, adjoint_hat)], jnp.asarray(table))


def swap(chunks):
    return lax.all_to_all(chunks, ("wide", "narrow"), 0, 0, tiled=True)


def forward(tiles):
    return lax.ppermute(tiles, "narrow", [(LIGHT[0], HEAVY[0]), (LIGHT[1], HEAVY[1])])


def local(adjoint_hat, velocity_hat):
    got = [swap(synth_z(adjoint_hat, velocity_hat, plane)) for plane in range(2)]
    out0, rest = run_plane(0, got[0])
    back0 = swap(out0)
    (out1,) = run_plane(1, got[1], rest)
    back1 = swap(out1)
    more0 = forward(back0[:, : 2 * ROWS_X])
    part = begin(back0, more0)
    back1, part = lax.optimization_barrier((back1, part))
    more1 = forward(back1[:, 3 * ROWS_X :])
    return finish([back0, back1, more1, part], adjoint_hat)


def solution(mesh):
    in_specs = (P(None, None, "wide", "narrow", None), P(None, None, "wide", "narrow", None))
    out_specs = P(None, None, "wide", "narrow", None)
    return jax.shard_map(local, mesh=mesh, in_specs=in_specs, out_specs=out_specs, check_vma=False)
```

```python
import functools
import math

import jax
import jax.numpy as jnp
import ml_dtypes
import numpy as np
from jax import lax
from jax.experimental import pallas as pl
from jax.experimental.pallas import tpu as pltpu
from jax.sharding import PartitionSpec as P

NX = 512
NY = 256
NZ = 256
KX = 256
ROWS_X = 8
ROWS_Y = 64
WIDE = 32
NARROW = 4
DEVICES = WIDE * NARROW
SENT = 8
BACK = 5
KEPT_X = 176
KEPT_W = KEPT_X // ROWS_X
HEAVY = (0, 3)
LIGHT = (1, 2)
LIGHT_ROW = (0, 40)
SLOT = 24

section_step = 0.25
viscous_rate = 0.05
vmem_bytes = 60 * 1024 * 1024
finish_bytes = 24 * 1024 * 1024


def halves(table):
    upper = table.astype(ml_dtypes.bfloat16)
    lower = (table - upper.astype(np.float64)).astype(ml_dtypes.bfloat16)
    return np.stack([upper, lower])


def turn(modes, places, length):
    angle = 2.0 * np.pi / length * (np.outer(modes, places) % length)
    return np.cos(angle), np.sin(angle)


def tables_synth_z():
    quarter = np.arange(128)
    parts = []
    for plane in range(2):
        cosine, sine = turn(2 * np.arange(128) + plane, quarter, NZ)
        upper, lower = halves(np.concatenate([cosine, sine], 0))
        parts.append(np.concatenate([upper, upper, lower], 1))
    return np.stack(parts)


def tables_synth_y():
    mode = np.arange(128)
    parts = []
    for parity in range(2):
        cosine, sine = turn(mode, 2 * np.arange(128) + parity, NY)
        real_rows = np.concatenate([cosine, sine], 1)
        imag_rows = np.concatenate([-sine, cosine], 1)
        stacked = np.stack([real_rows.reshape(2, 64, 256), imag_rows.reshape(2, 64, 256)], 1)
        parts.append(halves(stacked.reshape(256, 256)))
    return np.stack(parts)


def norm_scale():
    return 1.0 / math.sqrt(NX * NY * NZ)


def tables_synth_x():
    weight = np.where(np.arange(KX) == 0, 1.0, 2.0) * norm_scale()
    cosine, sine = turn(np.arange(256), np.arange(KX), NX)
    return np.stack([halves(cosine * weight), halves(-sine * weight)])


def tables_anal_x():
    cosine, sine = turn(np.arange(KEPT_X), np.arange(256), NX)
    return np.stack([halves(cosine * norm_scale()), halves(-sine * norm_scale())])


def tables_anal_y():
    parts = []
    mode = np.arange(128)
    for parity in range(2):
        cosine, sine = turn(2 * np.arange(128) + parity, mode, NY)
        cosine = cosine.reshape(128, 2, 1, 64)
        sine = sine.reshape(128, 2, 1, 64)
        real_rows = np.concatenate([cosine, -sine], 2).reshape(128, 256)
        imag_rows = np.concatenate([sine, cosine], 2).reshape(128, 256)
        parts.append(halves(np.concatenate([real_rows, imag_rows], 0)))
    return np.stack(parts)


def tables_anal_z():
    parts = []
    for plane in range(2):
        cosine, sine = turn(2 * np.arange(128) + plane, np.arange(128), NZ)
        upper, lower = halves(np.concatenate([cosine, sine], 1))
        parts.append(np.concatenate([upper, upper, lower], 0))
    return np.stack(parts)


def split(value):
    upper = value.astype(jnp.bfloat16)
    lower = (value - upper.astype(jnp.float32)).astype(jnp.bfloat16)
    return upper, lower


def dot(left, right, dims):
    return lax.dot_general(left, right, (dims, ((), ())), preferred_element_type=jnp.float32)


def dot3(left, right, dims=((1,), (0,))):
    return (
        dot(left[0], right[0], dims)
        + dot(left[0], right[1], dims)
        + dot(left[1], right[0], dims)
    )


def signed(number, length):
    return jnp.where(number < length // 2, number, number - length)


def wave_y(start, shape, axis):
    number = lax.broadcasted_iota(jnp.int32, shape, axis) + start
    return 2.0 * math.pi / NY * signed(number, NY).astype(jnp.float32)


def wave_z(shape, axis):
    number = lax.broadcasted_iota(jnp.int32, shape, axis)
    return 2.0 * math.pi / NZ * signed(number, NZ).astype(jnp.float32)


def synth_z_kernel(
    plane, adjoint_ref, velocity_ref, table_ref, out_ref, adj_ref, vel_ref, sent_ref, sems
):
    def load(k, which):
        source, target = ((adjoint_ref, adj_ref), (velocity_ref, vel_ref))[which]
        return pltpu.make_async_copy(source.at[:, :, k], target.at[:, :, k], sems.at[which, k])

    def store(k):
        return pltpu.make_async_copy(
            sent_ref.at[k], out_ref.at[:, pl.ds(k * SENT, SENT)], sems.at[2, k]
        )

    for k in range(ROWS_X):
        for which in range(2):
            load(k, which).start()
    ky = wave_y(lax.axis_index("narrow") * ROWS_Y, (ROWS_Y, 1), 0)
    kz = wave_z((1, NZ), 1)
    half_sign = jnp.where(lax.broadcasted_iota(jnp.int32, (1, 128), 1) < 64, -1.0, 1.0)

    for k in range(ROWS_X):
        number_x = lax.axis_index("wide") * ROWS_X + k
        kx = 2.0 * math.pi / NX * number_x.astype(jnp.float32)
        if k % 4 == 0:
            for near in range(k, k + 4):
                for which in range(2):
                    load(near, which).wait()
        vel = [[vel_ref[c, part, k] for part in range(2)] for c in range(3)]
        fields = [(adj_ref[c, 0, k], adj_ref[c, 1, k]) for c in range(3)]
        fields += [(vel[c][0], vel[c][1]) for c in range(3)]
        fields.append((kz * vel[1][1] - ky * vel[2][1], ky * vel[2][0] - kz * vel[1][0]))
        fields.append((kx * vel[2][1] - kz * vel[0][1], kz * vel[0][0] - kx * vel[2][0]))
        for pair in range(SENT // 2):
            rows = [part for field in fields[2 * pair : 2 * pair + 2] for part in field]
            value = jnp.concatenate(rows, 0)
            if plane == 0:
                merged = value[:, :128] + value[:, 128:]
            else:
                merged = value[:, :128] - value[:, 128:]
            upper, lower = split(merged)
            stacked = jnp.concatenate([upper, lower, upper], 1)
            both = dot(table_ref[...], stacked, ((1,), (1,)))
            for f in range(2):
                lanes = slice(128 * f, 128 * f + 128)
                turned = pltpu.roll(both[128:, lanes], 64, 1)
                sent_ref[k, :, 2 * pair + f, :] = both[:128, lanes] + half_sign * turned
        store(k).start()
    for k in range(ROWS_X):
        store(k).wait()


def synth_z(adjoint_hat, velocity_hat, plane):
    table = tables_synth_z()[plane]
    shape = (DEVICES, ROWS_X * SENT, 128)
    block = (3, 2, ROWS_X, ROWS_Y, NZ)
    return pl.pallas_call(
        functools.partial(synth_z_kernel, plane),
        in_specs=[
            pl.BlockSpec(memory_space=pl.ANY),
            pl.BlockSpec(memory_space=pl.ANY),
            pl.BlockSpec(memory_space=pltpu.VMEM),
        ],
        out_specs=pl.BlockSpec(memory_space=pl.ANY),
        out_shape=jax.ShapeDtypeStruct(shape, jnp.float32),
        scratch_shapes=[
            pltpu.VMEM(block, jnp.float32),
            pltpu.VMEM(block, jnp.float32),
            pltpu.VMEM((ROWS_X, DEVICES, SENT, 128), jnp.float32),
            pltpu.SemaphoreType.DMA((3, ROWS_X)),
        ],
        compiler_params=pltpu.CompilerParams(vmem_limit_bytes=vmem_bytes),
        name="synth_z",
    )(adjoint_hat, velocity_hat, jnp.asarray(table))


def plane_kernel(plane, got_ref, sy_ref, sx_ref, ax_ref, ay_ref, *refs):
    if plane == 0:
        out_ref, rest_ref, spec_ref, cell_ref = refs
    else:
        rest_ref, out_ref, spec_ref, cell_ref = refs
    chunk = ROWS_X * SENT
    half_sign = jnp.where(lax.broadcasted_iota(jnp.int32, (1, 128), 1) < 64, -1.0, 1.0)
    ky_lanes = []
    for n in range(NARROW):
        number = lax.broadcasted_iota(jnp.int32, (1, 128), 1) % 64 + n * ROWS_Y
        ky_lanes.append(2.0 * math.pi / NY * signed(number, NY).astype(jnp.float32))
    kx_rows = 2.0 * math.pi / NX * lax.broadcasted_iota(jnp.int32, (KX, 1), 0).astype(jnp.float32)
    alternate = jnp.where(lax.broadcasted_iota(jnp.int32, (KX, 1), 0) % 2 == 0, 1.0, -1.0)
    weight = (
        jnp.where(lax.broadcasted_iota(jnp.int32, (KX, 1), 0) == 0, 1.0, 2.0) * norm_scale()
    )
    first_row = lax.broadcasted_iota(jnp.int32, (256, 1), 0) == 0

    def rows_of(field, n):
        return jnp.concatenate(
            [
                got_ref[pl.ds((w * NARROW + n) * chunk + field, ROWS_X, stride=SENT), :]
                for w in range(WIDE)
            ],
            0,
        )

    def synth(parts, index):
        spans = []
        for parity in range(2):
            if parity == 0:
                merged = [parts[0] + parts[2], parts[1] + parts[3]]
            else:
                merged = [parts[0] - parts[2], parts[1] - parts[3]]
            spans.append(
                dot3(
                    split(jnp.concatenate(merged, 1)), (sy_ref[parity, 0], sy_ref[parity, 1])
                )
            )
        real = jnp.concatenate([spans[0][:, :128], spans[1][:, :128]], 1)
        imag = jnp.concatenate([spans[0][:, 128:], spans[1][:, 128:]], 1)
        cosine = dot3((sx_ref[0, 0], sx_ref[0, 1]), split(real))
        sine = dot3((sx_ref[1, 0], sx_ref[1, 1]), split(imag))
        middle = jnp.sum(real * (alternate * weight), 0, keepdims=True)
        cell_ref[index, 0] = cosine + sine
        cell_ref[index, 1] = jnp.where(first_row, middle, cosine - sine)

    def each_field(field, carry):
        synth([rows_of(field, n) for n in range(NARROW)], field)
        return carry

    lax.fori_loop(0, SENT, each_field, 0)
    swirl = []
    for n in range(NARROW):
        across = kx_rows * rows_of(4, n) - ky_lanes[n] * rows_of(3, n)
        swirl.append(pltpu.roll(across, 64, 1) * half_sign)
    synth(swirl, SENT)

    def product(kind, c, mirror):
        one, two = (c + 1) % 3, (c + 2) % 3
        if kind == 0:
            return (
                cell_ref[one, mirror] * cell_ref[6 + two, mirror]
                - cell_ref[two, mirror] * cell_ref[6 + one, mirror]
            )
        return (
            cell_ref[3 + one, mirror] * cell_ref[two, mirror]
            - cell_ref[3 + two, mirror] * cell_ref[one, mirror]
        )

    def analyse(index, kind, c):
        ahead = product(kind, c, 0)
        behind = product(kind, c, 1)
        middle = behind[0:1]
        both = ahead + jnp.where(first_row, 0.0, behind)
        apart = ahead - behind
        real = dot3((ax_ref[0, 0], ax_ref[0, 1]), split(both))
        real = real + alternate[:KEPT_X] * norm_scale() * middle
        imag = dot3((ax_ref[1, 0], ax_ref[1, 1]), split(apart))
        spans = []
        for parity in range(2):
            lanes = slice(128 * parity, 128 * parity + 128)
            spans.append(
                dot3(
                    split(jnp.concatenate([real[:, lanes], imag[:, lanes]], 1)),
                    (ay_ref[parity, 0], ay_ref[parity, 1]),
                )
            )
        spec_ref[index, 0] = spans[0] + spans[1]
        spec_ref[index, 1] = spans[0] - spans[1]

    for kind in range(2):
        for c in range(3):
            analyse(3 * kind + c, kind, c)

    kx_kept = kx_rows[:KEPT_X]

    def times_i(value):
        return pltpu.roll(value, 64, 1) * half_sign

    out_ref[KEPT_W:] = jnp.zeros((WIDE - KEPT_W,) + out_ref.shape[1:], jnp.float32)
    if plane == 0:
        rest_ref[KEPT_W:] = jnp.zeros((WIDE - KEPT_W,) + rest_ref.shape[1:], jnp.float32)

    def put(n, tile, value):
        rows = slice(tile * ROWS_X, tile * ROWS_X + ROWS_X)
        out_ref[:KEPT_W, n, rows, :] = value.reshape(KEPT_W, ROWS_X, 128)

    def values_of(n):
        at = (n // 2, slice(None), slice(128 * (n % 2), 128 * (n % 2) + 128))
        item = [spec_ref[(index,) + at] for index in range(6)]
        ky = ky_lanes[n]
        return [
            item[0] + times_i(ky * item[5]),
            item[1] - times_i(kx_kept * item[5]),
            item[2] + times_i(kx_kept * item[4] - ky * item[3]),
            item[3],
            item[4],
        ]

    lane = lax.broadcasted_iota(jnp.int32, (1, 128), 1)
    for half in range(2):
        heavy, light = HEAVY[half], LIGHT[half]
        values = values_of(heavy)
        direct = 3 if plane == 0 else 4
        for f in range(BACK):
            if f < direct:
                put(heavy, f, values[f])
            else:
                put(light, f - direct if plane == 0 else 3, values[f])
        values = values_of(light)
        packed = []
        for tile in range(2):
            value = jnp.zeros((KEPT_X, 128), jnp.float32)
            for slot in range(5):
                f, part = divmod(5 * tile + slot, 2)
                moved = pltpu.roll(
                    values[f], (SLOT * slot - 64 * part - LIGHT_ROW[half]) % 128, 1
                )
                value = jnp.where((lane >= SLOT * slot) & (lane < SLOT * slot + SLOT), moved, value)
            packed.append(value)
        if plane == 0:
            put(light, 2, packed[0])
            rest_ref[:KEPT_W, half] = packed[1].reshape(KEPT_W, ROWS_X, 128)
        else:
            out_ref[:, light, 0:ROWS_X, :] = rest_ref[:, half]
            put(light, 1, packed[0])
            put(light, 2, packed[1])


def run_plane(plane, got, rest=None):
    tables = [tables_synth_y(), tables_synth_x(), tables_anal_x(), tables_anal_y()]
    tiles = 3 + plane
    out_shape = [jax.ShapeDtypeStruct((WIDE, NARROW, tiles * ROWS_X, 128), jnp.float32)]
    operands = [got.reshape(DEVICES * ROWS_X * SENT, 128)] + [jnp.asarray(t) for t in tables]
    if plane == 0:
        out_shape.append(jax.ShapeDtypeStruct((WIDE, 2, ROWS_X, 128), jnp.float32))
    else:
        operands.append(rest)
    outs = pl.pallas_call(
        functools.partial(plane_kernel, plane),
        out_shape=out_shape,
        in_specs=[pl.BlockSpec(memory_space=pltpu.VMEM)] * len(operands),
        out_specs=[pl.BlockSpec(memory_space=pltpu.VMEM)] * len(out_shape),
        scratch_shapes=[
            pltpu.VMEM((6, 2, KEPT_X, 256), jnp.float32),
            pltpu.VMEM((9, 2, 256, 256), jnp.float32),
        ],
        compiler_params=pltpu.CompilerParams(vmem_limit_bytes=vmem_bytes),
        name="plane",
    )(*operands)
    return [outs[0].reshape(DEVICES, tiles * ROWS_X, 128)] + list(outs[1:])


def spans_of(tiles, table):
    upper, lower = split(jnp.concatenate([rows.T for rows in tiles], 0))
    span = dot(jnp.concatenate([upper, lower, upper], 1), table, ((1,), (0,)))
    return [span[128 * at : 128 * at + 128] for at in range(len(tiles))]


def unite(span, real_rows, imag_rows):
    real, imag = span[real_rows], span[imag_rows]
    return real[:, :128] + imag[:, 128:], imag[:, :128] - real[:, 128:]


def mirror(first, second):
    return tuple(
        jnp.concatenate([one + two, one - two], 1) for one, two in zip(first, second)
    )


def light_narrow(narrow):
    return (narrow == LIGHT[0]) | (narrow == LIGHT[1])


def tile_copies(source_ref, first, count, target_ref, at, sems):
    return [
        pltpu.make_async_copy(
            source_ref.at[:, pl.ds((first + tile) * ROWS_X, ROWS_X)],
            target_ref.at[at + tile],
            sems.at[at + tile],
        )
        for tile in range(count)
    ]


def begin_kernel(
    back_ref, more_ref, table_ref, part_ref, got_ref, new_ref, sems, whole_sems
):
    def store(k):
        return pltpu.make_async_copy(new_ref.at[:, :, k], part_ref.at[:, :, k], sems.at[k])

    @pl.when(jnp.logical_not(light_narrow(lax.axis_index("narrow"))))
    def _():
        pieces = tile_copies(back_ref, 0, 3, got_ref, 0, whole_sems)
        pieces += tile_copies(more_ref, 0, 2, got_ref, 3, whole_sems)
        for copy in pieces:
            copy.start()
        for copy in pieces:
            copy.wait()
        for k in range(ROWS_X):
            spans = spans_of([got_ref[f, :, k, :] for f in range(BACK)], table_ref[0])
            for f, span in enumerate(spans):
                real, imag = unite(span, slice(0, 64), slice(64, 128))
                new_ref[f, 0, k] = real
                new_ref[f, 1, k] = imag
            store(k).start()
        for k in range(ROWS_X):
            store(k).wait()


def begin(back, more):
    table = tables_anal_z()
    block = (BACK, 2, ROWS_X, ROWS_Y, 128)
    return pl.pallas_call(
        begin_kernel,
        in_specs=[
            pl.BlockSpec(memory_space=pltpu.HBM),
            pl.BlockSpec(memory_space=pltpu.HBM),
            pl.BlockSpec(memory_space=pltpu.VMEM),
        ],
        out_specs=pl.BlockSpec(memory_space=pltpu.HBM),
        out_shape=jax.ShapeDtypeStruct(block, jnp.float32),
        scratch_shapes=[
            pltpu.VMEM((BACK, DEVICES, ROWS_X, 128), jnp.float32),
            pltpu.VMEM(block, jnp.float32),
            pltpu.SemaphoreType.DMA((ROWS_X,)),
            pltpu.SemaphoreType.DMA((BACK,)),
        ],
        compiler_params=pltpu.CompilerParams(vmem_limit_bytes=finish_bytes),
        name="begin",
    )(back, more, jnp.asarray(table))


def in_hbm(array):
    return pltpu.with_memory_space_constraint(array, pltpu.HBM)


def in_vmem(array):
    return pltpu.with_memory_space_constraint(array, pltpu.VMEM)


def finish_kernel(
    back0_ref,
    back1_ref,
    more_ref,
    part_ref,
    adjoint_ref,
    table_ref,
    out_ref,
    new_ref,
    factor_ref,
    mid_ref,
    tile_ref,
    sems,
    mid_sems,
):
    wide, narrow = lax.axis_index("wide"), lax.axis_index("narrow")
    is_light = light_narrow(narrow)

    def fetch(k):
        return pltpu.make_async_copy(part_ref.at[:, :, k], mid_ref.at[:, :, k], mid_sems.at[k])

    tile_copy = pltpu.make_async_copy(
        back0_ref.at[:, pl.ds(2 * ROWS_X, ROWS_X)], tile_ref, mid_sems.at[0]
    )

    def store(k):
        return pltpu.make_async_copy(new_ref.at[:, :, k], out_ref.at[:, :, k], sems.at[k])

    number_z = signed(lax.broadcasted_iota(jnp.int32, (1, NZ), 1), NZ)
    kz = 2.0 * math.pi / NZ * number_z.astype(jnp.float32)

    number_y = signed(
        lax.broadcasted_iota(jnp.int32, (ROWS_Y, 1), 0) + narrow * ROWS_Y, NY
    )
    all_ky = 2.0 * math.pi / NY * number_y.astype(jnp.float32)

    def wave_x(k):
        number_x = wide * ROWS_X + k
        return number_x, 2.0 * math.pi / NX * number_x.astype(jnp.float32)

    def prepare():
        keep_yz = (3 * jnp.abs(number_y) < NY) & (3 * jnp.abs(number_z) < NZ)
        scale_yz = keep_yz.astype(jnp.float32) * section_step
        square_yz = all_ky * all_ky + kz * kz
        for k in range(ROWS_X):
            number_x, kx = wave_x(k)
            ksquare = kx * kx + square_yz
            decay = jnp.exp(-viscous_rate * ksquare)
            factor_ref[0, k] = 1.0 / (ksquare + (ksquare == 0).astype(jnp.float32))
            factor_ref[1, k] = decay
            factor_ref[2, k] = scale_yz * (3 * number_x < NX).astype(jnp.float32) * decay

    def emit(k, got, start, rows):
        at = pl.ds(start, rows)
        kx = wave_x(k)[1]
        row = lax.broadcasted_iota(jnp.int32, (rows, 1), 0) + start + narrow * ROWS_Y
        ky = 2.0 * math.pi / NY * signed(row, NY).astype(jnp.float32)
        conv = [
            (got[0][0] + kz * got[4][1], got[0][1] - kz * got[4][0]),
            (got[1][0] - kz * got[3][1], got[1][1] + kz * got[3][0]),
            got[2],
        ]
        inverse, decay, gain = [factor_ref[which, k, at, :] for which in range(3)]
        waves = (kx, ky, kz)
        for part in range(2):
            along = (kx * conv[0][part] + ky * conv[1][part] + kz * conv[2][part]) * inverse
            for c in range(3):
                new_ref[c, part, k, at, :] = decay * adjoint_ref[c, part, k, at, :] + gain * (
                    conv[c][part] - waves[c] * along
                )

    @pl.when(jnp.logical_not(is_light))
    def _():
        for k in range(ROWS_X):
            fetch(k).start()
        prepare()
        for k in range(ROWS_X):
            got = []
            spans = spans_of(
                [back1_ref[:, f * ROWS_X + k, :] for f in range(4)] + [more_ref[:, k, :]],
                table_ref[1],
            )
            fetch(k).wait()
            for f, span in enumerate(spans):
                second = unite(span, slice(0, 64), slice(64, 128))
                got.append(mirror((mid_ref[f, 0, k], mid_ref[f, 1, k]), second))
            emit(k, got, 0, ROWS_Y)
            store(k).start()

    @pl.when(is_light)
    def _():
        tile_copy.start()
        prepare()
        tile_copy.wait()
        for k in range(ROWS_X):
            by_plane = [
                spans_of([ref[:, tile * ROWS_X + k, :] for ref, tile in tiles], table_ref[plane])
                for plane, tiles in enumerate(
                    (((tile_ref, 0), (back1_ref, 0)), ((back1_ref, 1), (back1_ref, 2)))
                )
            ]

            def item(index, plane):
                tile, slot = divmod(index, 5)
                return by_plane[plane][tile][SLOT * slot : SLOT * slot + SLOT]

            got = []
            for f in range(BACK):
                halves_of = [
                    unite(
                        jnp.concatenate([item(2 * f, plane), item(2 * f + 1, plane)], 0),
                        slice(0, SLOT),
                        slice(SLOT, 2 * SLOT),
                    )
                    for plane in range(2)
                ]
                got.append(mirror(*halves_of))
            for c in range(3):
                for part in range(2):
                    new_ref[c, part, k] = factor_ref[1, k] * adjoint_ref[c, part, k]
            start = pl.multiple_of(jnp.where(narrow == LIGHT[0], 0, LIGHT_ROW[1]), 8)
            emit(k, got, start, SLOT)
            store(k).start()

    for k in range(ROWS_X):
        store(k).wait()


def finish(back0, back1, more, part, adjoint_hat):
    table = tables_anal_z()
    block = (3, 2, ROWS_X, ROWS_Y, NZ)
    return pl.pallas_call(
        finish_kernel,
        in_specs=[
            pl.BlockSpec(memory_space=pltpu.HBM),
            pl.BlockSpec(memory_space=pltpu.VMEM),
            pl.BlockSpec(memory_space=pltpu.VMEM),
            pl.BlockSpec(memory_space=pltpu.HBM),
            pl.BlockSpec(memory_space=pltpu.VMEM),
            pl.BlockSpec(memory_space=pltpu.VMEM),
        ],
        out_specs=pl.BlockSpec(memory_space=pltpu.HBM),
        out_shape=jax.ShapeDtypeStruct(block, jnp.float32),
        scratch_shapes=[
            pltpu.VMEM(block, jnp.float32),
            pltpu.VMEM((3, ROWS_X, ROWS_Y, NZ), jnp.float32),
            pltpu.VMEM((BACK, 2, ROWS_X, ROWS_Y, 128), jnp.float32),
            pltpu.VMEM((DEVICES, ROWS_X, 128), jnp.float32),
            pltpu.SemaphoreType.DMA((ROWS_X,)),
            pltpu.SemaphoreType.DMA((ROWS_X,)),
        ],
        compiler_params=pltpu.CompilerParams(vmem_limit_bytes=finish_bytes),
        name="finish",
    )(
        in_hbm(back0),
        in_vmem(back1),
        in_vmem(more),
        in_hbm(part),
        in_vmem(adjoint_hat),
        jnp.asarray(table),
    )


def swap(chunks):
    return lax.all_to_all(chunks, ("wide", "narrow"), 0, 0, tiled=True)


def forward(tiles):
    return lax.ppermute(tiles, "narrow", [(LIGHT[0], HEAVY[0]), (LIGHT[1], HEAVY[1])])


def local(adjoint_hat, velocity_hat):
    got = [swap(synth_z(adjoint_hat, velocity_hat, plane)) for plane in range(2)]
    out0, rest = run_plane(0, got[0])
    back0 = swap(out0)
    (out1,) = run_plane(1, got[1], rest)
    back1 = swap(out1)
    more0 = forward(back0[:, : 2 * ROWS_X])
    part = begin(back0, more0)
    back1, part = lax.optimization_barrier((back1, part))
    more1 = forward(back1[:, 3 * ROWS_X :])
    return finish(back0, back1, more1, part, adjoint_hat)


def solution(mesh):
    in_specs = (P(None, None, "wide", "narrow", None), P(None, None, "wide", "narrow", None))
    out_specs = P(None, None, "wide", "narrow", None)
    return jax.shard_map(local, mesh=mesh, in_specs=in_specs, out_specs=out_specs, check_vma=False)
```

```python
import functools
import math

import jax
import jax.numpy as jnp
import ml_dtypes
import numpy as np
from jax import lax
from jax.experimental import pallas as pl
from jax.experimental.pallas import tpu as pltpu
from jax.sharding import PartitionSpec as P

NX = 512
NY = 256
NZ = 256
KX = 256
ROWS_X = 8
ROWS_Y = 64
WIDE = 32
NARROW = 4
DEVICES = WIDE * NARROW
SENT = 8
BACK = 5
KEPT_X = 176
KEPT_W = KEPT_X // ROWS_X
HEAVY = (0, 3)
LIGHT = (1, 2)
LIGHT_ROW = (0, 40)
SLOT = 24

section_step = 0.25
viscous_rate = 0.05
vmem_bytes = 60 * 1024 * 1024
finish_bytes = 24 * 1024 * 1024


def halves(table):
    upper = table.astype(ml_dtypes.bfloat16)
    lower = (table - upper.astype(np.float64)).astype(ml_dtypes.bfloat16)
    return np.stack([upper, lower])


def turn(modes, places, length):
    angle = 2.0 * np.pi / length * (np.outer(modes, places) % length)
    return np.cos(angle), np.sin(angle)


def tables_synth_z():
    quarter = np.arange(128)
    parts = []
    for plane in range(2):
        cosine, sine = turn(2 * np.arange(128) + plane, quarter, NZ)
        upper, lower = halves(np.concatenate([cosine, sine], 0))
        parts.append(np.concatenate([upper, upper, lower], 1))
    return np.stack(parts)


def tables_synth_y():
    mode = np.arange(128)
    parts = []
    for parity in range(2):
        cosine, sine = turn(mode, 2 * np.arange(128) + parity, NY)
        real_rows = np.concatenate([cosine, sine], 1)
        imag_rows = np.concatenate([-sine, cosine], 1)
        stacked = np.stack([real_rows.reshape(2, 64, 256), imag_rows.reshape(2, 64, 256)], 1)
        parts.append(halves(stacked.reshape(256, 256)))
    return np.stack(parts)


def norm_scale():
    return 1.0 / math.sqrt(NX * NY * NZ)


def tables_synth_x():
    weight = np.where(np.arange(KX) == 0, 1.0, 2.0) * norm_scale()
    cosine, sine = turn(np.arange(256), np.arange(KX), NX)
    return np.stack([halves(cosine * weight), halves(-sine * weight)])


def tables_anal_x():
    cosine, sine = turn(np.arange(KEPT_X), np.arange(256), NX)
    return np.stack([halves(cosine * norm_scale()), halves(-sine * norm_scale())])


def tables_anal_y():
    parts = []
    mode = np.arange(128)
    for parity in range(2):
        cosine, sine = turn(2 * np.arange(128) + parity, mode, NY)
        cosine = cosine.reshape(128, 2, 1, 64)
        sine = sine.reshape(128, 2, 1, 64)
        real_rows = np.concatenate([cosine, -sine], 2).reshape(128, 256)
        imag_rows = np.concatenate([sine, cosine], 2).reshape(128, 256)
        parts.append(halves(np.concatenate([real_rows, imag_rows], 0)))
    return np.stack(parts)


def tables_anal_z():
    parts = []
    for plane in range(2):
        cosine, sine = turn(2 * np.arange(128) + plane, np.arange(128), NZ)
        upper, lower = halves(np.concatenate([cosine, sine], 1))
        parts.append(np.concatenate([upper, upper, lower], 0))
    return np.stack(parts)


def split(value):
    upper = value.astype(jnp.bfloat16)
    lower = (value - upper.astype(jnp.float32)).astype(jnp.bfloat16)
    return upper, lower


def dot(left, right, dims):
    return lax.dot_general(left, right, (dims, ((), ())), preferred_element_type=jnp.float32)


def dot3(left, right, dims=((1,), (0,))):
    return (
        dot(left[0], right[0], dims)
        + dot(left[0], right[1], dims)
        + dot(left[1], right[0], dims)
    )


def signed(number, length):
    return jnp.where(number < length // 2, number, number - length)


def wave_y(start, shape, axis):
    number = lax.broadcasted_iota(jnp.int32, shape, axis) + start
    return 2.0 * math.pi / NY * signed(number, NY).astype(jnp.float32)


def wave_z(shape, axis):
    number = lax.broadcasted_iota(jnp.int32, shape, axis)
    return 2.0 * math.pi / NZ * signed(number, NZ).astype(jnp.float32)


def synth_z_kernel(
    plane, adjoint_ref, velocity_ref, table_ref, out_ref, adj_ref, vel_ref, sent_ref, sems
):
    def load(k, which):
        source, target = ((adjoint_ref, adj_ref), (velocity_ref, vel_ref))[which]
        return pltpu.make_async_copy(source.at[:, :, k], target.at[:, :, k], sems.at[which, k])

    def store(k):
        return pltpu.make_async_copy(
            sent_ref.at[k], out_ref.at[:, pl.ds(k * SENT, SENT)], sems.at[2, k]
        )

    for k in range(ROWS_X):
        for which in range(2):
            load(k, which).start()
    ky = wave_y(lax.axis_index("narrow") * ROWS_Y, (ROWS_Y, 1), 0)
    kz = wave_z((1, NZ), 1)
    half_sign = jnp.where(lax.broadcasted_iota(jnp.int32, (1, 128), 1) < 64, -1.0, 1.0)

    for k in range(ROWS_X):
        number_x = lax.axis_index("wide") * ROWS_X + k
        kx = 2.0 * math.pi / NX * number_x.astype(jnp.float32)
        if k % 4 == 0:
            for near in range(k, k + 4):
                for which in range(2):
                    load(near, which).wait()
        vel = [[vel_ref[c, part, k] for part in range(2)] for c in range(3)]
        fields = [(adj_ref[c, 0, k], adj_ref[c, 1, k]) for c in range(3)]
        fields += [(vel[c][0], vel[c][1]) for c in range(3)]
        fields.append((kz * vel[1][1] - ky * vel[2][1], ky * vel[2][0] - kz * vel[1][0]))
        fields.append((kx * vel[2][1] - kz * vel[0][1], kz * vel[0][0] - kx * vel[2][0]))
        for pair in range(SENT // 2):
            rows = [part for field in fields[2 * pair : 2 * pair + 2] for part in field]
            value = jnp.concatenate(rows, 0)
            if plane == 0:
                merged = value[:, :128] + value[:, 128:]
            else:
                merged = value[:, :128] - value[:, 128:]
            upper, lower = split(merged)
            stacked = jnp.concatenate([upper, lower, upper], 1)
            both = dot(table_ref[...], stacked, ((1,), (1,)))
            for f in range(2):
                lanes = slice(128 * f, 128 * f + 128)
                turned = pltpu.roll(both[128:, lanes], 64, 1)
                sent_ref[k, :, 2 * pair + f, :] = both[:128, lanes] + half_sign * turned
        store(k).start()
    for k in range(ROWS_X):
        store(k).wait()


def synth_z(adjoint_hat, velocity_hat, plane):
    table = tables_synth_z()[plane]
    shape = (DEVICES, ROWS_X * SENT, 128)
    block = (3, 2, ROWS_X, ROWS_Y, NZ)
    return pl.pallas_call(
        functools.partial(synth_z_kernel, plane),
        in_specs=[
            pl.BlockSpec(memory_space=pl.ANY),
            pl.BlockSpec(memory_space=pl.ANY),
            pl.BlockSpec(memory_space=pltpu.VMEM),
        ],
        out_specs=pl.BlockSpec(memory_space=pl.ANY),
        out_shape=jax.ShapeDtypeStruct(shape, jnp.float32),
        scratch_shapes=[
            pltpu.VMEM(block, jnp.float32),
            pltpu.VMEM(block, jnp.float32),
            pltpu.VMEM((ROWS_X, DEVICES, SENT, 128), jnp.float32),
            pltpu.SemaphoreType.DMA((3, ROWS_X)),
        ],
        compiler_params=pltpu.CompilerParams(vmem_limit_bytes=vmem_bytes),
        name="synth_z",
    )(adjoint_hat, velocity_hat, jnp.asarray(table))


def plane_kernel(plane, got_ref, sy_ref, sx_ref, ax_ref, ay_ref, *refs):
    if plane == 0:
        out_ref, rest_ref, spec_ref, cell_ref = refs
    else:
        rest_ref, out_ref, spec_ref, cell_ref = refs
    chunk = ROWS_X * SENT
    half_sign = jnp.where(lax.broadcasted_iota(jnp.int32, (1, 128), 1) < 64, -1.0, 1.0)
    ky_lanes = []
    for n in range(NARROW):
        number = lax.broadcasted_iota(jnp.int32, (1, 128), 1) % 64 + n * ROWS_Y
        ky_lanes.append(2.0 * math.pi / NY * signed(number, NY).astype(jnp.float32))
    kx_rows = 2.0 * math.pi / NX * lax.broadcasted_iota(jnp.int32, (KX, 1), 0).astype(jnp.float32)
    alternate = jnp.where(lax.broadcasted_iota(jnp.int32, (KX, 1), 0) % 2 == 0, 1.0, -1.0)
    weight = (
        jnp.where(lax.broadcasted_iota(jnp.int32, (KX, 1), 0) == 0, 1.0, 2.0) * norm_scale()
    )
    first_row = lax.broadcasted_iota(jnp.int32, (256, 1), 0) == 0

    def rows_of(field, n):
        return jnp.concatenate(
            [
                got_ref[pl.ds((w * NARROW + n) * chunk + field, ROWS_X, stride=SENT), :]
                for w in range(WIDE)
            ],
            0,
        )

    def synth(parts, index):
        spans = []
        for parity in range(2):
            if parity == 0:
                merged = [parts[0] + parts[2], parts[1] + parts[3]]
            else:
                merged = [parts[0] - parts[2], parts[1] - parts[3]]
            spans.append(
                dot3(
                    split(jnp.concatenate(merged, 1)), (sy_ref[parity, 0], sy_ref[parity, 1])
                )
            )
        real = jnp.concatenate([spans[0][:, :128], spans[1][:, :128]], 1)
        imag = jnp.concatenate([spans[0][:, 128:], spans[1][:, 128:]], 1)
        cosine = dot3((sx_ref[0, 0], sx_ref[0, 1]), split(real))
        sine = dot3((sx_ref[1, 0], sx_ref[1, 1]), split(imag))
        middle = jnp.sum(real * (alternate * weight), 0, keepdims=True)
        cell_ref[index, 0] = cosine + sine
        cell_ref[index, 1] = jnp.where(first_row, middle, cosine - sine)

    def each_field(field, carry):
        synth([rows_of(field, n) for n in range(NARROW)], field)
        return carry

    lax.fori_loop(0, SENT, each_field, 0)
    swirl = []
    for n in range(NARROW):
        across = kx_rows * rows_of(4, n) - ky_lanes[n] * rows_of(3, n)
        swirl.append(pltpu.roll(across, 64, 1) * half_sign)
    synth(swirl, SENT)

    def product(kind, c, mirror):
        one, two = (c + 1) % 3, (c + 2) % 3
        if kind == 0:
            return (
                cell_ref[one, mirror] * cell_ref[6 + two, mirror]
                - cell_ref[two, mirror] * cell_ref[6 + one, mirror]
            )
        return (
            cell_ref[3 + one, mirror] * cell_ref[two, mirror]
            - cell_ref[3 + two, mirror] * cell_ref[one, mirror]
        )

    def analyse(index, kind, c):
        ahead = product(kind, c, 0)
        behind = product(kind, c, 1)
        middle = behind[0:1]
        both = ahead + jnp.where(first_row, 0.0, behind)
        apart = ahead - behind
        real = dot3((ax_ref[0, 0], ax_ref[0, 1]), split(both))
        real = real + alternate[:KEPT_X] * norm_scale() * middle
        imag = dot3((ax_ref[1, 0], ax_ref[1, 1]), split(apart))
        spans = []
        for parity in range(2):
            lanes = slice(128 * parity, 128 * parity + 128)
            spans.append(
                dot3(
                    split(jnp.concatenate([real[:, lanes], imag[:, lanes]], 1)),
                    (ay_ref[parity, 0], ay_ref[parity, 1]),
                )
            )
        spec_ref[index, 0] = spans[0] + spans[1]
        spec_ref[index, 1] = spans[0] - spans[1]

    for kind in range(2):
        for c in range(3):
            analyse(3 * kind + c, kind, c)

    kx_kept = kx_rows[:KEPT_X]

    def times_i(value):
        return pltpu.roll(value, 64, 1) * half_sign

    out_ref[KEPT_W:] = jnp.zeros((WIDE - KEPT_W,) + out_ref.shape[1:], jnp.float32)
    if plane == 0:
        rest_ref[KEPT_W:] = jnp.zeros((WIDE - KEPT_W,) + rest_ref.shape[1:], jnp.float32)

    def put(n, tile, value):
        rows = slice(tile * ROWS_X, tile * ROWS_X + ROWS_X)
        out_ref[:KEPT_W, n, rows, :] = value.reshape(KEPT_W, ROWS_X, 128)

    def values_of(n):
        at = (n // 2, slice(None), slice(128 * (n % 2), 128 * (n % 2) + 128))
        item = [spec_ref[(index,) + at] for index in range(6)]
        ky = ky_lanes[n]
        return [
            item[0] + times_i(ky * item[5]),
            item[1] - times_i(kx_kept * item[5]),
            item[2] + times_i(kx_kept * item[4] - ky * item[3]),
            item[3],
            item[4],
        ]

    lane = lax.broadcasted_iota(jnp.int32, (1, 128), 1)
    for half in range(2):
        heavy, light = HEAVY[half], LIGHT[half]
        values = values_of(heavy)
        direct = 3 if plane == 0 else 4
        for f in range(BACK):
            if f < direct:
                put(heavy, f, values[f])
            else:
                put(light, f - direct if plane == 0 else 3, values[f])
        values = values_of(light)
        packed = []
        for tile in range(2):
            value = jnp.zeros((KEPT_X, 128), jnp.float32)
            for slot in range(5):
                f, part = divmod(5 * tile + slot, 2)
                moved = pltpu.roll(
                    values[f], (SLOT * slot - 64 * part - LIGHT_ROW[half]) % 128, 1
                )
                value = jnp.where((lane >= SLOT * slot) & (lane < SLOT * slot + SLOT), moved, value)
            packed.append(value)
        if plane == 0:
            put(light, 2, packed[0])
            rest_ref[:KEPT_W, half] = packed[1].reshape(KEPT_W, ROWS_X, 128)
        else:
            out_ref[:, light, 0:ROWS_X, :] = rest_ref[:, half]
            put(light, 1, packed[0])
            put(light, 2, packed[1])


def run_plane(plane, got, rest=None):
    tables = [tables_synth_y(), tables_synth_x(), tables_anal_x(), tables_anal_y()]
    tiles = 3 + plane
    out_shape = [jax.ShapeDtypeStruct((WIDE, NARROW, tiles * ROWS_X, 128), jnp.float32)]
    operands = [got.reshape(DEVICES * ROWS_X * SENT, 128)] + [jnp.asarray(t) for t in tables]
    if plane == 0:
        out_shape.append(jax.ShapeDtypeStruct((WIDE, 2, ROWS_X, 128), jnp.float32))
    else:
        operands.append(rest)
    outs = pl.pallas_call(
        functools.partial(plane_kernel, plane),
        out_shape=out_shape,
        in_specs=[pl.BlockSpec(memory_space=pltpu.VMEM)] * len(operands),
        out_specs=[pl.BlockSpec(memory_space=pltpu.VMEM)] * len(out_shape),
        scratch_shapes=[
            pltpu.VMEM((6, 2, KEPT_X, 256), jnp.float32),
            pltpu.VMEM((9, 2, 256, 256), jnp.float32),
        ],
        compiler_params=pltpu.CompilerParams(vmem_limit_bytes=vmem_bytes),
        name="plane",
    )(*operands)
    return [outs[0].reshape(DEVICES, tiles * ROWS_X, 128)] + list(outs[1:])


def spans_of(tiles, table):
    upper, lower = split(jnp.concatenate([rows.T for rows in tiles], 0))
    span = dot(jnp.concatenate([upper, lower, upper], 1), table, ((1,), (0,)))
    return [span[128 * at : 128 * at + 128] for at in range(len(tiles))]


def unite(span, real_rows, imag_rows):
    real, imag = span[real_rows], span[imag_rows]
    return real[:, :128] + imag[:, 128:], imag[:, :128] - real[:, 128:]


def mirror(first, second):
    return tuple(
        jnp.concatenate([one + two, one - two], 1) for one, two in zip(first, second)
    )


def light_narrow(narrow):
    return (narrow == LIGHT[0]) | (narrow == LIGHT[1])


def tile_copies(source_ref, first, count, target_ref, at, sems):
    return [
        pltpu.make_async_copy(
            source_ref.at[:, pl.ds((first + tile) * ROWS_X, ROWS_X)],
            target_ref.at[at + tile],
            sems.at[at + tile],
        )
        for tile in range(count)
    ]


def begin_kernel(
    back_ref, more_ref, table_ref, part_ref, got_ref, new_ref, sems, whole_sems
):
    def store(k):
        return pltpu.make_async_copy(new_ref.at[k], part_ref.at[k], sems.at[k])

    @pl.when(jnp.logical_not(light_narrow(lax.axis_index("narrow"))))
    def _():
        pieces = tile_copies(back_ref, 0, 3, got_ref, 0, whole_sems)
        pieces += tile_copies(more_ref, 0, 2, got_ref, 3, whole_sems)
        for copy in pieces:
            copy.start()
        for copy in pieces:
            copy.wait()
        for k in range(ROWS_X):
            spans = spans_of([got_ref[f, :, k, :] for f in range(BACK)], table_ref[0])
            for f, span in enumerate(spans):
                real, imag = unite(span, slice(0, 64), slice(64, 128))
                new_ref[k, f, 0] = real
                new_ref[k, f, 1] = imag
            store(k).start()
        for k in range(ROWS_X):
            store(k).wait()


def begin(back, more):
    table = tables_anal_z()
    block = (ROWS_X, BACK, 2, ROWS_Y, 128)
    return pl.pallas_call(
        begin_kernel,
        in_specs=[
            pl.BlockSpec(memory_space=pltpu.HBM),
            pl.BlockSpec(memory_space=pltpu.HBM),
            pl.BlockSpec(memory_space=pltpu.VMEM),
        ],
        out_specs=pl.BlockSpec(memory_space=pltpu.HBM),
        out_shape=jax.ShapeDtypeStruct(block, jnp.float32),
        scratch_shapes=[
            pltpu.VMEM((BACK, DEVICES, ROWS_X, 128), jnp.float32),
            pltpu.VMEM(block, jnp.float32),
            pltpu.SemaphoreType.DMA((ROWS_X,)),
            pltpu.SemaphoreType.DMA((BACK,)),
        ],
        compiler_params=pltpu.CompilerParams(vmem_limit_bytes=finish_bytes),
        name="begin",
    )(back, more, jnp.asarray(table))


def in_hbm(array):
    return pltpu.with_memory_space_constraint(array, pltpu.HBM)


def in_vmem(array):
    return pltpu.with_memory_space_constraint(array, pltpu.VMEM)


def finish_kernel(
    back0_ref,
    back1_ref,
    more_ref,
    part_ref,
    adjoint_ref,
    table_ref,
    out_ref,
    new_ref,
    factor_ref,
    mid_ref,
    tile_ref,
    got_ref,
    sems,
    mid_sems,
    tile_sems,
):
    wide, narrow = lax.axis_index("wide"), lax.axis_index("narrow")
    is_light = light_narrow(narrow)

    def fetch(k):
        return pltpu.make_async_copy(part_ref.at[k], mid_ref.at[k], mid_sems.at[k])

    tile_copy = pltpu.make_async_copy(
        back0_ref.at[:, pl.ds(2 * ROWS_X, ROWS_X)], tile_ref, mid_sems.at[0]
    )

    def store(k):
        return pltpu.make_async_copy(new_ref.at[:, :, k], out_ref.at[:, :, k], sems.at[k])

    number_z = signed(lax.broadcasted_iota(jnp.int32, (1, NZ), 1), NZ)
    kz = 2.0 * math.pi / NZ * number_z.astype(jnp.float32)

    number_y = signed(
        lax.broadcasted_iota(jnp.int32, (ROWS_Y, 1), 0) + narrow * ROWS_Y, NY
    )
    all_ky = 2.0 * math.pi / NY * number_y.astype(jnp.float32)

    def wave_x(k):
        number_x = wide * ROWS_X + k
        return number_x, 2.0 * math.pi / NX * number_x.astype(jnp.float32)

    def prepare():
        keep_yz = (3 * jnp.abs(number_y) < NY) & (3 * jnp.abs(number_z) < NZ)
        scale_yz = keep_yz.astype(jnp.float32) * section_step
        square_yz = all_ky * all_ky + kz * kz
        for k in range(ROWS_X):
            number_x, kx = wave_x(k)
            ksquare = kx * kx + square_yz
            decay = jnp.exp(-viscous_rate * ksquare)
            factor_ref[0, k] = 1.0 / (ksquare + (ksquare == 0).astype(jnp.float32))
            factor_ref[1, k] = decay
            factor_ref[2, k] = scale_yz * (3 * number_x < NX).astype(jnp.float32) * decay

    def emit(k, got, start, rows):
        at = pl.ds(start, rows)
        kx = wave_x(k)[1]
        row = lax.broadcasted_iota(jnp.int32, (rows, 1), 0) + start + narrow * ROWS_Y
        ky = 2.0 * math.pi / NY * signed(row, NY).astype(jnp.float32)
        conv = [
            (got[0][0] + kz * got[4][1], got[0][1] - kz * got[4][0]),
            (got[1][0] - kz * got[3][1], got[1][1] + kz * got[3][0]),
            got[2],
        ]
        inverse, decay, gain = [factor_ref[which, k, at, :] for which in range(3)]
        waves = (kx, ky, kz)
        for part in range(2):
            along = (kx * conv[0][part] + ky * conv[1][part] + kz * conv[2][part]) * inverse
            for c in range(3):
                new_ref[c, part, k, at, :] = decay * adjoint_ref[c, part, k, at, :] + gain * (
                    conv[c][part] - waves[c] * along
                )

    @pl.when(jnp.logical_not(is_light))
    def _():
        pieces = tile_copies(back1_ref, 0, 4, got_ref, 0, tile_sems)
        for copy in pieces:
            copy.start()
        for k in range(ROWS_X):
            fetch(k).start()
        prepare()
        for copy in pieces:
            copy.wait()
        for k in range(ROWS_X):
            got = []
            spans = spans_of(
                [got_ref[f, :, k, :] for f in range(4)] + [more_ref[:, k, :]],
                table_ref[1],
            )
            fetch(k).wait()
            for f, span in enumerate(spans):
                second = unite(span, slice(0, 64), slice(64, 128))
                got.append(mirror((mid_ref[k, f, 0], mid_ref[k, f, 1]), second))
            emit(k, got, 0, ROWS_Y)
            store(k).start()

    @pl.when(is_light)
    def _():
        pieces = tile_copies(back1_ref, 0, 3, got_ref, 0, tile_sems) + [tile_copy]
        for copy in pieces:
            copy.start()
        prepare()
        for copy in pieces:
            copy.wait()
        for k in range(ROWS_X):
            by_plane = [
                spans_of(rows, table_ref[plane])
                for plane, rows in enumerate(
                    (
                        (tile_ref[:, k, :], got_ref[0, :, k, :]),
                        (got_ref[1, :, k, :], got_ref[2, :, k, :]),
                    )
                )
            ]

            def item(index, plane):
                tile, slot = divmod(index, 5)
                return by_plane[plane][tile][SLOT * slot : SLOT * slot + SLOT]

            got = []
            for f in range(BACK):
                halves_of = [
                    unite(
                        jnp.concatenate([item(2 * f, plane), item(2 * f + 1, plane)], 0),
                        slice(0, SLOT),
                        slice(SLOT, 2 * SLOT),
                    )
                    for plane in range(2)
                ]
                got.append(mirror(*halves_of))
            for c in range(3):
                for part in range(2):
                    new_ref[c, part, k] = factor_ref[1, k] * adjoint_ref[c, part, k]
            start = pl.multiple_of(jnp.where(narrow == LIGHT[0], 0, LIGHT_ROW[1]), 8)
            emit(k, got, start, SLOT)
            store(k).start()

    for k in range(ROWS_X):
        store(k).wait()


def finish(back0, back1, more, part, adjoint_hat):
    table = tables_anal_z()
    block = (3, 2, ROWS_X, ROWS_Y, NZ)
    return pl.pallas_call(
        finish_kernel,
        in_specs=[
            pl.BlockSpec(memory_space=pltpu.HBM),
            pl.BlockSpec(memory_space=pltpu.HBM),
            pl.BlockSpec(memory_space=pltpu.VMEM),
            pl.BlockSpec(memory_space=pltpu.HBM),
            pl.BlockSpec(memory_space=pltpu.VMEM),
            pl.BlockSpec(memory_space=pltpu.VMEM),
        ],
        out_specs=pl.BlockSpec(memory_space=pltpu.HBM),
        out_shape=jax.ShapeDtypeStruct(block, jnp.float32),
        scratch_shapes=[
            pltpu.VMEM(block, jnp.float32),
            pltpu.VMEM((3, ROWS_X, ROWS_Y, NZ), jnp.float32),
            pltpu.VMEM((ROWS_X, BACK, 2, ROWS_Y, 128), jnp.float32),
            pltpu.VMEM((DEVICES, ROWS_X, 128), jnp.float32),
            pltpu.VMEM((4, DEVICES, ROWS_X, 128), jnp.float32),
            pltpu.SemaphoreType.DMA((ROWS_X,)),
            pltpu.SemaphoreType.DMA((ROWS_X,)),
            pltpu.SemaphoreType.DMA((4,)),
        ],
        compiler_params=pltpu.CompilerParams(vmem_limit_bytes=finish_bytes),
        name="finish",
    )(
        in_hbm(back0),
        in_hbm(back1),
        in_vmem(more),
        in_hbm(part),
        in_vmem(adjoint_hat),
        jnp.asarray(table),
    )


def swap(chunks):
    return lax.all_to_all(chunks, ("wide", "narrow"), 0, 0, tiled=True)


def forward(tiles):
    return lax.ppermute(tiles, "narrow", [(LIGHT[0], HEAVY[0]), (LIGHT[1], HEAVY[1])])


def local(adjoint_hat, velocity_hat):
    got = [swap(synth_z(adjoint_hat, velocity_hat, plane)) for plane in range(2)]
    out0, rest = run_plane(0, got[0])
    back0 = swap(out0)
    (out1,) = run_plane(1, got[1], rest)
    back1 = swap(out1)
    more0 = forward(back0[:, : 2 * ROWS_X])
    part = begin(back0, more0)
    back1, part = lax.optimization_barrier((back1, part))
    more1 = forward(back1[:, 3 * ROWS_X :])
    return finish(back0, back1, more1, part, adjoint_hat)


def solution(mesh):
    in_specs = (P(None, None, "wide", "narrow", None), P(None, None, "wide", "narrow", None))
    out_specs = P(None, None, "wide", "narrow", None)
    return jax.shard_map(local, mesh=mesh, in_specs=in_specs, out_specs=out_specs, check_vma=False)
```

```python
import functools
import math

import jax
import jax.numpy as jnp
import ml_dtypes
import numpy as np
from jax import lax
from jax.experimental import pallas as pl
from jax.experimental.pallas import tpu as pltpu
from jax.sharding import PartitionSpec as P

NX = 512
NY = 256
NZ = 256
KX = 256
ROWS_X = 8
ROWS_Y = 64
WIDE = 32
NARROW = 4
DEVICES = WIDE * NARROW
SENT = 8
BACK = 5
KEPT_X = 176
KEPT_W = KEPT_X // ROWS_X
HEAVY = (0, 3)
LIGHT = (1, 2)
LIGHT_ROW = (0, 40)
SLOT = 24
WAITS = {0: 1, 1: 4, 4: 8}

section_step = 0.25
viscous_rate = 0.05
vmem_bytes = 60 * 1024 * 1024
finish_bytes = 24 * 1024 * 1024


def halves(table):
    upper = table.astype(ml_dtypes.bfloat16)
    lower = (table - upper.astype(np.float64)).astype(ml_dtypes.bfloat16)
    return np.stack([upper, lower])


def turn(modes, places, length):
    angle = 2.0 * np.pi / length * (np.outer(modes, places) % length)
    return np.cos(angle), np.sin(angle)


def tables_synth_z():
    quarter = np.arange(128)
    parts = []
    for plane in range(2):
        cosine, sine = turn(2 * np.arange(128) + plane, quarter, NZ)
        upper, lower = halves(np.concatenate([cosine, sine], 0))
        parts.append(np.concatenate([upper, upper, lower], 1))
    return np.stack(parts)


def tables_synth_y():
    mode = np.arange(128)
    parts = []
    for parity in range(2):
        cosine, sine = turn(mode, 2 * np.arange(128) + parity, NY)
        real_rows = np.concatenate([cosine, sine], 1)
        imag_rows = np.concatenate([-sine, cosine], 1)
        stacked = np.stack([real_rows.reshape(2, 64, 256), imag_rows.reshape(2, 64, 256)], 1)
        parts.append(halves(stacked.reshape(256, 256)))
    return np.stack(parts)


def norm_scale():
    return 1.0 / math.sqrt(NX * NY * NZ)


def tables_synth_x():
    weight = np.where(np.arange(KX) == 0, 1.0, 2.0) * norm_scale()
    cosine, sine = turn(np.arange(256), np.arange(KX), NX)
    return np.stack([halves(cosine * weight), halves(-sine * weight)])


def tables_anal_x():
    cosine, sine = turn(np.arange(KEPT_X), np.arange(256), NX)
    return np.stack([halves(cosine * norm_scale()), halves(-sine * norm_scale())])


def tables_anal_y():
    parts = []
    mode = np.arange(128)
    for parity in range(2):
        cosine, sine = turn(2 * np.arange(128) + parity, mode, NY)
        cosine = cosine.reshape(128, 2, 1, 64)
        sine = sine.reshape(128, 2, 1, 64)
        real_rows = np.concatenate([cosine, -sine], 2).reshape(128, 256)
        imag_rows = np.concatenate([sine, cosine], 2).reshape(128, 256)
        parts.append(halves(np.concatenate([real_rows, imag_rows], 0)))
    return np.stack(parts)


def tables_anal_z():
    parts = []
    for plane in range(2):
        cosine, sine = turn(2 * np.arange(128) + plane, np.arange(128), NZ)
        upper, lower = halves(np.concatenate([cosine, sine], 1))
        parts.append(np.concatenate([upper, upper, lower], 0))
    return np.stack(parts)


def split(value):
    upper = value.astype(jnp.bfloat16)
    lower = (value - upper.astype(jnp.float32)).astype(jnp.bfloat16)
    return upper, lower


def dot(left, right, dims):
    return lax.dot_general(left, right, (dims, ((), ())), preferred_element_type=jnp.float32)


def dot3(left, right, dims=((1,), (0,))):
    return (
        dot(left[0], right[0], dims)
        + dot(left[0], right[1], dims)
        + dot(left[1], right[0], dims)
    )


def signed(number, length):
    return jnp.where(number < length // 2, number, number - length)


def wave_y(start, shape, axis):
    number = lax.broadcasted_iota(jnp.int32, shape, axis) + start
    return 2.0 * math.pi / NY * signed(number, NY).astype(jnp.float32)


def wave_z(shape, axis):
    number = lax.broadcasted_iota(jnp.int32, shape, axis)
    return 2.0 * math.pi / NZ * signed(number, NZ).astype(jnp.float32)


def synth_z_kernel(
    plane, adjoint_ref, velocity_ref, table_ref, out_ref, adj_ref, vel_ref, turn_ref, sent_ref, sems
):
    def load(k, which):
        source, target = ((adjoint_ref, adj_ref), (velocity_ref, vel_ref))[which]
        return pltpu.make_async_copy(source.at[:, :, k], target.at[:, :, k], sems.at[which, k])

    def store(k):
        return pltpu.make_async_copy(
            sent_ref.at[k], out_ref.at[:, pl.ds(k * SENT, SENT)], sems.at[2, k]
        )

    turn_copy = pltpu.make_async_copy(table_ref, turn_ref, sems.at[3, 0])
    for k in range(ROWS_X):
        for which in range(2):
            load(k, which).start()
        if k == 0:
            turn_copy.start()
    ky = wave_y(lax.axis_index("narrow") * ROWS_Y, (ROWS_Y, 1), 0)
    kz = wave_z((1, NZ), 1)
    half_sign = jnp.where(lax.broadcasted_iota(jnp.int32, (1, 128), 1) < 64, -1.0, 1.0)

    for k in range(ROWS_X):
        number_x = lax.axis_index("wide") * ROWS_X + k
        kx = 2.0 * math.pi / NX * number_x.astype(jnp.float32)
        if k == 0:
            turn_copy.wait()
        if k in WAITS:
            for near in range(k, WAITS[k]):
                for which in range(2):
                    load(near, which).wait()
        vel = [[vel_ref[c, part, k] for part in range(2)] for c in range(3)]
        fields = [(adj_ref[c, 0, k], adj_ref[c, 1, k]) for c in range(3)]
        fields += [(vel[c][0], vel[c][1]) for c in range(3)]
        fields.append((kz * vel[1][1] - ky * vel[2][1], ky * vel[2][0] - kz * vel[1][0]))
        fields.append((kx * vel[2][1] - kz * vel[0][1], kz * vel[0][0] - kx * vel[2][0]))
        for pair in range(SENT // 2):
            rows = [part for field in fields[2 * pair : 2 * pair + 2] for part in field]
            value = jnp.concatenate(rows, 0)
            if plane == 0:
                merged = value[:, :128] + value[:, 128:]
            else:
                merged = value[:, :128] - value[:, 128:]
            upper, lower = split(merged)
            stacked = jnp.concatenate([upper, lower, upper], 1)
            both = dot(turn_ref[...], stacked, ((1,), (1,)))
            for f in range(2):
                lanes = slice(128 * f, 128 * f + 128)
                turned = pltpu.roll(both[128:, lanes], 64, 1)
                sent_ref[k, :, 2 * pair + f, :] = both[:128, lanes] + half_sign * turned
        store(k).start()
    for k in range(ROWS_X):
        store(k).wait()


def synth_z(adjoint_hat, velocity_hat, plane):
    table = tables_synth_z()[plane]
    shape = (DEVICES, ROWS_X * SENT, 128)
    block = (3, 2, ROWS_X, ROWS_Y, NZ)
    return pl.pallas_call(
        functools.partial(synth_z_kernel, plane),
        in_specs=[
            pl.BlockSpec(memory_space=pl.ANY),
            pl.BlockSpec(memory_space=pl.ANY),
            pl.BlockSpec(memory_space=pl.ANY),
        ],
        out_specs=pl.BlockSpec(memory_space=pl.ANY),
        out_shape=jax.ShapeDtypeStruct(shape, jnp.float32),
        scratch_shapes=[
            pltpu.VMEM(block, jnp.float32),
            pltpu.VMEM(block, jnp.float32),
            pltpu.VMEM(table.shape, jnp.bfloat16),
            pltpu.VMEM((ROWS_X, DEVICES, SENT, 128), jnp.float32),
            pltpu.SemaphoreType.DMA((4, ROWS_X)),
        ],
        compiler_params=pltpu.CompilerParams(vmem_limit_bytes=vmem_bytes),
        name="synth_z",
    )(adjoint_hat, velocity_hat, jnp.asarray(table))


def plane_kernel(plane, got_ref, sy_ref, sx_ref, ax_ref, ay_ref, *refs):
    if plane == 0:
        out_ref, rest_ref, spec_ref, cell_ref = refs
    else:
        rest_ref, out_ref, spec_ref, cell_ref = refs
    chunk = ROWS_X * SENT
    half_sign = jnp.where(lax.broadcasted_iota(jnp.int32, (1, 128), 1) < 64, -1.0, 1.0)
    ky_lanes = []
    for n in range(NARROW):
        number = lax.broadcasted_iota(jnp.int32, (1, 128), 1) % 64 + n * ROWS_Y
        ky_lanes.append(2.0 * math.pi / NY * signed(number, NY).astype(jnp.float32))
    kx_rows = 2.0 * math.pi / NX * lax.broadcasted_iota(jnp.int32, (KX, 1), 0).astype(jnp.float32)
    alternate = jnp.where(lax.broadcasted_iota(jnp.int32, (KX, 1), 0) % 2 == 0, 1.0, -1.0)
    weight = (
        jnp.where(lax.broadcasted_iota(jnp.int32, (KX, 1), 0) == 0, 1.0, 2.0) * norm_scale()
    )
    first_row = lax.broadcasted_iota(jnp.int32, (256, 1), 0) == 0

    def rows_of(field, n):
        return jnp.concatenate(
            [
                got_ref[pl.ds((w * NARROW + n) * chunk + field, ROWS_X, stride=SENT), :]
                for w in range(WIDE)
            ],
            0,
        )

    def synth(parts, index):
        spans = []
        for parity in range(2):
            if parity == 0:
                merged = [parts[0] + parts[2], parts[1] + parts[3]]
            else:
                merged = [parts[0] - parts[2], parts[1] - parts[3]]
            spans.append(
                dot3(
                    split(jnp.concatenate(merged, 1)), (sy_ref[parity, 0], sy_ref[parity, 1])
                )
            )
        real = jnp.concatenate([spans[0][:, :128], spans[1][:, :128]], 1)
        imag = jnp.concatenate([spans[0][:, 128:], spans[1][:, 128:]], 1)
        cosine = dot3((sx_ref[0, 0], sx_ref[0, 1]), split(real))
        sine = dot3((sx_ref[1, 0], sx_ref[1, 1]), split(imag))
        middle = jnp.sum(real * (alternate * weight), 0, keepdims=True)
        cell_ref[index, 0] = cosine + sine
        cell_ref[index, 1] = jnp.where(first_row, middle, cosine - sine)

    def each_field(field, carry):
        synth([rows_of(field, n) for n in range(NARROW)], field)
        return carry

    lax.fori_loop(0, SENT, each_field, 0)
    swirl = []
    for n in range(NARROW):
        across = kx_rows * rows_of(4, n) - ky_lanes[n] * rows_of(3, n)
        swirl.append(pltpu.roll(across, 64, 1) * half_sign)
    synth(swirl, SENT)

    def product(kind, c, mirror):
        one, two = (c + 1) % 3, (c + 2) % 3
        if kind == 0:
            return (
                cell_ref[one, mirror] * cell_ref[6 + two, mirror]
                - cell_ref[two, mirror] * cell_ref[6 + one, mirror]
            )
        return (
            cell_ref[3 + one, mirror] * cell_ref[two, mirror]
            - cell_ref[3 + two, mirror] * cell_ref[one, mirror]
        )

    def analyse(index, kind, c):
        ahead = product(kind, c, 0)
        behind = product(kind, c, 1)
        middle = behind[0:1]
        both = ahead + jnp.where(first_row, 0.0, behind)
        apart = ahead - behind
        real = dot3((ax_ref[0, 0], ax_ref[0, 1]), split(both))
        real = real + alternate[:KEPT_X] * norm_scale() * middle
        imag = dot3((ax_ref[1, 0], ax_ref[1, 1]), split(apart))
        spans = []
        for parity in range(2):
            lanes = slice(128 * parity, 128 * parity + 128)
            spans.append(
                dot3(
                    split(jnp.concatenate([real[:, lanes], imag[:, lanes]], 1)),
                    (ay_ref[parity, 0], ay_ref[parity, 1]),
                )
            )
        spec_ref[index, 0] = spans[0] + spans[1]
        spec_ref[index, 1] = spans[0] - spans[1]

    for kind in range(2):
        for c in range(3):
            analyse(3 * kind + c, kind, c)

    kx_kept = kx_rows[:KEPT_X]

    def times_i(value):
        return pltpu.roll(value, 64, 1) * half_sign

    out_ref[KEPT_W:] = jnp.zeros((WIDE - KEPT_W,) + out_ref.shape[1:], jnp.float32)
    if plane == 0:
        rest_ref[KEPT_W:] = jnp.zeros((WIDE - KEPT_W,) + rest_ref.shape[1:], jnp.float32)

    def put(n, tile, value):
        rows = slice(tile * ROWS_X, tile * ROWS_X + ROWS_X)
        out_ref[:KEPT_W, n, rows, :] = value.reshape(KEPT_W, ROWS_X, 128)

    def values_of(n):
        at = (n // 2, slice(None), slice(128 * (n % 2), 128 * (n % 2) + 128))
        item = [spec_ref[(index,) + at] for index in range(6)]
        ky = ky_lanes[n]
        return [
            item[0] + times_i(ky * item[5]),
            item[1] - times_i(kx_kept * item[5]),
            item[2] + times_i(kx_kept * item[4] - ky * item[3]),
            item[3],
            item[4],
        ]

    lane = lax.broadcasted_iota(jnp.int32, (1, 128), 1)
    for half in range(2):
        heavy, light = HEAVY[half], LIGHT[half]
        values = values_of(heavy)
        direct = 3 if plane == 0 else 4
        for f in range(BACK):
            if f < direct:
                put(heavy, f, values[f])
            else:
                put(light, f - direct if plane == 0 else 3, values[f])
        values = values_of(light)
        packed = []
        for tile in range(2):
            value = jnp.zeros((KEPT_X, 128), jnp.float32)
            for slot in range(5):
                f, part = divmod(5 * tile + slot, 2)
                moved = pltpu.roll(
                    values[f], (SLOT * slot - 64 * part - LIGHT_ROW[half]) % 128, 1
                )
                value = jnp.where((lane >= SLOT * slot) & (lane < SLOT * slot + SLOT), moved, value)
            packed.append(value)
        if plane == 0:
            put(light, 2, packed[0])
            rest_ref[:KEPT_W, half] = packed[1].reshape(KEPT_W, ROWS_X, 128)
        else:
            out_ref[:, light, 0:ROWS_X, :] = rest_ref[:, half]
            put(light, 1, packed[0])
            put(light, 2, packed[1])


def run_plane(plane, got, rest=None):
    tables = [tables_synth_y(), tables_synth_x(), tables_anal_x(), tables_anal_y()]
    tiles = 3 + plane
    out_shape = [jax.ShapeDtypeStruct((WIDE, NARROW, tiles * ROWS_X, 128), jnp.float32)]
    operands = [got.reshape(DEVICES * ROWS_X * SENT, 128)] + [jnp.asarray(t) for t in tables]
    if plane == 0:
        out_shape.append(jax.ShapeDtypeStruct((WIDE, 2, ROWS_X, 128), jnp.float32))
    else:
        operands.append(rest)
    outs = pl.pallas_call(
        functools.partial(plane_kernel, plane),
        out_shape=out_shape,
        in_specs=[pl.BlockSpec(memory_space=pltpu.VMEM)] * len(operands),
        out_specs=[pl.BlockSpec(memory_space=pltpu.VMEM)] * len(out_shape),
        scratch_shapes=[
            pltpu.VMEM((6, 2, KEPT_X, 256), jnp.float32),
            pltpu.VMEM((9, 2, 256, 256), jnp.float32),
        ],
        compiler_params=pltpu.CompilerParams(vmem_limit_bytes=vmem_bytes),
        name="plane",
    )(*operands)
    return [outs[0].reshape(DEVICES, tiles * ROWS_X, 128)] + list(outs[1:])


def spans_of(tiles, table):
    upper, lower = split(jnp.concatenate([rows.T for rows in tiles], 0))
    span = dot(jnp.concatenate([upper, lower, upper], 1), table, ((1,), (0,)))
    return [span[128 * at : 128 * at + 128] for at in range(len(tiles))]


def unite(span, real_rows, imag_rows):
    real, imag = span[real_rows], span[imag_rows]
    return real[:, :128] + imag[:, 128:], imag[:, :128] - real[:, 128:]


def mirror(first, second):
    return tuple(
        jnp.concatenate([one + two, one - two], 1) for one, two in zip(first, second)
    )


def light_narrow(narrow):
    return (narrow == LIGHT[0]) | (narrow == LIGHT[1])


def tile_copies(source_ref, first, count, target_ref, at, sems):
    return [
        pltpu.make_async_copy(
            source_ref.at[:, pl.ds((first + tile) * ROWS_X, ROWS_X)],
            target_ref.at[at + tile],
            sems.at[at + tile],
        )
        for tile in range(count)
    ]


def begin_kernel(
    back_ref, more_ref, table_ref, part_ref, got_ref, new_ref, sems, whole_sems
):
    def store(k):
        return pltpu.make_async_copy(new_ref.at[k], part_ref.at[k], sems.at[k])

    @pl.when(jnp.logical_not(light_narrow(lax.axis_index("narrow"))))
    def _():
        pieces = tile_copies(back_ref, 0, 3, got_ref, 0, whole_sems)
        pieces += tile_copies(more_ref, 0, 2, got_ref, 3, whole_sems)
        for copy in pieces:
            copy.start()
        for copy in pieces:
            copy.wait()
        for k in range(ROWS_X):
            spans = spans_of([got_ref[f, :, k, :] for f in range(BACK)], table_ref[0])
            for f, span in enumerate(spans):
                real, imag = unite(span, slice(0, 64), slice(64, 128))
                new_ref[k, f, 0] = real
                new_ref[k, f, 1] = imag
            store(k).start()
        for k in range(ROWS_X):
            store(k).wait()


def begin(back, more):
    table = tables_anal_z()
    block = (ROWS_X, BACK, 2, ROWS_Y, 128)
    return pl.pallas_call(
        begin_kernel,
        in_specs=[
            pl.BlockSpec(memory_space=pltpu.HBM),
            pl.BlockSpec(memory_space=pltpu.HBM),
            pl.BlockSpec(memory_space=pltpu.VMEM),
        ],
        out_specs=pl.BlockSpec(memory_space=pltpu.HBM),
        out_shape=jax.ShapeDtypeStruct(block, jnp.float32),
        scratch_shapes=[
            pltpu.VMEM((BACK, DEVICES, ROWS_X, 128), jnp.float32),
            pltpu.VMEM(block, jnp.float32),
            pltpu.SemaphoreType.DMA((ROWS_X,)),
            pltpu.SemaphoreType.DMA((BACK,)),
        ],
        compiler_params=pltpu.CompilerParams(vmem_limit_bytes=finish_bytes),
        name="begin",
    )(back, more, jnp.asarray(table))


def in_hbm(array):
    return pltpu.with_memory_space_constraint(array, pltpu.HBM)


def in_vmem(array):
    return pltpu.with_memory_space_constraint(array, pltpu.VMEM)


def finish_kernel(
    back0_ref,
    back1_ref,
    more_ref,
    part_ref,
    adjoint_ref,
    table_ref,
    out_ref,
    new_ref,
    factor_ref,
    mid_ref,
    tile_ref,
    got_ref,
    sems,
    mid_sems,
    tile_sems,
):
    wide, narrow = lax.axis_index("wide"), lax.axis_index("narrow")
    is_light = light_narrow(narrow)

    def fetch(k):
        return pltpu.make_async_copy(part_ref.at[k], mid_ref.at[k], mid_sems.at[k])

    tile_copy = pltpu.make_async_copy(
        back0_ref.at[:, pl.ds(2 * ROWS_X, ROWS_X)], tile_ref, mid_sems.at[0]
    )

    def store(k):
        return pltpu.make_async_copy(new_ref.at[:, :, k], out_ref.at[:, :, k], sems.at[k])

    number_z = signed(lax.broadcasted_iota(jnp.int32, (1, NZ), 1), NZ)
    kz = 2.0 * math.pi / NZ * number_z.astype(jnp.float32)

    number_y = signed(
        lax.broadcasted_iota(jnp.int32, (ROWS_Y, 1), 0) + narrow * ROWS_Y, NY
    )
    all_ky = 2.0 * math.pi / NY * number_y.astype(jnp.float32)

    def wave_x(k):
        number_x = wide * ROWS_X + k
        return number_x, 2.0 * math.pi / NX * number_x.astype(jnp.float32)

    def prepare():
        keep_yz = (3 * jnp.abs(number_y) < NY) & (3 * jnp.abs(number_z) < NZ)
        scale_yz = keep_yz.astype(jnp.float32) * section_step
        square_yz = all_ky * all_ky + kz * kz
        for k in range(ROWS_X):
            number_x, kx = wave_x(k)
            ksquare = kx * kx + square_yz
            decay = jnp.exp(-viscous_rate * ksquare)
            factor_ref[0, k] = 1.0 / (ksquare + (ksquare == 0).astype(jnp.float32))
            factor_ref[1, k] = decay
            factor_ref[2, k] = scale_yz * (3 * number_x < NX).astype(jnp.float32) * decay

    def emit(k, got, start, rows):
        at = pl.ds(start, rows)
        kx = wave_x(k)[1]
        row = lax.broadcasted_iota(jnp.int32, (rows, 1), 0) + start + narrow * ROWS_Y
        ky = 2.0 * math.pi / NY * signed(row, NY).astype(jnp.float32)
        conv = [
            (got[0][0] + kz * got[4][1], got[0][1] - kz * got[4][0]),
            (got[1][0] - kz * got[3][1], got[1][1] + kz * got[3][0]),
            got[2],
        ]
        inverse, decay, gain = [factor_ref[which, k, at, :] for which in range(3)]
        waves = (kx, ky, kz)
        for part in range(2):
            along = (kx * conv[0][part] + ky * conv[1][part] + kz * conv[2][part]) * inverse
            for c in range(3):
                new_ref[c, part, k, at, :] = decay * adjoint_ref[c, part, k, at, :] + gain * (
                    conv[c][part] - waves[c] * along
                )

    @pl.when(jnp.logical_not(is_light))
    def _():
        pieces = tile_copies(back1_ref, 0, 4, got_ref, 0, tile_sems)
        for copy in pieces:
            copy.start()
        for k in range(ROWS_X):
            fetch(k).start()
        prepare()
        for copy in pieces:
            copy.wait()
        for k in range(ROWS_X):
            got = []
            spans = spans_of(
                [got_ref[f, :, k, :] for f in range(4)] + [more_ref[:, k, :]],
                table_ref[1],
            )
            if k in (0, 2):
                for near in range(k, 2 if k == 0 else ROWS_X):
                    fetch(near).wait()
            for f, span in enumerate(spans):
                second = unite(span, slice(0, 64), slice(64, 128))
                got.append(mirror((mid_ref[k, f, 0], mid_ref[k, f, 1]), second))
            emit(k, got, 0, ROWS_Y)
            store(k).start()

    @pl.when(is_light)
    def _():
        pieces = tile_copies(back1_ref, 0, 3, got_ref, 0, tile_sems) + [tile_copy]
        for copy in pieces:
            copy.start()
        prepare()
        for copy in pieces:
            copy.wait()
        for k in range(ROWS_X):
            by_plane = [
                spans_of(rows, table_ref[plane])
                for plane, rows in enumerate(
                    (
                        (tile_ref[:, k, :], got_ref[0, :, k, :]),
                        (got_ref[1, :, k, :], got_ref[2, :, k, :]),
                    )
                )
            ]

            def item(index, plane):
                tile, slot = divmod(index, 5)
                return by_plane[plane][tile][SLOT * slot : SLOT * slot + SLOT]

            got = []
            for f in range(BACK):
                halves_of = [
                    unite(
                        jnp.concatenate([item(2 * f, plane), item(2 * f + 1, plane)], 0),
                        slice(0, SLOT),
                        slice(SLOT, 2 * SLOT),
                    )
                    for plane in range(2)
                ]
                got.append(mirror(*halves_of))
            for c in range(3):
                for part in range(2):
                    new_ref[c, part, k] = factor_ref[1, k] * adjoint_ref[c, part, k]
            start = pl.multiple_of(jnp.where(narrow == LIGHT[0], 0, LIGHT_ROW[1]), 8)
            emit(k, got, start, SLOT)
            store(k).start()

    for k in range(ROWS_X):
        store(k).wait()


def finish(back0, back1, more, part, adjoint_hat):
    table = tables_anal_z()
    block = (3, 2, ROWS_X, ROWS_Y, NZ)
    return pl.pallas_call(
        finish_kernel,
        in_specs=[
            pl.BlockSpec(memory_space=pltpu.HBM),
            pl.BlockSpec(memory_space=pltpu.HBM),
            pl.BlockSpec(memory_space=pltpu.VMEM),
            pl.BlockSpec(memory_space=pltpu.HBM),
            pl.BlockSpec(memory_space=pltpu.VMEM),
            pl.BlockSpec(memory_space=pltpu.VMEM),
        ],
        out_specs=pl.BlockSpec(memory_space=pltpu.HBM),
        out_shape=jax.ShapeDtypeStruct(block, jnp.float32),
        scratch_shapes=[
            pltpu.VMEM(block, jnp.float32),
            pltpu.VMEM((3, ROWS_X, ROWS_Y, NZ), jnp.float32),
            pltpu.VMEM((ROWS_X, BACK, 2, ROWS_Y, 128), jnp.float32),
            pltpu.VMEM((DEVICES, ROWS_X, 128), jnp.float32),
            pltpu.VMEM((4, DEVICES, ROWS_X, 128), jnp.float32),
            pltpu.SemaphoreType.DMA((ROWS_X,)),
            pltpu.SemaphoreType.DMA((ROWS_X,)),
            pltpu.SemaphoreType.DMA((4,)),
        ],
        compiler_params=pltpu.CompilerParams(vmem_limit_bytes=finish_bytes),
        name="finish",
    )(
        in_hbm(back0),
        in_hbm(back1),
        in_vmem(more),
        in_hbm(part),
        in_vmem(adjoint_hat),
        jnp.asarray(table),
    )


def swap(chunks):
    return lax.all_to_all(chunks, ("wide", "narrow"), 0, 0, tiled=True)


def forward(tiles):
    return lax.ppermute(tiles, "narrow", [(LIGHT[0], HEAVY[0]), (LIGHT[1], HEAVY[1])])


def local(adjoint_hat, velocity_hat):
    got = [swap(synth_z(adjoint_hat, velocity_hat, plane)) for plane in range(2)]
    out0, rest = run_plane(0, got[0])
    back0 = swap(out0)
    (out1,) = run_plane(1, got[1], rest)
    back1 = swap(out1)
    more0 = forward(back0[:, : 2 * ROWS_X])
    part = begin(back0, more0)
    back1, part = lax.optimization_barrier((back1, part))
    more1 = forward(back1[:, 3 * ROWS_X :])
    return finish(back0, back1, more1, part, adjoint_hat)


def solution(mesh):
    in_specs = (P(None, None, "wide", "narrow", None), P(None, None, "wide", "narrow", None))
    out_specs = P(None, None, "wide", "narrow", None)
    return jax.shard_map(local, mesh=mesh, in_specs=in_specs, out_specs=out_specs, check_vma=False)
```

```python
import functools
import math

import jax
import jax.numpy as jnp
import ml_dtypes
import numpy as np
from jax import lax
from jax.experimental import pallas as pl
from jax.experimental.pallas import tpu as pltpu
from jax.sharding import PartitionSpec as P

NX = 512
NY = 256
NZ = 256
KX = 256
ROWS_X = 8
ROWS_Y = 64
WIDE = 32
NARROW = 4
DEVICES = WIDE * NARROW
SENT = 8
BACK = 5
KEPT_X = 176
KEPT_W = KEPT_X // ROWS_X
HEAVY = (0, 3)
LIGHT = (1, 2)
LIGHT_ROW = (0, 40)
SLOT = 24
WAITS = {0: 1, 1: 3, 3: 8}

section_step = 0.25
viscous_rate = 0.05
vmem_bytes = 60 * 1024 * 1024
finish_bytes = 24 * 1024 * 1024


def halves(table):
    upper = table.astype(ml_dtypes.bfloat16)
    lower = (table - upper.astype(np.float64)).astype(ml_dtypes.bfloat16)
    return np.stack([upper, lower])


def turn(modes, places, length):
    angle = 2.0 * np.pi / length * (np.outer(modes, places) % length)
    return np.cos(angle), np.sin(angle)


def tables_synth_z():
    quarter = np.arange(128)
    parts = []
    for plane in range(2):
        cosine, sine = turn(2 * np.arange(128) + plane, quarter, NZ)
        upper, lower = halves(np.concatenate([cosine, sine], 0))
        parts.append(np.concatenate([upper, upper, lower], 1))
    return np.stack(parts)


def tables_synth_y():
    mode = np.arange(128)
    parts = []
    for parity in range(2):
        cosine, sine = turn(mode, 2 * np.arange(128) + parity, NY)
        real_rows = np.concatenate([cosine, sine], 1)
        imag_rows = np.concatenate([-sine, cosine], 1)
        stacked = np.stack([real_rows.reshape(2, 64, 256), imag_rows.reshape(2, 64, 256)], 1)
        parts.append(halves(stacked.reshape(256, 256)))
    return np.stack(parts)


def norm_scale():
    return 1.0 / math.sqrt(NX * NY * NZ)


def tables_synth_x():
    weight = np.where(np.arange(KX) == 0, 1.0, 2.0) * norm_scale()
    cosine, sine = turn(np.arange(256), np.arange(KX), NX)
    return np.stack([halves(cosine * weight), halves(-sine * weight)])


def tables_anal_x():
    cosine, sine = turn(np.arange(KEPT_X), np.arange(256), NX)
    return np.stack([halves(cosine * norm_scale()), halves(-sine * norm_scale())])


def tables_anal_y():
    parts = []
    mode = np.arange(128)
    for parity in range(2):
        cosine, sine = turn(2 * np.arange(128) + parity, mode, NY)
        cosine = cosine.reshape(128, 2, 1, 64)
        sine = sine.reshape(128, 2, 1, 64)
        real_rows = np.concatenate([cosine, -sine], 2).reshape(128, 256)
        imag_rows = np.concatenate([sine, cosine], 2).reshape(128, 256)
        parts.append(halves(np.concatenate([real_rows, imag_rows], 0)))
    return np.stack(parts)


def tables_anal_z():
    parts = []
    for plane in range(2):
        cosine, sine = turn(2 * np.arange(128) + plane, np.arange(128), NZ)
        upper, lower = halves(np.concatenate([cosine, sine], 1))
        parts.append(np.concatenate([upper, upper, lower], 0))
    return np.stack(parts)


def split(value):
    upper = value.astype(jnp.bfloat16)
    lower = (value - upper.astype(jnp.float32)).astype(jnp.bfloat16)
    return upper, lower


def dot(left, right, dims):
    return lax.dot_general(left, right, (dims, ((), ())), preferred_element_type=jnp.float32)


def dot3(left, right, dims=((1,), (0,))):
    return (
        dot(left[0], right[0], dims)
        + dot(left[0], right[1], dims)
        + dot(left[1], right[0], dims)
    )


def signed(number, length):
    return jnp.where(number < length // 2, number, number - length)


def wave_y(start, shape, axis):
    number = lax.broadcasted_iota(jnp.int32, shape, axis) + start
    return 2.0 * math.pi / NY * signed(number, NY).astype(jnp.float32)


def wave_z(shape, axis):
    number = lax.broadcasted_iota(jnp.int32, shape, axis)
    return 2.0 * math.pi / NZ * signed(number, NZ).astype(jnp.float32)


def synth_z_kernel(
    plane, adjoint_ref, velocity_ref, table_ref, out_ref, adj_ref, vel_ref, turn_ref, sent_ref, sems
):
    def load(k, which):
        source, target = ((adjoint_ref, adj_ref), (velocity_ref, vel_ref))[which]
        return pltpu.make_async_copy(source.at[:, :, k], target.at[:, :, k], sems.at[which, k])

    def store(k):
        return pltpu.make_async_copy(
            sent_ref.at[k], out_ref.at[:, pl.ds(k * SENT, SENT)], sems.at[2, k]
        )

    turn_copy = pltpu.make_async_copy(table_ref, turn_ref, sems.at[3, 0])
    for k in range(ROWS_X):
        for which in range(2):
            load(k, which).start()
        if k == 0:
            turn_copy.start()
    ky = wave_y(lax.axis_index("narrow") * ROWS_Y, (ROWS_Y, 1), 0)
    kz = wave_z((1, NZ), 1)
    half_sign = jnp.where(lax.broadcasted_iota(jnp.int32, (1, 128), 1) < 64, -1.0, 1.0)

    for k in range(ROWS_X):
        number_x = lax.axis_index("wide") * ROWS_X + k
        kx = 2.0 * math.pi / NX * number_x.astype(jnp.float32)
        if k == 0:
            turn_copy.wait()
        if k in WAITS:
            for near in range(k, WAITS[k]):
                for which in range(2):
                    load(near, which).wait()
        vel = [[vel_ref[c, part, k] for part in range(2)] for c in range(3)]
        fields = [(adj_ref[c, 0, k], adj_ref[c, 1, k]) for c in range(3)]
        fields += [(vel[c][0], vel[c][1]) for c in range(3)]
        fields.append((kz * vel[1][1] - ky * vel[2][1], ky * vel[2][0] - kz * vel[1][0]))
        fields.append((kx * vel[2][1] - kz * vel[0][1], kz * vel[0][0] - kx * vel[2][0]))
        for pair in range(SENT // 2):
            rows = [part for field in fields[2 * pair : 2 * pair + 2] for part in field]
            value = jnp.concatenate(rows, 0)
            if plane == 0:
                merged = value[:, :128] + value[:, 128:]
            else:
                merged = value[:, :128] - value[:, 128:]
            upper, lower = split(merged)
            stacked = jnp.concatenate([upper, lower, upper], 1)
            both = dot(turn_ref[...], stacked, ((1,), (1,)))
            for f in range(2):
                lanes = slice(128 * f, 128 * f + 128)
                turned = pltpu.roll(both[128:, lanes], 64, 1)
                sent_ref[k, :, 2 * pair + f, :] = both[:128, lanes] + half_sign * turned
        store(k).start()
    for k in range(ROWS_X):
        store(k).wait()


def synth_z(adjoint_hat, velocity_hat, plane):
    table = tables_synth_z()[plane]
    shape = (DEVICES, ROWS_X * SENT, 128)
    block = (3, 2, ROWS_X, ROWS_Y, NZ)
    return pl.pallas_call(
        functools.partial(synth_z_kernel, plane),
        in_specs=[
            pl.BlockSpec(memory_space=pl.ANY),
            pl.BlockSpec(memory_space=pl.ANY),
            pl.BlockSpec(memory_space=pl.ANY),
        ],
        out_specs=pl.BlockSpec(memory_space=pl.ANY),
        out_shape=jax.ShapeDtypeStruct(shape, jnp.float32),
        scratch_shapes=[
            pltpu.VMEM(block, jnp.float32),
            pltpu.VMEM(block, jnp.float32),
            pltpu.VMEM(table.shape, jnp.bfloat16),
            pltpu.VMEM((ROWS_X, DEVICES, SENT, 128), jnp.float32),
            pltpu.SemaphoreType.DMA((4, ROWS_X)),
        ],
        compiler_params=pltpu.CompilerParams(vmem_limit_bytes=vmem_bytes),
        name="synth_z",
    )(adjoint_hat, velocity_hat, jnp.asarray(table))


def plane_kernel(plane, got_ref, sy_ref, sx_ref, ax_ref, ay_ref, *refs):
    if plane == 0:
        out_ref, rest_ref, spec_ref, cell_ref = refs
    else:
        rest_ref, out_ref, spec_ref, cell_ref = refs
    chunk = ROWS_X * SENT
    half_sign = jnp.where(lax.broadcasted_iota(jnp.int32, (1, 128), 1) < 64, -1.0, 1.0)
    ky_lanes = []
    for n in range(NARROW):
        number = lax.broadcasted_iota(jnp.int32, (1, 128), 1) % 64 + n * ROWS_Y
        ky_lanes.append(2.0 * math.pi / NY * signed(number, NY).astype(jnp.float32))
    kx_rows = 2.0 * math.pi / NX * lax.broadcasted_iota(jnp.int32, (KX, 1), 0).astype(jnp.float32)
    alternate = jnp.where(lax.broadcasted_iota(jnp.int32, (KX, 1), 0) % 2 == 0, 1.0, -1.0)
    weight = (
        jnp.where(lax.broadcasted_iota(jnp.int32, (KX, 1), 0) == 0, 1.0, 2.0) * norm_scale()
    )
    first_row = lax.broadcasted_iota(jnp.int32, (256, 1), 0) == 0

    def rows_of(field, n):
        return jnp.concatenate(
            [
                got_ref[pl.ds((w * NARROW + n) * chunk + field, ROWS_X, stride=SENT), :]
                for w in range(WIDE)
            ],
            0,
        )

    def synth(parts, index):
        spans = []
        for parity in range(2):
            if parity == 0:
                merged = [parts[0] + parts[2], parts[1] + parts[3]]
            else:
                merged = [parts[0] - parts[2], parts[1] - parts[3]]
            spans.append(
                dot3(
                    split(jnp.concatenate(merged, 1)), (sy_ref[parity, 0], sy_ref[parity, 1])
                )
            )
        real = jnp.concatenate([spans[0][:, :128], spans[1][:, :128]], 1)
        imag = jnp.concatenate([spans[0][:, 128:], spans[1][:, 128:]], 1)
        cosine = dot3((sx_ref[0, 0], sx_ref[0, 1]), split(real))
        sine = dot3((sx_ref[1, 0], sx_ref[1, 1]), split(imag))
        middle = jnp.sum(real * (alternate * weight), 0, keepdims=True)
        cell_ref[index, 0] = cosine + sine
        cell_ref[index, 1] = jnp.where(first_row, middle, cosine - sine)

    def each_field(field, carry):
        synth([rows_of(field, n) for n in range(NARROW)], field)
        return carry

    lax.fori_loop(0, SENT, each_field, 0)
    swirl = []
    for n in range(NARROW):
        across = kx_rows * rows_of(4, n) - ky_lanes[n] * rows_of(3, n)
        swirl.append(pltpu.roll(across, 64, 1) * half_sign)
    synth(swirl, SENT)

    def product(kind, c, mirror):
        one, two = (c + 1) % 3, (c + 2) % 3
        if kind == 0:
            return (
                cell_ref[one, mirror] * cell_ref[6 + two, mirror]
                - cell_ref[two, mirror] * cell_ref[6 + one, mirror]
            )
        return (
            cell_ref[3 + one, mirror] * cell_ref[two, mirror]
            - cell_ref[3 + two, mirror] * cell_ref[one, mirror]
        )

    def analyse(index, kind, c):
        ahead = product(kind, c, 0)
        behind = product(kind, c, 1)
        middle = behind[0:1]
        both = ahead + jnp.where(first_row, 0.0, behind)
        apart = ahead - behind
        real = dot3((ax_ref[0, 0], ax_ref[0, 1]), split(both))
        real = real + alternate[:KEPT_X] * norm_scale() * middle
        imag = dot3((ax_ref[1, 0], ax_ref[1, 1]), split(apart))
        spans = []
        for parity in range(2):
            lanes = slice(128 * parity, 128 * parity + 128)
            spans.append(
                dot3(
                    split(jnp.concatenate([real[:, lanes], imag[:, lanes]], 1)),
                    (ay_ref[parity, 0], ay_ref[parity, 1]),
                )
            )
        spec_ref[index, 0] = spans[0] + spans[1]
        spec_ref[index, 1] = spans[0] - spans[1]

    for kind in range(2):
        for c in range(3):
            analyse(3 * kind + c, kind, c)

    kx_kept = kx_rows[:KEPT_X]

    def times_i(value):
        return pltpu.roll(value, 64, 1) * half_sign

    out_ref[KEPT_W:] = jnp.zeros((WIDE - KEPT_W,) + out_ref.shape[1:], jnp.float32)
    if plane == 0:
        rest_ref[KEPT_W:] = jnp.zeros((WIDE - KEPT_W,) + rest_ref.shape[1:], jnp.float32)

    def put(n, tile, value):
        rows = slice(tile * ROWS_X, tile * ROWS_X + ROWS_X)
        out_ref[:KEPT_W, n, rows, :] = value.reshape(KEPT_W, ROWS_X, 128)

    def values_of(n):
        at = (n // 2, slice(None), slice(128 * (n % 2), 128 * (n % 2) + 128))
        item = [spec_ref[(index,) + at] for index in range(6)]
        ky = ky_lanes[n]
        return [
            item[0] + times_i(ky * item[5]),
            item[1] - times_i(kx_kept * item[5]),
            item[2] + times_i(kx_kept * item[4] - ky * item[3]),
            item[3],
            item[4],
        ]

    lane = lax.broadcasted_iota(jnp.int32, (1, 128), 1)
    for half in range(2):
        heavy, light = HEAVY[half], LIGHT[half]
        values = values_of(heavy)
        direct = 3 if plane == 0 else 4
        for f in range(BACK):
            if f < direct:
                put(heavy, f, values[f])
            else:
                put(light, f - direct if plane == 0 else 3, values[f])
        values = values_of(light)
        packed = []
        for tile in range(2):
            value = jnp.zeros((KEPT_X, 128), jnp.float32)
            for slot in range(5):
                f, part = divmod(5 * tile + slot, 2)
                moved = pltpu.roll(
                    values[f], (SLOT * slot - 64 * part - LIGHT_ROW[half]) % 128, 1
                )
                value = jnp.where((lane >= SLOT * slot) & (lane < SLOT * slot + SLOT), moved, value)
            packed.append(value)
        if plane == 0:
            put(light, 2, packed[0])
            rest_ref[:KEPT_W, half] = packed[1].reshape(KEPT_W, ROWS_X, 128)
        else:
            out_ref[:, light, 0:ROWS_X, :] = rest_ref[:, half]
            put(light, 1, packed[0])
            put(light, 2, packed[1])


def run_plane(plane, got, rest=None):
    tables = [tables_synth_y(), tables_synth_x(), tables_anal_x(), tables_anal_y()]
    tiles = 3 + plane
    out_shape = [jax.ShapeDtypeStruct((WIDE, NARROW, tiles * ROWS_X, 128), jnp.float32)]
    operands = [got.reshape(DEVICES * ROWS_X * SENT, 128)] + [jnp.asarray(t) for t in tables]
    if plane == 0:
        out_shape.append(jax.ShapeDtypeStruct((WIDE, 2, ROWS_X, 128), jnp.float32))
    else:
        operands.append(rest)
    outs = pl.pallas_call(
        functools.partial(plane_kernel, plane),
        out_shape=out_shape,
        in_specs=[pl.BlockSpec(memory_space=pltpu.VMEM)] * len(operands),
        out_specs=[pl.BlockSpec(memory_space=pltpu.VMEM)] * len(out_shape),
        scratch_shapes=[
            pltpu.VMEM((6, 2, KEPT_X, 256), jnp.float32),
            pltpu.VMEM((9, 2, 256, 256), jnp.float32),
        ],
        compiler_params=pltpu.CompilerParams(vmem_limit_bytes=vmem_bytes),
        name="plane",
    )(*operands)
    return [outs[0].reshape(DEVICES, tiles * ROWS_X, 128)] + list(outs[1:])


def spans_of(tiles, table):
    upper, lower = split(jnp.concatenate([rows.T for rows in tiles], 0))
    span = dot(jnp.concatenate([upper, lower, upper], 1), table, ((1,), (0,)))
    return [span[128 * at : 128 * at + 128] for at in range(len(tiles))]


def unite(span, real_rows, imag_rows):
    real, imag = span[real_rows], span[imag_rows]
    return real[:, :128] + imag[:, 128:], imag[:, :128] - real[:, 128:]


def mirror(first, second):
    return tuple(
        jnp.concatenate([one + two, one - two], 1) for one, two in zip(first, second)
    )


def light_narrow(narrow):
    return (narrow == LIGHT[0]) | (narrow == LIGHT[1])


def tile_copies(source_ref, first, count, target_ref, at, sems):
    return [
        pltpu.make_async_copy(
            source_ref.at[:, pl.ds((first + tile) * ROWS_X, ROWS_X)],
            target_ref.at[at + tile],
            sems.at[at + tile],
        )
        for tile in range(count)
    ]


def begin_kernel(
    back_ref, more_ref, table_ref, part_ref, got_ref, new_ref, sems, whole_sems
):
    def store(k):
        return pltpu.make_async_copy(new_ref.at[k], part_ref.at[k], sems.at[k])

    @pl.when(jnp.logical_not(light_narrow(lax.axis_index("narrow"))))
    def _():
        pieces = tile_copies(back_ref, 0, 3, got_ref, 0, whole_sems)
        pieces += tile_copies(more_ref, 0, 2, got_ref, 3, whole_sems)
        for copy in pieces:
            copy.start()
        for copy in pieces:
            copy.wait()
        for k in range(ROWS_X):
            spans = spans_of([got_ref[f, :, k, :] for f in range(BACK)], table_ref[0])
            for f, span in enumerate(spans):
                real, imag = unite(span, slice(0, 64), slice(64, 128))
                new_ref[k, f, 0] = real
                new_ref[k, f, 1] = imag
            store(k).start()
        for k in range(ROWS_X):
            store(k).wait()


def begin(back, more):
    table = tables_anal_z()
    block = (ROWS_X, BACK, 2, ROWS_Y, 128)
    return pl.pallas_call(
        begin_kernel,
        in_specs=[
            pl.BlockSpec(memory_space=pltpu.HBM),
            pl.BlockSpec(memory_space=pltpu.HBM),
            pl.BlockSpec(memory_space=pltpu.VMEM),
        ],
        out_specs=pl.BlockSpec(memory_space=pltpu.HBM),
        out_shape=jax.ShapeDtypeStruct(block, jnp.float32),
        scratch_shapes=[
            pltpu.VMEM((BACK, DEVICES, ROWS_X, 128), jnp.float32),
            pltpu.VMEM(block, jnp.float32),
            pltpu.SemaphoreType.DMA((ROWS_X,)),
            pltpu.SemaphoreType.DMA((BACK,)),
        ],
        compiler_params=pltpu.CompilerParams(vmem_limit_bytes=finish_bytes),
        name="begin",
    )(back, more, jnp.asarray(table))


def in_hbm(array):
    return pltpu.with_memory_space_constraint(array, pltpu.HBM)


def in_vmem(array):
    return pltpu.with_memory_space_constraint(array, pltpu.VMEM)


def finish_kernel(
    back0_ref,
    back1_ref,
    more_ref,
    part_ref,
    adjoint_ref,
    table_ref,
    out_ref,
    new_ref,
    factor_ref,
    mid_ref,
    tile_ref,
    got_ref,
    sems,
    mid_sems,
    tile_sems,
):
    wide, narrow = lax.axis_index("wide"), lax.axis_index("narrow")
    is_light = light_narrow(narrow)

    def fetch(k):
        return pltpu.make_async_copy(part_ref.at[k], mid_ref.at[k], mid_sems.at[k])

    tile_copy = pltpu.make_async_copy(
        back0_ref.at[:, pl.ds(2 * ROWS_X, ROWS_X)], tile_ref, mid_sems.at[0]
    )

    def store(k):
        return pltpu.make_async_copy(new_ref.at[:, :, k], out_ref.at[:, :, k], sems.at[k])

    number_z = signed(lax.broadcasted_iota(jnp.int32, (1, NZ), 1), NZ)
    kz = 2.0 * math.pi / NZ * number_z.astype(jnp.float32)

    number_y = signed(
        lax.broadcasted_iota(jnp.int32, (ROWS_Y, 1), 0) + narrow * ROWS_Y, NY
    )
    all_ky = 2.0 * math.pi / NY * number_y.astype(jnp.float32)

    def wave_x(k):
        number_x = wide * ROWS_X + k
        return number_x, 2.0 * math.pi / NX * number_x.astype(jnp.float32)

    def prepare():
        keep_yz = (3 * jnp.abs(number_y) < NY) & (3 * jnp.abs(number_z) < NZ)
        scale_yz = keep_yz.astype(jnp.float32) * section_step
        square_yz = all_ky * all_ky + kz * kz
        for k in range(ROWS_X):
            number_x, kx = wave_x(k)
            ksquare = kx * kx + square_yz
            decay = jnp.exp(-viscous_rate * ksquare)
            factor_ref[0, k] = 1.0 / (ksquare + (ksquare == 0).astype(jnp.float32))
            factor_ref[1, k] = decay
            factor_ref[2, k] = scale_yz * (3 * number_x < NX).astype(jnp.float32) * decay

    def emit(k, got, start, rows):
        at = pl.ds(start, rows)
        kx = wave_x(k)[1]
        row = lax.broadcasted_iota(jnp.int32, (rows, 1), 0) + start + narrow * ROWS_Y
        ky = 2.0 * math.pi / NY * signed(row, NY).astype(jnp.float32)
        conv = [
            (got[0][0] + kz * got[4][1], got[0][1] - kz * got[4][0]),
            (got[1][0] - kz * got[3][1], got[1][1] + kz * got[3][0]),
            got[2],
        ]
        inverse, decay, gain = [factor_ref[which, k, at, :] for which in range(3)]
        waves = (kx, ky, kz)
        for part in range(2):
            along = (kx * conv[0][part] + ky * conv[1][part] + kz * conv[2][part]) * inverse
            for c in range(3):
                new_ref[c, part, k, at, :] = decay * adjoint_ref[c, part, k, at, :] + gain * (
                    conv[c][part] - waves[c] * along
                )

    @pl.when(jnp.logical_not(is_light))
    def _():
        pieces = tile_copies(back1_ref, 0, 4, got_ref, 0, tile_sems)
        for copy in pieces:
            copy.start()
        for k in range(ROWS_X):
            fetch(k).start()
        prepare()
        for copy in pieces:
            copy.wait()
        for k in range(ROWS_X):
            got = []
            spans = spans_of(
                [got_ref[f, :, k, :] for f in range(4)] + [more_ref[:, k, :]],
                table_ref[1],
            )
            if k in (0, 1):
                for near in range(k, 1 if k == 0 else ROWS_X):
                    fetch(near).wait()
            for f, span in enumerate(spans):
                second = unite(span, slice(0, 64), slice(64, 128))
                got.append(mirror((mid_ref[k, f, 0], mid_ref[k, f, 1]), second))
            emit(k, got, 0, ROWS_Y)
            store(k).start()

    @pl.when(is_light)
    def _():
        pieces = tile_copies(back1_ref, 0, 3, got_ref, 0, tile_sems) + [tile_copy]
        for copy in pieces:
            copy.start()
        prepare()
        for copy in pieces:
            copy.wait()
        for k in range(ROWS_X):
            by_plane = [
                spans_of(rows, table_ref[plane])
                for plane, rows in enumerate(
                    (
                        (tile_ref[:, k, :], got_ref[0, :, k, :]),
                        (got_ref[1, :, k, :], got_ref[2, :, k, :]),
                    )
                )
            ]

            def item(index, plane):
                tile, slot = divmod(index, 5)
                return by_plane[plane][tile][SLOT * slot : SLOT * slot + SLOT]

            got = []
            for f in range(BACK):
                halves_of = [
                    unite(
                        jnp.concatenate([item(2 * f, plane), item(2 * f + 1, plane)], 0),
                        slice(0, SLOT),
                        slice(SLOT, 2 * SLOT),
                    )
                    for plane in range(2)
                ]
                got.append(mirror(*halves_of))
            for c in range(3):
                for part in range(2):
                    new_ref[c, part, k] = factor_ref[1, k] * adjoint_ref[c, part, k]
            start = pl.multiple_of(jnp.where(narrow == LIGHT[0], 0, LIGHT_ROW[1]), 8)
            emit(k, got, start, SLOT)
            store(k).start()

    for k in range(ROWS_X):
        store(k).wait()


def finish(back0, back1, more, part, adjoint_hat):
    table = tables_anal_z()
    block = (3, 2, ROWS_X, ROWS_Y, NZ)
    return pl.pallas_call(
        finish_kernel,
        in_specs=[
            pl.BlockSpec(memory_space=pltpu.HBM),
            pl.BlockSpec(memory_space=pltpu.HBM),
            pl.BlockSpec(memory_space=pltpu.VMEM),
            pl.BlockSpec(memory_space=pltpu.HBM),
            pl.BlockSpec(memory_space=pltpu.VMEM),
            pl.BlockSpec(memory_space=pltpu.VMEM),
        ],
        out_specs=pl.BlockSpec(memory_space=pltpu.HBM),
        out_shape=jax.ShapeDtypeStruct(block, jnp.float32),
        scratch_shapes=[
            pltpu.VMEM(block, jnp.float32),
            pltpu.VMEM((3, ROWS_X, ROWS_Y, NZ), jnp.float32),
            pltpu.VMEM((ROWS_X, BACK, 2, ROWS_Y, 128), jnp.float32),
            pltpu.VMEM((DEVICES, ROWS_X, 128), jnp.float32),
            pltpu.VMEM((4, DEVICES, ROWS_X, 128), jnp.float32),
            pltpu.SemaphoreType.DMA((ROWS_X,)),
            pltpu.SemaphoreType.DMA((ROWS_X,)),
            pltpu.SemaphoreType.DMA((4,)),
        ],
        compiler_params=pltpu.CompilerParams(vmem_limit_bytes=finish_bytes),
        name="finish",
    )(
        in_hbm(back0),
        in_hbm(back1),
        in_vmem(more),
        in_hbm(part),
        in_vmem(adjoint_hat),
        jnp.asarray(table),
    )


def swap(chunks):
    return lax.all_to_all(chunks, ("wide", "narrow"), 0, 0, tiled=True)


def forward(tiles):
    return lax.ppermute(tiles, "narrow", [(LIGHT[0], HEAVY[0]), (LIGHT[1], HEAVY[1])])


def local(adjoint_hat, velocity_hat):
    got = [swap(synth_z(adjoint_hat, velocity_hat, plane)) for plane in range(2)]
    out0, rest = run_plane(0, got[0])
    back0 = swap(out0)
    (out1,) = run_plane(1, got[1], rest)
    back1 = swap(out1)
    more0 = forward(back0[:, : 2 * ROWS_X])
    part = begin(back0, more0)
    back1, part = lax.optimization_barrier((back1, part))
    more1 = forward(back1[:, 3 * ROWS_X :])
    return finish(back0, back1, more1, part, adjoint_hat)


def solution(mesh):
    in_specs = (P(None, None, "wide", "narrow", None), P(None, None, "wide", "narrow", None))
    out_specs = P(None, None, "wide", "narrow", None)
    return jax.shard_map(local, mesh=mesh, in_specs=in_specs, out_specs=out_specs, check_vma=False)
```
